32 devices in a mesh: dp: 8 (over z, core), expert: 4 (over y, x).
Axes of the slice: x: 2, y: 2, z: 4, core: 2. Of those that a mesh axis runs over, the one named last changes fastest.
Arguments:
- tokens: bfloat16 [4096, 2048], P(('dp', 'expert')), may hold values from -6 to 6
- out_grad: bfloat16 [4096, 2048], P(('dp', 'expert')), may hold values from -1.5 to 1.5
- routes: int32 [4096, 2], P(('dp', 'expert')), may hold values from 0 to 3, all different within a row; in each aligned block of 128 rows (0 to 127, 128 to 255, ...) at most 128 rows name the same one
- route_probs: bfloat16 [4096, 2], P(('dp', 'expert')), may hold values from 0.049804688 to 1
- kept_count: int32 [8], P('dp'), may hold values from 128 to 512, as said below
- gate_weight: bfloat16 [4, 2048, 768], P('expert', 'dp'), may hold values from -0.125 to 0.125
- up_weight: bfloat16 [4, 2048, 768], P('expert', 'dp'), may hold values from -0.125 to 0.125
- down_weight: bfloat16 [4, 2048, 768], P('expert', 'dp'), may hold values from -0.21875 to 0.21875
Outputs:
- token_grad: bfloat16 [4096, 2048], P(('dp', 'expert'))
- prob_grad: bfloat16 [4096, 2], P(('dp', 'expert'))
- weight_grad: bfloat16 [4, 2048, 2304], P('expert', 'dp')
The draws below stay inside these ranges and needn't reach their ends.
Inputs may be any that keep to these rules, and one draw needn't show every extreme that they name: `routes`: among the rows of one device, no expert is named more than 128 times, and a row names 2 different experts. `kept_count`: rows of a data group whose index within the group is below its count are kept; in every draw some group keeps all its rows and another keeps a quarter of them.
All inputs are finite; a program needn't handle non-finite values.
Results may differ from the reference program's by a relative error of at most 0.018.
Values may be sent and summed in bfloat16 or wider, within the bound.
A program may use at most 128 MiB of HBM per device.

```python
import math
import jax
import jax.numpy as jnp
import numpy as np
from jax import lax

D = 2048
FF = 768
TOP = 2
TOK_DEV = 128
EXPERTS = 4
CAP = 128
GROUP_ROWS = 512
TOKENS = 4096
N_DP = 8
N_EXPERT = 4


def draw_kept_count(key, part):
    counts = jax.random.randint(jax.random.fold_in(key, 11), (N_DP,), GROUP_ROWS // 4, GROUP_ROWS + 1).astype(jnp.int32)
    order = jax.random.permutation(jax.random.fold_in(key, 12), N_DP)
    counts = counts.at[order[0]].set(GROUP_ROWS)
    counts = counts.at[order[1]].set(GROUP_ROWS // 4)
    return counts.astype(jnp.int32)


def steps_of(key, dims, shards, low, top_value):
    level, own = 1.0, jax.random.fold_in(key, 6)
    for axis_at, parts in shards:
        heights = jnp.exp(jax.random.uniform(jax.random.fold_in(own, axis_at), (parts,), jnp.float32, low / len(shards), top_value / len(shards)))
        level = level * jnp.repeat(heights, dims[axis_at] // parts).reshape([-1 if axis == axis_at else 1 for axis in range(len(dims))])
    return level


def routed_block(own_key, own, number, rows, amount, top, limit, slope):
    sequence = jax.random.permutation(own_key, amount)
    crowded, common = shares(amount, rows * top, limit, slope, True), shares(amount, rows * top, limit, slope, False)
    places = jnp.arange(amount)

    def named(tallies, turn):
        used = int((tallies > 0).sum())
        fixed = max(1, used // 4)
        passed = fixed + (places - fixed + turn * (used - fixed)) % max(1, amount - fixed)
        return jnp.zeros((amount,), jnp.int32).at[sequence[jnp.where(places < fixed, places, passed)]].set(jnp.asarray(tallies, jnp.int32))

    tallies = jnp.where(number % 4 == 0, named(crowded, number // 4), named(common, number - number // 4 - 1))
    mixed = jax.random.permutation(jax.random.fold_in(own, 3), amount)
    donor, sink = mixed[0:amount // 2 * 2:2], mixed[1:amount // 2 * 2:2]
    slack = jnp.minimum(tallies[donor] - 1, limit - tallies[sink]) // 2
    slack = jnp.where((donor == sequence[0]) | (sink == sequence[0]) | (tallies[sink] == 0), 0, jnp.maximum(slack, 0))
    passed = jax.random.randint(jax.random.fold_in(own, 4), (amount // 2,), 0, 1 << 20) % (slack + 1)
    tallies = tallies.at[donor].add(-passed).at[sink].add(passed)
    members = jnp.searchsorted(jnp.cumsum(tallies), jnp.arange(rows * top), side="right").astype(jnp.int32)
    listing = members.reshape(top, rows).T
    listing = listing[jax.random.permutation(jax.random.fold_in(own, 1), rows)]
    turn = jax.random.randint(jax.random.fold_in(own, 2), (rows, 1), 0, top)
    return jnp.take_along_axis(listing, (jnp.arange(top)[None, :] + turn) % top, axis=1)


def shares(number_of, total, limit, lean, full):
    loads = [(1 << 20) // math.isqrt(grade ** lean) + 1 for grade in range(1, number_of + 1)]
    largest = limit if full else min(limit, max(-(-total // number_of), total * loads[0] // sum(loads)))
    least = 1 if total - largest >= number_of - 1 else 0
    holding, spare = [largest] + [least] * (number_of - 1), total - largest - least * (number_of - 1)
    while spare > 0:
        free = [i for i in range(1, number_of) if holding[i] < largest] or [i for i in range(1, number_of) if holding[i] < limit]
        mass, budget = sum([loads[i] for i in free]), spare
        for i in free:
            more = min(limit - holding[i], max(1, budget * loads[i] // mass), spare)
            holding[i] = holding[i] + more
            spare = spare - more
    return np.array(holding)


def bell_draw(rng, extent, deviation, reach, pieces=(), held_as=jnp.bfloat16):
    drawn = deviation * jax.random.normal(rng, extent, jnp.float32)
    if pieces:
        drawn = drawn * steps_of(rng, extent, pieces, -0.22, 0.18)
    return jnp.clip(drawn, -reach, reach).astype(held_as)


def setup_inputs(seed: int = 0) -> dict:
    arg_keys = jax.random.split(jax.random.key(seed), 9)
    tokens = bell_draw(arg_keys[0], (TOKENS, D), 1.0, 6.0, ((0, 32),))
    out_grad = bell_draw(arg_keys[1], (TOKENS, D), 0.25, 1.5, ((0, 32),))
    routes_keys = jax.random.split(jax.random.fold_in(arg_keys[2], 1), TOKENS // TOK_DEV)
    routes_turns = jax.random.permutation(jax.random.fold_in(arg_keys[2], 3), TOKENS // TOK_DEV)
    routes = jax.vmap(lambda own, number: routed_block(jax.random.fold_in(arg_keys[2], 2), own, number, TOK_DEV, EXPERTS, TOP, CAP, 2))(routes_keys, routes_turns).reshape((TOKENS, TOP))
    route_probs = jnp.clip(jnp.exp(math.log(1.0) - 2.9996462 * jax.random.uniform(arg_keys[3], (TOKENS, TOP), jnp.float32) ** steps_of(arg_keys[3], (TOKENS, TOP), ((0, 32),), -0.2, 0.2)), 0.049804688, 1.0).astype(jnp.bfloat16)
    kept_count = draw_kept_count(jax.random.fold_in(arg_keys[8], 71), 0)
    gate_weight = bell_draw(arg_keys[5], (EXPERTS, D, FF), D ** -0.5, 0.125, ((0, 4), (1, 8)))
    up_weight = bell_draw(arg_keys[6], (EXPERTS, D, FF), D ** -0.5, 0.125, ((0, 4), (1, 8)))
    down_weight = bell_draw(arg_keys[7], (EXPERTS, D, FF), FF ** -0.5, 0.21875, ((0, 4), (1, 8)))
    return {"tokens": tokens, "out_grad": out_grad, "routes": routes, "route_probs": route_probs, "kept_count": kept_count, "gate_weight": gate_weight, "up_weight": up_weight, "down_weight": down_weight}


def slot_positions(routes):
    blocks = routes.reshape(N_DP * N_EXPERT, TOK_DEV * TOP)
    onehot = (blocks[:, :, None] == jnp.arange(EXPERTS, dtype=jnp.int32)[None, None, :]).astype(jnp.int32)
    before = jnp.cumsum(onehot, axis=1) - onehot
    position = jnp.sum(before * onehot, axis=2)
    return position.reshape(TOKENS, TOP).astype(jnp.int32)


def reference(tokens, out_grad, routes, route_probs, kept_count, gate_weight, up_weight, down_weight):
    row = jnp.arange(TOKENS, dtype=jnp.int32)
    kept = (row % GROUP_ROWS) < kept_count[row // GROUP_ROWS]
    masked = jnp.where(kept[:, None], out_grad, jnp.zeros_like(out_grad))
    position = slot_positions(routes)
    block = row // TOK_DEV
    group = (block // N_EXPERT).astype(jnp.int32)
    source = (block % N_EXPERT).astype(jnp.int32)
    route_id = (row[:, None] * TOP + jnp.arange(TOP, dtype=jnp.int32)[None, :]).astype(jnp.int32)
    empty_id = TOKENS * TOP
    table = jnp.full((EXPERTS, N_DP, N_EXPERT, CAP), empty_id, jnp.int32)
    table = table.at[routes, group[:, None], source[:, None], position].set(route_id)
    flat_probs = route_probs.reshape(-1)

    def expert_step(carry, inputs):
        contrib, prob_acc = carry
        ids, w_gate, w_up, w_down = inputs
        ids = ids.reshape(-1)
        valid = ids < empty_id
        safe = jnp.where(valid, ids, 0).astype(jnp.int32)
        token_of = (safe // TOP).astype(jnp.int32)
        rows_in = jnp.where(valid[:, None], tokens[token_of], jnp.zeros((), jnp.bfloat16))
        grad_in = jnp.where(valid[:, None], masked[token_of], jnp.zeros((), jnp.bfloat16))
        prob_in = jnp.where(valid, flat_probs[safe], jnp.zeros((), jnp.bfloat16))
        pre_gate = jnp.dot(rows_in, w_gate, preferred_element_type=jnp.float32)
        pre_up = jnp.dot(rows_in, w_up, preferred_element_type=jnp.float32)
        sig = jax.nn.sigmoid(pre_gate)
        act = (pre_gate * sig * pre_up).astype(jnp.bfloat16)
        output_rows = jnp.dot(act, w_down.T, preferred_element_type=jnp.float32)
        prob_part = jnp.sum(grad_in.astype(jnp.float32) * output_rows, axis=1).astype(jnp.bfloat16)
        scaled = (prob_in.astype(jnp.float32)[:, None] * grad_in.astype(jnp.float32)).astype(jnp.bfloat16)
        back_hidden = jnp.dot(scaled, w_down, preferred_element_type=jnp.float32)
        d_gate = (back_hidden * pre_up * sig * (1.0 + pre_gate * (1.0 - sig))).astype(jnp.bfloat16)
        d_up = (back_hidden * pre_gate * sig).astype(jnp.bfloat16)
        route_back = (jnp.dot(d_gate, w_gate.T, preferred_element_type=jnp.float32)
                      + jnp.dot(d_up, w_up.T, preferred_element_type=jnp.float32)).astype(jnp.bfloat16)
        rows_g = rows_in.reshape(N_DP, N_EXPERT * CAP, D).astype(jnp.float32)
        scaled_g = scaled.reshape(N_DP, N_EXPERT * CAP, D).astype(jnp.float32)
        gate_g = d_gate.reshape(N_DP, N_EXPERT * CAP, FF).astype(jnp.float32)
        up_g = d_up.reshape(N_DP, N_EXPERT * CAP, FF).astype(jnp.float32)
        act_g = act.reshape(N_DP, N_EXPERT * CAP, FF).astype(jnp.float32)
        partial_value = jnp.concatenate((jnp.einsum('grd,grf->gdf', rows_g, gate_g),
                                   jnp.einsum('grd,grf->gdf', rows_g, up_g),
                                   jnp.einsum('grd,grf->gdf', scaled_g, act_g)), axis=2).astype(jnp.bfloat16)
        summed = jnp.sum(partial_value.astype(jnp.float32), axis=0).astype(jnp.bfloat16)
        contrib = contrib.at[ids].set(route_back, mode="drop")
        prob_acc = prob_acc.at[ids].set(prob_part, mode="drop")
        return (contrib, prob_acc), summed

    start = (jnp.zeros((TOKENS * TOP, D), jnp.bfloat16), jnp.zeros((TOKENS * TOP,), jnp.bfloat16))
    (contrib, prob_acc), weight_grad = lax.scan(expert_step, start, (table, gate_weight, up_weight, down_weight))
    token_grad = jnp.sum(contrib.reshape(TOKENS, TOP, D).astype(jnp.float32), axis=1).astype(jnp.bfloat16)
    prob_grad = prob_acc.reshape(TOKENS, TOP)
    return token_grad, prob_grad, weight_grad
```

```python
import jax
import jax.numpy as jnp
from jax import lax
from jax.sharding import PartitionSpec as P
from jax.experimental import pallas as pl
from jax.experimental.pallas import tpu as pltpu

MESH = pl.DeviceIdType.MESH
CORES = 2


def dot_f32(left, right):
    return jnp.dot(left, right, preferred_element_type=jnp.float32)


def contract_rows(left, right):
    return lax.dot_general(
        left, right, (((0,), (0,)), ((), ())), preferred_element_type=jnp.float32
    )


def contract_last(left, right):
    return lax.dot_general(
        left, right, (((1,), (1,)), ((), ())), preferred_element_type=jnp.float32
    )


def hop(x, axis, mask, name):
    size = lax.axis_size(axis)
    with jax.named_scope(name):
        return lax.ppermute(x, axis, [(i, i ^ mask) for i in range(size)])


def z_send(x, moves, name):
    pairs = [(a * CORES + c, b * CORES + c) for a, b in moves for c in range(CORES)]
    with jax.named_scope(name):
        return lax.ppermute(x, "dp", pairs)


def xor_blocks(x, blocks):
    me = lax.axis_index("dp")
    rows, width = x.shape
    size = width // blocks
    depth = blocks // CORES
    parts = [x[:, i * size : (i + 1) * size] for i in range(blocks)]
    bit = 1
    while bit < blocks:
        flip = (me & bit) != 0
        parts = [jnp.where(flip, parts[i ^ bit], parts[i]) for i in range(blocks)]
        bit *= 2
    return parts, depth


def to_local(x, blocks):
    parts, depth = xor_blocks(x, blocks)
    return jnp.concatenate([parts[kz * CORES + kc] for kc in range(CORES) for kz in range(depth)], 1)


def from_local(x, blocks):
    depth = blocks // CORES
    size = x.shape[1] // blocks
    cut = [x[:, i * size : (i + 1) * size] for i in range(blocks)]
    natural = [cut[kc * depth + kz] for kz in range(depth) for kc in range(CORES)]
    parts, _ = xor_blocks(jnp.concatenate(natural, 1), blocks)
    return jnp.concatenate(parts, 1)


def spread(x, experts, name):
    if experts != 4:
        return jnp.concatenate([x] + [hop(x, "expert", k, f"{name}{k}") for k in range(1, experts)], 0)
    half = x.shape[0] // 2
    along_x = hop(x, "expert", 1, f"{name}_x")
    along_y = hop(x, "expert", 2, f"{name}_y")
    top = hop(along_x[:half], "expert", 2, f"{name}_xy")
    bottom = hop(along_y[half:], "expert", 1, f"{name}_yx")
    return jnp.concatenate([x, along_x, along_y, top, bottom], 0)


def reduce_line(q, depth, tag):
    def add(a, b):
        return (a.astype(jnp.float32) + b.astype(jnp.float32)).astype(jnp.bfloat16)

    if depth != 4:
        total = q[0].astype(jnp.float32)
        for kz in range(1, depth):
            total = total + hop(q[kz], "dp", kz * CORES, f"{tag}_{kz}").astype(jnp.float32)
        return total.astype(jnp.bfloat16)
    outer, middle, inner = [(3, 2), (0, 1)], [(2, 1), (1, 2)], [(1, 0), (2, 3)]
    a0 = z_send(q[3], outer, f"{tag}_a0")
    a1 = z_send(q[2], outer, f"{tag}_a1")
    a2 = z_send(q[1], outer, f"{tag}_a2")
    b0 = z_send(add(q[2], a0), middle, f"{tag}_b0")
    b1 = z_send(add(q[3], a1), middle, f"{tag}_b1")
    c0 = z_send(add(q[1], b0), inner, f"{tag}_c0")
    total = q[0].astype(jnp.float32) + a2.astype(jnp.float32)
    return (total + b1.astype(jnp.float32) + c0.astype(jnp.float32)).astype(jnp.bfloat16)


def gather_line(own, depth, tag):
    if depth != 4:
        return jnp.concatenate(
            [own] + [hop(own, "dp", kz * CORES, f"{tag}_{kz}") for kz in range(1, depth)], 0
        )
    z = lax.axis_index("dp") // CORES
    inside = (z == 1) | (z == 2)
    outer, middle, inner = [(3, 2), (0, 1)], [(2, 1), (1, 2)], [(1, 0), (2, 3)]
    o = z_send(own, outer, f"{tag}_o")
    m0 = z_send(own, middle, f"{tag}_m0")
    i0 = z_send(own, inner, f"{tag}_i0")
    m1 = z_send(o, middle, f"{tag}_m1")
    i1 = z_send(m0, inner, f"{tag}_i1")
    i2 = z_send(m1, inner, f"{tag}_i2")
    return jnp.concatenate(
        [own, jnp.where(inside, o, i0), jnp.where(inside, m1, i1), jnp.where(inside, m0, i2)], 0
    )


def chunks_of(hidden):
    return 3 if hidden % 384 == 0 else 1


def per_device(
    tokens, out_grad, routes, route_probs, kept_count, gate_weight, up_weight, down_weight
):
    tok_rows, width = tokens.shape
    experts = lax.axis_size("expert")
    groups = lax.axis_size("dp")
    depth = groups // CORES
    hidden = gate_weight.shape[2]
    count = chunks_of(hidden)
    step = hidden // count
    me = lax.axis_index("expert")

    row = me * tok_rows + jnp.arange(tok_rows, dtype=jnp.int32)
    kept = row < kept_count[0]
    masked = jnp.where(kept[:, None], out_grad, jnp.zeros_like(out_grad))
    probs = route_probs.astype(jnp.float32)

    def share(k):
        return jnp.sum(jnp.where(routes == (me ^ k), probs, 0.0), axis=1)

    prob_in = jnp.concatenate(
        [share(0)] + [hop(share(k)[None], "expert", k, f"prob{k}")[0] for k in range(1, experts)]
    )
    rows_in = spread(to_local(tokens, groups), experts, "rows")
    grad_in = spread(to_local(masked, groups), experts, "grad")

    half = width // CORES
    scores = 0.0
    back = [0.0, 0.0]
    sums = []
    for j in range(count):
        cut = slice(j * step, (j + 1) * step)
        own = jnp.concatenate(
            [gate_weight[0][:, cut], up_weight[0][:, cut], down_weight[0][:, cut]], 1
        )
        mine = gather_line(own, depth, f"g{j}")
        other = hop(mine, "dp", 1, f"pair{j}")
        both = (mine, other)
        pre = sum(dot_f32(rows_in[:, i * half : (i + 1) * half], both[i][:, : 2 * step]) for i in range(2))
        cot = sum(dot_f32(grad_in[:, i * half : (i + 1) * half], both[i][:, 2 * step :]) for i in range(2))
        a, b = pre[:, :step], pre[:, step:]
        sig = jax.nn.sigmoid(a)
        act = a * sig * b
        act_low = act.astype(jnp.bfloat16).astype(jnp.float32)
        scores = scores + jnp.sum(act_low * cot, axis=1)
        back_hidden = cot * prob_in[:, None]
        d_gate = (back_hidden * b * sig * (1.0 + a * (1.0 - sig))).astype(jnp.bfloat16)
        d_up = (back_hidden * a * sig).astype(jnp.bfloat16)
        d_both = jnp.concatenate([d_gate, d_up], 1)
        weighted = (act_low * prob_in[:, None]).astype(jnp.bfloat16)
        terms = [
            jnp.concatenate(
                [
                    contract_rows(rows_in[:, i * half : (i + 1) * half], d_both).astype(jnp.bfloat16),
                    contract_rows(grad_in[:, i * half : (i + 1) * half], weighted).astype(jnp.bfloat16),
                ],
                1,
            )
            for i in range(2)
        ]
        arrived = hop(terms[1], "dp", 1, f"swap{j}")
        block = half // depth
        q = tuple(
            (
                terms[0][kz * block : (kz + 1) * block].astype(jnp.float32)
                + arrived[kz * block : (kz + 1) * block].astype(jnp.float32)
            ).astype(jnp.bfloat16)
            for kz in range(depth)
        )
        sums.append(reduce_line(lax.optimization_barrier(q), depth, f"s{j}"))
        back = [back[i] + contract_last(d_both, both[i][:, : 2 * step]) for i in range(2)]

    route_back = jnp.concatenate(back, 1).astype(jnp.bfloat16)
    parts = [route_back[k * tok_rows : (k + 1) * tok_rows] for k in range(experts)]
    scored = [scores[k * tok_rows : (k + 1) * tok_rows] for k in range(experts)]
    for k in range(1, experts):
        parts[k] = hop(parts[k], "expert", k, f"home{k}")
        scored[k] = hop(scored[k][None], "expert", k, f"score{k}")[0]
    token_sum = parts[0].astype(jnp.float32)
    for k in range(1, experts):
        token_sum = token_sum + parts[k].astype(jnp.float32)
    token_grad = from_local(token_sum.astype(jnp.bfloat16), groups)
    prob_grad = sum(
        jnp.where(routes == (me ^ k), scored[k][:, None], 0.0) for k in range(experts)
    ).astype(jnp.bfloat16)
    weight_grad = jnp.concatenate(
        [s[:, i * step : (i + 1) * step] for i in range(3) for s in sums], 1
    )[None]
    return (token_grad, prob_grad, weight_grad)


def add_low(a, b):
    return (a.astype(jnp.float32) + b.astype(jnp.float32)).astype(jnp.bfloat16)


def kernel(
    gate, up_w, down_w, tok, grad, routes_in, probs_in, kept, token_out, prob_out, weight_out,
    w, x, m, xt, mt, q, pc, du, wt, term, swapped, inbox, sb, st, sr, ha, hs, hr, wo, to, po,
    routes, probs,
    gs, gr, ps, pr, ds, dr, ws, wr, rs, rr, hsem, hrec, lw, ls, os,
):
    dp, e = lax.axis_index("dp"), lax.axis_index("expert")
    z, c = dp // 2, dp % 2
    ey, ex = e // 2, e % 2
    near = {1: 2 * ey + 1 - ex, 2: 2 * (1 - ey) + ex, 3: 2 * (1 - ey) + 1 - ex}
    count, _, rows, cols = w.shape
    step = cols // 3
    toks, width = tok.shape
    partner = z * 2 + 1 - c
    upper = z // 2
    middle = (z > 0) & (z < 3)
    edge = (z == 0) | (z == 3)
    sent = []

    def pos(k):
        return upper * k + (1 - upper) * (3 - k)

    side_in, side_out = upper, 1 - upper
    depth = jnp.where(edge, pos(2), pos(1))
    inn, out = (depth * 2 + c, e), (pos(3) * 2 + c, e)

    def copy(src, dst, s, r, dev):
        return pltpu.make_async_remote_copy(
            src_ref=src, dst_ref=dst, send_sem=s, recv_sem=r, device_id=dev, device_id_type=MESH
        )

    def send(src, dst, s, r, dev, cond=None):
        d = copy(src, dst, s, r, dev)
        if cond is None:
            d.start()
        else:
            pl.when(cond)(d.start)
        sent.append((cond, d))

    def arrive(dst, s, r, cond=None):
        d = copy(dst, dst, s, r, (partner, e))
        if cond is None:
            d.wait_recv()
        else:
            pl.when(cond)(d.wait_recv)

    barrier = pltpu.get_barrier_semaphore()

    def greet(dev):
        pl.semaphore_signal(barrier, inc=1, device_id=dev, device_id_type=MESH)

    for dev in [(partner, e), inn] + [(dp, near[k]) for k in (1, 2, 3)]:
        greet(dev)
    pl.when(middle)(lambda: greet(out))

    own = [
        [
            pltpu.make_async_copy(
                ref.at[0, :, pl.ds(j * step, step)], w.at[j, dp, :, pl.ds(k * step, step)], lw.at[j, k]
            )
            for k, ref in enumerate((gate, up_w, down_w))
        ]
        for j in range(count)
    ]
    small = [
        pltpu.make_async_copy(routes_in, routes, ls.at[0]),
        pltpu.make_async_copy(probs_in, probs, ls.at[1]),
        pltpu.make_async_copy(tok, x.at[e], ls.at[2]),
        pltpu.make_async_copy(grad, m.at[e], ls.at[3]),
    ]
    for d in own[0] + small[:2] + own[1] + own[2] + small[2:]:
        d.start()
    pl.semaphore_wait(barrier, 5 + jnp.where(middle, 1, 0))

    def spread_own(src, dst, at):
        send(src, dst.at[e], ds.at[at], dr.at[at], (dp, near[1]))
        send(src, dst.at[e], ds.at[at + 1], dr.at[at + 1], (dp, near[2]))

    half = toks // 2

    def spread_more(dst, at):
        first, second = pl.ds(0, half), pl.ds(half, half)
        arrive(dst.at[near[1]], ds.at[at], dr.at[at])
        top = dst.at[near[1], first]
        send(top, top, ds.at[at + 2], dr.at[at + 2], (dp, near[2]))
        arrive(dst.at[near[2]], ds.at[at + 1], dr.at[at + 1])
        low = dst.at[near[2], second]
        send(low, low, ds.at[at + 3], dr.at[at + 3], (dp, near[1]))

    def spread_done(dst, at):
        first, second = pl.ds(0, half), pl.ds(half, half)
        arrive(dst.at[near[3], first], ds.at[at + 2], dr.at[at + 2])
        arrive(dst.at[near[3], second], ds.at[at + 3], dr.at[at + 3])

    def gather_own(j, cond=None):
        block = w.at[j, dp]
        outward = middle if cond is None else cond
        send(block, block, gs.at[j, z, 0], gr.at[j, z], inn, cond)
        send(block, block, gs.at[j, z, 1], gr.at[j, z], out, outward)
        send(block, block, ps.at[j, z], pr.at[j, z], (partner, e), cond)

    def gather_pass(j, at, dev, cond):
        block = w.at[j, at * 2 + c]
        arrive(block, gs.at[j, at, 0], gr.at[j, at], cond)
        if dev is not None:
            send(block, block, gs.at[j, at, 0], gr.at[j, at], dev, cond)
        send(block, block, ps.at[j, at], pr.at[j, at], (partner, e), cond)

    def gather_edge(j, r):
        gather_pass(j, pos(2 - r), None, edge)

    def gather_mid(j, s):
        if s == 0:
            gather_pass(j, pos(3), inn, middle)
            gather_pass(j, pos(1), out, middle)
        else:
            gather_pass(j, pos(0), out, middle)

    def pairs_done(j):
        for i in range(4):
            arrive(w.at[j, i * 2 + 1 - c], ps.at[j, i], pr.at[j, i])

    def block_of(k):
        return ((ey + k // 2) % 2) * 2 + (ex + k % 2) % 2

    tall_rows = lax.broadcasted_iota(jnp.int32, (8, toks), 0)

    def forward(j, first=0, last=4):
        def body(k, _):
            i = block_of(k)
            if j == 0:
                row = jnp.sum(jnp.where(tall_rows == e, q[i], 0.0), axis=0, keepdims=True)
                pc[i] = jnp.broadcast_to(row, (128, toks)).T
            p = pc[i][:, :1]
            part = lambda k: w[j, :, :, k * step : (k + 1) * step].reshape(width, step)
            a, b, cot = dot_f32(x[i], part(0)), dot_f32(x[i], part(1)), dot_f32(m[i], part(2))
            sig = jax.nn.sigmoid(a)
            act = (a * sig * b).astype(jnp.bfloat16).astype(jnp.float32)
            score = jnp.sum(act * cot, axis=1, keepdims=True)
            sb[i] = jnp.broadcast_to(score, (toks, 128)) + (0.0 if j == 0 else sb[i])
            back = cot * p
            here = pl.ds(pl.multiple_of(i * toks, toks), toks)
            du[j, here, :step] = (back * b * sig * (1.0 + a * (1.0 - sig))).astype(jnp.bfloat16)
            du[j, here, step:] = (back * a * sig).astype(jnp.bfloat16)
            wt[here, :] = (act * p).astype(jnp.bfloat16)
            if j == 0:
                xt[:, here] = x[i].T
                mt[:, here] = m[i].T
            return 0

        lax.fori_loop(first, last, body, 0)

    def gradient(j):
        def block(d):
            here = pl.ds(pl.multiple_of(d * rows, rows), rows)
            term[j, d, :, : 2 * step] = dot_f32(xt[here, :], du[j]).astype(jnp.bfloat16)
            term[j, d, :, 2 * step :] = dot_f32(mt[here, :], wt[...]).astype(jnp.bfloat16)

        def settle(r, ship):
            t = pos(r)
            arrive(swapped.at[j, t], ws.at[j, t], wr.at[j, t])
            mine = term.at[j, t * 2 + c]
            mine[...] = add_low(mine[...], swapped[j, t])
            if ship:
                d = copy(mine, inbox.at[side_in, j, t], rs.at[j, t], rr.at[side_in, j, t], inn)
                pl.when(edge)(d.start)

        def body(r, _):
            t = pos(r)

            def pair(s, _):
                block(t * 2 + jnp.where(s == 0, 1 - c, c))

                @pl.when(s == 0)
                def _():
                    copy(
                        term.at[j, t * 2 + 1 - c], swapped.at[j, t],
                        ws.at[j, t], wr.at[j, t], (partner, e),
                    ).start()

                return 0

            lax.fori_loop(0, 2, pair, 0)
            pl.when(r > 0)(lambda: settle(r - 1, True))
            return 0

        lax.fori_loop(0, 4, body, 0)
        settle(3, False)
        for r in range(4):
            t = pos(r)
            sent.append((None, copy(
                term.at[j, t * 2 + 1 - c], swapped.at[j, t], ws.at[j, t], wr.at[j, t], (partner, e)
            )))
            if r < 3:
                sent.append((edge, copy(
                    term.at[j, t * 2 + c], inbox.at[side_in, j, t], rs.at[j, t],
                    rr.at[side_in, j, t], inn,
                )))

    def relay(j, side, t, dev):
        box = inbox.at[side, j, t]
        arrive(box, rs.at[j, t], rr.at[side, j, t], middle)

        @pl.when(middle)
        def _():
            term[j, t * 2 + c] = add_low(term[j, t * 2 + c], inbox[side, j, t])

        send(term.at[j, t * 2 + c], box, rs.at[j, t], rr.at[side, j, t], dev, middle)

    def relay_in(j, r):
        relay(j, side_in, pos(r), inn)

    def relay_out(j):
        relay(j, side_out, pos(3), out)

    def final(j):
        arrive(inbox.at[side_in, j, z], rs.at[j, z], rr.at[side_in, j, z], middle)
        arrive(inbox.at[side_out, j, z], rs.at[j, z], rr.at[side_out, j, z])
        total = term[j, dp].astype(jnp.float32) + inbox[side_out, j, z].astype(jnp.float32)

        def put(total):
            total = total.astype(jnp.bfloat16)
            for k in range(3):
                at = (k * count + j) * step
                wo[:, at : at + step] = total[:, k * step : (k + 1) * step]

        pl.when(edge)(lambda: put(total))
        pl.when(middle)(lambda: put(total + inbox[side_in, j, z].astype(jnp.float32)))
        for k in range(3):
            at = (k * count + j) * step
            piece(j, k).start()

    def piece(j, k):
        at = pl.ds((k * count + j) * step, step)
        return pltpu.make_async_copy(wo.at[:, at], weight_out.at[0, :, at], os.at[j, k])

    def home(j):
        def body(k, _):
            i = block_of(3 - k)
            at = pl.ds(pl.multiple_of(i * toks, toks), toks)
            new = contract_last(du[j, at, :], w[j, :, :, : 2 * step].reshape(width, 2 * step))
            if j == 0:
                ha[i] = new
            elif j < count - 1:
                ha[i] = ha[i] + new
            else:
                hs[i] = (ha[i] + new).astype(jnp.bfloat16)
                st[i] = sb[i].T[:8, :]

                @pl.when(k < 3)
                def _():
                    copy(hs.at[i], hr.at[e], hsem.at[3 - k], hrec.at[3 - k], (dp, i)).start()
                    copy(st.at[i], sr.at[e], hsem.at[7 - k], hrec.at[7 - k], (dp, i)).start()

            return 0

        lax.fori_loop(0, 4, body, 0)
        if j == count - 1:
            for k in (1, 2, 3):
                i = near[k]
                sent.append((None, copy(hs.at[i], hr.at[e], hsem.at[k], hrec.at[k], (dp, i))))
                sent.append((None, copy(st.at[i], sr.at[e], hsem.at[4 + k], hrec.at[4 + k], (dp, i))))
            sr[e] = st[e]

    outs = [
        pltpu.make_async_copy(to, token_out, os.at[0, 3]),
        pltpu.make_async_copy(po, prob_out, os.at[1, 3]),
    ]

    def home_done():
        total = hs[e].astype(jnp.float32)
        for k in (1, 2, 3):
            arrive(hr.at[near[k]], hsem.at[k], hrec.at[k])
            total = total + hr[near[k]].astype(jnp.float32)
            arrive(sr.at[near[k]], hsem.at[4 + k], hrec.at[4 + k])
        to[...] = total.astype(jnp.bfloat16)
        top = routes.shape[0]
        score = sum(jnp.where(routes[...] == i, sr[i][:top, :], 0.0) for i in range(4))
        lane = lax.broadcasted_iota(jnp.int32, (top, toks), 1)
        po[...] = jnp.where(e * toks + lane < kept[0], score, 0.0).astype(jnp.bfloat16)
        for d in outs:
            d.start()

    spread_own(tok, x, 0)
    for d in own[0]:
        d.wait()
    gather_own(0)
    spread_own(grad, m, 4)
    for j in (1, 2):
        for d in own[j]:
            d.wait()
    for j in (1, 2):
        block = w.at[j, dp]
        send(block, block, gs.at[j, z, 0], gr.at[j, z], inn, edge)
        send(block, block, ps.at[j, z], pr.at[j, z], (partner, e))
    for d in small[:2]:
        d.wait()
    lanes = lax.broadcasted_iota(jnp.int32, (8, toks), 1)
    rate = sum(
        jnp.where(routes[k : k + 1, :] == tall_rows, probs[k : k + 1, :].astype(jnp.float32), 0.0)
        for k in range(routes.shape[0])
    )
    q[e] = jnp.where(e * toks + lanes < kept[0], rate, 0.0)
    for k in (1, 2, 3):
        send(q.at[e], q.at[e], ds.at[7 + k], dr.at[7 + k], (dp, near[k]))

    def own_mid(j):
        block = w.at[j, dp]
        send(block, block, gs.at[j, z, 0], gr.at[j, z], inn, middle)
        send(block, block, gs.at[j, z, 1], gr.at[j, z], out, middle)

    for d in small[2:]:
        d.wait()
    gather_mid(0, 0)
    gather_edge(0, 0)
    spread_more(x, 0)
    gather_mid(0, 1)
    own_mid(1)
    gather_edge(0, 1)
    spread_more(m, 4)
    gather_mid(1, 0)
    gather_edge(0, 2)
    for k in (1, 2, 3):
        arrive(q.at[near[k]], ds.at[7 + k], dr.at[7 + k])
    pairs_done(0)
    forward(0, 0, 3)
    gather_mid(1, 1)
    own_mid(2)
    spread_done(x, 0)
    spread_done(m, 4)
    forward(0, 3, 4)
    gradient(0)
    gather_mid(2, 0)
    gather_edge(1, 0)
    home(0)
    gather_edge(1, 1)
    gather_edge(1, 2)
    pairs_done(1)
    forward(1)
    gradient(1)
    relay_in(0, 0)
    gather_mid(2, 1)
    home(1)
    relay_in(0, 1)
    gather_edge(2, 0)
    gather_edge(2, 1)
    gather_edge(2, 2)
    pairs_done(2)
    forward(2)
    home(2)
    relay_out(0)
    gradient(2)
    final(0)
    relay_in(1, 0)
    relay_in(1, 1)
    relay_out(1)
    final(1)
    home_done()
    relay_in(2, 0)
    relay_in(2, 1)
    relay_out(2)
    final(2)
    for cond, d in sent:
        if cond is None:
            d.wait_send()
        else:
            pl.when(cond)(d.wait_send)
    for j in range(count):
        for k in range(3):
            piece(j, k).wait()
    for d in outs:
        d.wait()


def per_device_line(
    tokens, out_grad, routes, route_probs, kept_count, gate_weight, up_weight, down_weight
):
    toks, width = tokens.shape
    rows, hidden = gate_weight.shape[1:]
    count, step = 3, hidden // 3
    cols = 3 * step
    low, full = jnp.bfloat16, jnp.float32
    dma = pltpu.SemaphoreType.DMA
    hbm = pl.BlockSpec(memory_space=pl.ANY)
    top = routes.shape[1]
    token_grad, prob_grad, weight_grad = pl.pallas_call(
        kernel,
        out_shape=(
            jax.ShapeDtypeStruct((toks, width), low),
            jax.ShapeDtypeStruct((top, toks), low),
            jax.ShapeDtypeStruct((1, rows, 3 * hidden), low),
        ),
        in_specs=[hbm] * 7 + [pl.BlockSpec(memory_space=pltpu.SMEM)],
        out_specs=(hbm,) * 3,
        scratch_shapes=[
            pltpu.VMEM((count, 8, rows, cols), low),
            pltpu.VMEM((4, toks, width), low),
            pltpu.VMEM((4, toks, width), low),
            pltpu.VMEM((width, 4 * toks), low),
            pltpu.VMEM((width, 4 * toks), low),
            pltpu.VMEM((4, 8, toks), full),
            pltpu.VMEM((4, toks, 128), full),
            pltpu.VMEM((count, 4 * toks, 2 * step), low),
            pltpu.VMEM((4 * toks, step), low),
            pltpu.VMEM((count, 8, rows, cols), low),
            pltpu.VMEM((count, 4, rows, cols), low),
            pltpu.VMEM((2, count, 4, rows, cols), low),
            pltpu.VMEM((4, toks, 128), full),
            pltpu.VMEM((4, 8, toks), full),
            pltpu.VMEM((4, 8, toks), full),
            pltpu.VMEM((4, toks, width), full),
            pltpu.VMEM((4, toks, width), low),
            pltpu.VMEM((4, toks, width), low),
            pltpu.VMEM((rows, 3 * hidden), low),
            pltpu.VMEM((toks, width), low),
            pltpu.VMEM((top, toks), low),
            pltpu.VMEM((top, toks), jnp.int32),
            pltpu.VMEM((top, toks), low),
            dma((count, 4, 2)), dma((count, 4)),
            dma((count, 4)), dma((count, 4)),
            dma((11,)), dma((11,)),
            dma((count, 4)), dma((count, 4)),
            dma((count, 4)), dma((2, count, 4)),
            dma((8,)), dma((8,)),
            dma((count, 3)), dma((4,)), dma((count, 4)),
        ],
        compiler_params=pltpu.CompilerParams(
            collective_id=0, has_side_effects=True, vmem_limit_bytes=67043328
        ),
    )(
        gate_weight, up_weight, down_weight, tokens, out_grad, routes.T, route_probs.T, kept_count
    )
    return (token_grad, prob_grad.T, weight_grad)


def solution(mesh):
    in_specs = (
        P(("dp", "expert"), None),
        P(("dp", "expert"), None),
        P(("dp", "expert"), None),
        P(("dp", "expert"), None),
        P("dp"),
        P("expert", "dp", None),
        P("expert", "dp", None),
        P("expert", "dp", None),
    )
    out_specs = (P(("dp", "expert"), None), P(("dp", "expert"), None), P("expert", "dp", None))

    line = mesh.shape["dp"] == 4 * CORES and mesh.shape["expert"] == 4
    return jax.shard_map(
        per_device_line if line else per_device,
        mesh=mesh, in_specs=in_specs, out_specs=out_specs, check_vma=False,
    )
```

```python
import jax
import jax.numpy as jnp
from jax import lax
from jax.sharding import PartitionSpec as P
from jax.experimental import pallas as pl
from jax.experimental.pallas import tpu as pltpu

MESH = pl.DeviceIdType.MESH
CORES = 2
SHARES = (2, 1, 1, 2)


def dot_f32(left, right):
    return jnp.dot(left, right, preferred_element_type=jnp.float32)


def contract_rows(left, right):
    return lax.dot_general(
        left, right, (((0,), (0,)), ((), ())), preferred_element_type=jnp.float32
    )


def contract_last(left, right):
    return lax.dot_general(
        left, right, (((1,), (1,)), ((), ())), preferred_element_type=jnp.float32
    )


def hop(x, axis, mask, name):
    size = lax.axis_size(axis)
    with jax.named_scope(name):
        return lax.ppermute(x, axis, [(i, i ^ mask) for i in range(size)])


def z_send(x, moves, name):
    pairs = [(a * CORES + c, b * CORES + c) for a, b in moves for c in range(CORES)]
    with jax.named_scope(name):
        return lax.ppermute(x, "dp", pairs)


def xor_blocks(x, blocks):
    me = lax.axis_index("dp")
    rows, width = x.shape
    size = width // blocks
    depth = blocks // CORES
    parts = [x[:, i * size : (i + 1) * size] for i in range(blocks)]
    bit = 1
    while bit < blocks:
        flip = (me & bit) != 0
        parts = [jnp.where(flip, parts[i ^ bit], parts[i]) for i in range(blocks)]
        bit *= 2
    return parts, depth


def to_local(x, blocks):
    parts, depth = xor_blocks(x, blocks)
    return jnp.concatenate([parts[kz * CORES + kc] for kc in range(CORES) for kz in range(depth)], 1)


def from_local(x, blocks):
    depth = blocks // CORES
    size = x.shape[1] // blocks
    cut = [x[:, i * size : (i + 1) * size] for i in range(blocks)]
    natural = [cut[kc * depth + kz] for kz in range(depth) for kc in range(CORES)]
    parts, _ = xor_blocks(jnp.concatenate(natural, 1), blocks)
    return jnp.concatenate(parts, 1)


def spread(x, experts, name):
    if experts != 4:
        return jnp.concatenate([x] + [hop(x, "expert", k, f"{name}{k}") for k in range(1, experts)], 0)
    half = x.shape[0] // 2
    along_x = hop(x, "expert", 1, f"{name}_x")
    along_y = hop(x, "expert", 2, f"{name}_y")
    top = hop(along_x[:half], "expert", 2, f"{name}_xy")
    bottom = hop(along_y[half:], "expert", 1, f"{name}_yx")
    return jnp.concatenate([x, along_x, along_y, top, bottom], 0)


def reduce_line(q, depth, tag):
    def add(a, b):
        return (a.astype(jnp.float32) + b.astype(jnp.float32)).astype(jnp.bfloat16)

    if depth != 4:
        total = q[0].astype(jnp.float32)
        for kz in range(1, depth):
            total = total + hop(q[kz], "dp", kz * CORES, f"{tag}_{kz}").astype(jnp.float32)
        return total.astype(jnp.bfloat16)
    outer, middle, inner = [(3, 2), (0, 1)], [(2, 1), (1, 2)], [(1, 0), (2, 3)]
    a0 = z_send(q[3], outer, f"{tag}_a0")
    a1 = z_send(q[2], outer, f"{tag}_a1")
    a2 = z_send(q[1], outer, f"{tag}_a2")
    b0 = z_send(add(q[2], a0), middle, f"{tag}_b0")
    b1 = z_send(add(q[3], a1), middle, f"{tag}_b1")
    c0 = z_send(add(q[1], b0), inner, f"{tag}_c0")
    total = q[0].astype(jnp.float32) + a2.astype(jnp.float32)
    return (total + b1.astype(jnp.float32) + c0.astype(jnp.float32)).astype(jnp.bfloat16)


def gather_line(own, depth, tag):
    if depth != 4:
        return jnp.concatenate(
            [own] + [hop(own, "dp", kz * CORES, f"{tag}_{kz}") for kz in range(1, depth)], 0
        )
    z = lax.axis_index("dp") // CORES
    inside = (z == 1) | (z == 2)
    outer, middle, inner = [(3, 2), (0, 1)], [(2, 1), (1, 2)], [(1, 0), (2, 3)]
    o = z_send(own, outer, f"{tag}_o")
    m0 = z_send(own, middle, f"{tag}_m0")
    i0 = z_send(own, inner, f"{tag}_i0")
    m1 = z_send(o, middle, f"{tag}_m1")
    i1 = z_send(m0, inner, f"{tag}_i1")
    i2 = z_send(m1, inner, f"{tag}_i2")
    return jnp.concatenate(
        [own, jnp.where(inside, o, i0), jnp.where(inside, m1, i1), jnp.where(inside, m0, i2)], 0
    )


def chunks_of(hidden):
    return 3 if hidden % 384 == 0 else 1


def per_device(
    tokens, out_grad, routes, route_probs, kept_count, gate_weight, up_weight, down_weight
):
    tok_rows, width = tokens.shape
    experts = lax.axis_size("expert")
    groups = lax.axis_size("dp")
    depth = groups // CORES
    hidden = gate_weight.shape[2]
    count = chunks_of(hidden)
    step = hidden // count
    me = lax.axis_index("expert")

    row = me * tok_rows + jnp.arange(tok_rows, dtype=jnp.int32)
    kept = row < kept_count[0]
    masked = jnp.where(kept[:, None], out_grad, jnp.zeros_like(out_grad))
    probs = route_probs.astype(jnp.float32)

    def share(k):
        return jnp.sum(jnp.where(routes == (me ^ k), probs, 0.0), axis=1)

    prob_in = jnp.concatenate(
        [share(0)] + [hop(share(k)[None], "expert", k, f"prob{k}")[0] for k in range(1, experts)]
    )
    rows_in = spread(to_local(tokens, groups), experts, "rows")
    grad_in = spread(to_local(masked, groups), experts, "grad")

    half = width // CORES
    scores = 0.0
    back = [0.0, 0.0]
    sums = []
    for j in range(count):
        cut = slice(j * step, (j + 1) * step)
        own = jnp.concatenate(
            [gate_weight[0][:, cut], up_weight[0][:, cut], down_weight[0][:, cut]], 1
        )
        mine = gather_line(own, depth, f"g{j}")
        other = hop(mine, "dp", 1, f"pair{j}")
        both = (mine, other)
        pre = sum(dot_f32(rows_in[:, i * half : (i + 1) * half], both[i][:, : 2 * step]) for i in range(2))
        cot = sum(dot_f32(grad_in[:, i * half : (i + 1) * half], both[i][:, 2 * step :]) for i in range(2))
        a, b = pre[:, :step], pre[:, step:]
        sig = jax.nn.sigmoid(a)
        act = a * sig * b
        act_low = act.astype(jnp.bfloat16).astype(jnp.float32)
        scores = scores + jnp.sum(act_low * cot, axis=1)
        back_hidden = cot * prob_in[:, None]
        d_gate = (back_hidden * b * sig * (1.0 + a * (1.0 - sig))).astype(jnp.bfloat16)
        d_up = (back_hidden * a * sig).astype(jnp.bfloat16)
        d_both = jnp.concatenate([d_gate, d_up], 1)
        weighted = (act_low * prob_in[:, None]).astype(jnp.bfloat16)
        terms = [
            jnp.concatenate(
                [
                    contract_rows(rows_in[:, i * half : (i + 1) * half], d_both).astype(jnp.bfloat16),
                    contract_rows(grad_in[:, i * half : (i + 1) * half], weighted).astype(jnp.bfloat16),
                ],
                1,
            )
            for i in range(2)
        ]
        arrived = hop(terms[1], "dp", 1, f"swap{j}")
        block = half // depth
        q = tuple(
            (
                terms[0][kz * block : (kz + 1) * block].astype(jnp.float32)
                + arrived[kz * block : (kz + 1) * block].astype(jnp.float32)
            ).astype(jnp.bfloat16)
            for kz in range(depth)
        )
        sums.append(reduce_line(lax.optimization_barrier(q), depth, f"s{j}"))
        back = [back[i] + contract_last(d_both, both[i][:, : 2 * step]) for i in range(2)]

    route_back = jnp.concatenate(back, 1).astype(jnp.bfloat16)
    parts = [route_back[k * tok_rows : (k + 1) * tok_rows] for k in range(experts)]
    scored = [scores[k * tok_rows : (k + 1) * tok_rows] for k in range(experts)]
    for k in range(1, experts):
        parts[k] = hop(parts[k], "expert", k, f"home{k}")
        scored[k] = hop(scored[k][None], "expert", k, f"score{k}")[0]
    token_sum = parts[0].astype(jnp.float32)
    for k in range(1, experts):
        token_sum = token_sum + parts[k].astype(jnp.float32)
    token_grad = from_local(token_sum.astype(jnp.bfloat16), groups)
    prob_grad = sum(
        jnp.where(routes == (me ^ k), scored[k][:, None], 0.0) for k in range(experts)
    ).astype(jnp.bfloat16)
    weight_grad = jnp.concatenate(
        [s[:, i * step : (i + 1) * step] for i in range(3) for s in sums], 1
    )[None]
    return (token_grad, prob_grad, weight_grad)


def add_low(a, b):
    return (a.astype(jnp.float32) + b.astype(jnp.float32)).astype(jnp.bfloat16)


def kernel(
    gate, up_w, down_w, tok, grad, routes_in, probs_in, kept, token_out, prob_out, weight_out,
    w, term, swapped, inbox, du, wt, fac, low_act,
    x, m, xt, mt, q, pc, sb, st, sr, ha, hs, hr, wo, to, po, routes, probs,
    gs, gr, ps, pr, ds, dr, ws, wr, rs, rr, hsem, hrec, lw, ls, os,
):
    dp, e = lax.axis_index("dp"), lax.axis_index("expert")
    z, c = dp // 2, dp % 2
    ey, ex = e // 2, e % 2
    near = {1: 2 * ey + 1 - ex, 2: 2 * (1 - ey) + ex, 3: 2 * (1 - ey) + 1 - ex}
    units = len(w)
    count = units // 2
    rows = w[0].shape[1]
    sizes = [ref.shape[2] for ref in w[1::2]]
    offsets = [sum(sizes[:j]) for j in range(count)]
    hidden = sum(sizes)
    toks, width = tok.shape
    part = width // 2
    partner = z * 2 + 1 - c
    upper = z // 2
    middle = (z > 0) & (z < 3)
    edge = (z == 0) | (z == 3)
    sent = []

    def pos(k):
        return upper * k + (1 - upper) * (3 - k)

    side_in, side_out = upper, 1 - upper
    depth = jnp.where(edge, pos(2), pos(1))
    inn, out = (depth * 2 + c, e), (pos(3) * 2 + c, e)

    def copy(src, dst, s, r, dev):
        return pltpu.make_async_remote_copy(
            src_ref=src, dst_ref=dst, send_sem=s, recv_sem=r, device_id=dev, device_id_type=MESH
        )

    def send(src, dst, s, r, dev, cond=None):
        d = copy(src, dst, s, r, dev)
        if cond is None:
            d.start()
        else:
            pl.when(cond)(d.start)
        sent.append((cond, d))

    def arrive(dst, s, r, cond=None):
        d = copy(dst, dst, s, r, (partner, e))
        if cond is None:
            d.wait_recv()
        else:
            pl.when(cond)(d.wait_recv)

    barrier = pltpu.get_barrier_semaphore()

    def greet(dev):
        pl.semaphore_signal(barrier, inc=1, device_id=dev, device_id_type=MESH)

    for dev in [(partner, e), inn] + [(dp, near[k]) for k in (1, 2, 3)]:
        greet(dev)
    pl.when(middle)(lambda: greet(out))

    own = []
    for u in range(units):
        j = u // 2
        at = pl.ds(offsets[j], sizes[j])
        if u % 2 == 0:
            pairs = [(gate, pl.ds(0, sizes[j])), (up_w, pl.ds(sizes[j], sizes[j]))]
        else:
            pairs = [(down_w, pl.ds(0, sizes[j]))]
        own.append([
            pltpu.make_async_copy(ref.at[0, :, at], w[u].at[dp, :, to_at], lw.at[u, k])
            for k, (ref, to_at) in enumerate(pairs)
        ])
    small = [
        pltpu.make_async_copy(routes_in, routes, ls.at[0]),
        pltpu.make_async_copy(probs_in, probs, ls.at[1]),
        pltpu.make_async_copy(tok, x.at[e], ls.at[2]),
        pltpu.make_async_copy(grad.at[:, pl.ds(0, part)], m.at[0, e], ls.at[3]),
        pltpu.make_async_copy(grad.at[:, pl.ds(part, part)], m.at[1, e], ls.at[4]),
    ]
    for d in own[0] + small[:2] + sum(own[1:], []) + small[2:]:
        d.start()
    pl.semaphore_wait(barrier, 5 + jnp.where(middle, 1, 0))

    half = toks // 2
    first, second = pl.ds(0, half), pl.ds(half, half)

    def spread_own(src, dst, at):
        for k, (row, n) in enumerate(((first, 1), (second, 2), (second, 1), (first, 2))):
            send(src(row), dst(e, row), ds.at[at + k], dr.at[at + k], (dp, near[n]))

    def spread_more(dst, at):
        top, low = dst(near[1], first), dst(near[2], second)
        arrive(top, ds.at[at], dr.at[at])
        send(top, top, ds.at[at + 4], dr.at[at + 4], (dp, near[2]))
        arrive(low, ds.at[at + 1], dr.at[at + 1])
        send(low, low, ds.at[at + 5], dr.at[at + 5], (dp, near[1]))

    def spread_rest(dst, at):
        arrive(dst(near[1], second), ds.at[at + 2], dr.at[at + 2])
        arrive(dst(near[2], first), ds.at[at + 3], dr.at[at + 3])

    def spread_done(dst, at):
        arrive(dst(near[3], first), ds.at[at + 4], dr.at[at + 4])
        arrive(dst(near[3], second), ds.at[at + 5], dr.at[at + 5])

    early, late = 1 - upper, upper

    def tok_src(row):
        return tok.at[row, :]

    def grad_src(side):
        return lambda row: grad.at[row, pl.ds(pl.multiple_of(side * part, part), part)]

    def x_dst(i, row):
        return x.at[i, row]

    def m_dst(side):
        return lambda i, row: m.at[side, i, row]

    def own_in(u, cond):
        block = w[u].at[dp]
        send(block, block, gs.at[u, z, 0], gr.at[u, z], inn, cond)

    def own_out(u):
        block = w[u].at[dp]
        send(block, block, gs.at[u, z, 1], gr.at[u, z], out, middle)

    def own_pair(u):
        block = w[u].at[dp]
        send(block, block, ps.at[u, z], pr.at[u, z], (partner, e))

    def gather_pass(u, at, dev, cond):
        block = w[u].at[at * 2 + c]
        arrive(block, gs.at[u, at, 0], gr.at[u, at], cond)
        if dev is not None:
            send(block, block, gs.at[u, at, 0], gr.at[u, at], dev, cond)
        send(block, block, ps.at[u, at], pr.at[u, at], (partner, e), cond)

    def pairs_done(u):
        for i in range(4):
            arrive(w[u].at[i * 2 + 1 - c], ps.at[u, i], pr.at[u, i])

    def block_of(k):
        return ((ey + k // 2) % 2) * 2 + (ex + k % 2) % 2

    def rows_of(i):
        return pl.ds(pl.multiple_of(i * toks, toks), toks)

    expert_rows = lax.broadcasted_iota(jnp.int32, (8, toks), 0)

    def turn_x(lo, hi):
        def body(k, _):
            i = block_of(k)
            xt[:, rows_of(i)] = x[i].T
            return 0

        lax.fori_loop(lo, hi, body, 0)

    def turn_m(side, lo, hi):
        def body(k, _):
            i = block_of(k)
            mt[pl.ds(pl.multiple_of(side * part, part), part), rows_of(i)] = m[side, i].T
            return 0

        lax.fori_loop(lo, hi, body, 0)

    def tall_probs():
        def body(i, _):
            row = jnp.sum(jnp.where(expert_rows == e, q[i], 0.0), axis=0, keepdims=True)
            pc[i] = jnp.broadcast_to(row, (128, toks)).T
            return 0

        lax.fori_loop(0, 4, body, 0)

    def forward_up(j, lo=0, hi=4):
        size, at = sizes[j], offsets[j]

        def body(k, _):
            i = block_of(k)
            here = rows_of(i)
            a = dot_f32(x[i], w[2 * j][:, :, :size].reshape(width, size))
            b = dot_f32(x[i], w[2 * j][:, :, size:].reshape(width, size))
            sig = jax.nn.sigmoid(a)
            act = (a * sig * b).astype(jnp.bfloat16)
            low_act[here, at : at + size] = act
            wt[j][here, :] = (act.astype(jnp.float32) * pc[i][:, :1]).astype(jnp.bfloat16)
            fac[here, 2 * at : 2 * at + size] = b * sig * (1.0 + a * (1.0 - sig))
            fac[here, 2 * at + size : 2 * (at + size)] = a * sig
            return 0

        lax.fori_loop(lo, hi, body, 0)

    def forward_down(j):
        size, at = sizes[j], offsets[j]

        def body(k, _):
            i = block_of(k)
            here = rows_of(i)
            cot = dot_f32(m[0, i], w[2 * j + 1][:4].reshape(part, size))
            cot = cot + dot_f32(m[1, i], w[2 * j + 1][4:].reshape(part, size))
            act = low_act[here, at : at + size].astype(jnp.float32)
            score = jnp.sum(act * cot, axis=1, keepdims=True)
            sb[i] = jnp.broadcast_to(score, (toks, 128)) + (0.0 if j == 0 else sb[i])
            back = cot * pc[i][:, :1]
            du[j][here, :size] = (back * fac[here, 2 * at : 2 * at + size]).astype(jnp.bfloat16)
            du[j][here, size:] = (
                back * fac[here, 2 * at + size : 2 * (at + size)]
            ).astype(jnp.bfloat16)
            return 0

        lax.fori_loop(0, 4, body, 0)

    def gradient(u, lo=0, hi=4):
        left, right = (xt, du[u // 2]) if u % 2 == 0 else (mt, wt[u // 2])

        def swap(t):
            return copy(
                term[u].at[t * 2 + 1 - c], swapped[u].at[t], ws.at[u, t], wr.at[u, t], (partner, e)
            )

        def ship(t):
            return copy(
                term[u].at[t * 2 + c], inbox[u].at[side_in, t], rs.at[u, t], rr.at[u, side_in, t], inn
            )

        def settle(r):
            t = pos(r)
            arrive(swapped[u].at[t], ws.at[u, t], wr.at[u, t])
            term[u][t * 2 + c] = add_low(term[u][t * 2 + c], swapped[u][t])
            pl.when(edge & (r < 3))(lambda: ship(t).start())

        def body(r, _):
            t = pos(r)

            def pair(s, _):
                d = t * 2 + jnp.where(s == 0, 1 - c, c)
                here = pl.ds(pl.multiple_of(d * rows, rows), rows)
                term[u][d] = dot_f32(left[here, :], right[...]).astype(jnp.bfloat16)
                pl.when(s == 0)(lambda: swap(t).start())
                return 0

            lax.fori_loop(0, 2, pair, 0)
            pl.when(r > lo)(lambda: settle(r - 1))
            return 0

        lax.fori_loop(lo, hi, body, 0)
        settle(hi - 1)
        for r in range(lo, hi):
            sent.append((None, swap(pos(r))))
            if r < 3:
                sent.append((edge, ship(pos(r))))

    def relay(u, side, t, dev):
        box = inbox[u].at[side, t]
        arrive(box, rs.at[u, t], rr.at[u, side, t], middle)

        @pl.when(middle)
        def _():
            term[u][t * 2 + c] = add_low(term[u][t * 2 + c], inbox[u][side, t])

        send(term[u].at[t * 2 + c], box, rs.at[u, t], rr.at[u, side, t], dev, middle)

    def spots(u):
        at = offsets[u // 2]
        return [at, hidden + at] if u % 2 == 0 else [2 * hidden + at]

    def pieces(u):
        cuts = [pl.ds(spot, sizes[u // 2]) for spot in spots(u)]
        return [
            pltpu.make_async_copy(wo.at[:, cut], weight_out.at[0, :, cut], os.at[u, k])
            for k, cut in enumerate(cuts)
        ]

    def final(u):
        size = sizes[u // 2]
        arrive(inbox[u].at[side_in, z], rs.at[u, z], rr.at[u, side_in, z], middle)
        arrive(inbox[u].at[side_out, z], rs.at[u, z], rr.at[u, side_out, z])

        def put(total):
            total = total.astype(jnp.bfloat16)
            for k, spot in enumerate(spots(u)):
                wo[:, spot : spot + size] = total[:, k * size : (k + 1) * size]

        def base():
            return term[u][dp].astype(jnp.float32) + inbox[u][side_out, z].astype(jnp.float32)

        pl.when(edge)(lambda: put(base()))
        pl.when(middle)(lambda: put(base() + inbox[u][side_in, z].astype(jnp.float32)))
        for d in pieces(u):
            d.start()

    def home(j):
        def body(k, _):
            i = block_of(3 - k)
            new = contract_last(du[j][rows_of(i), :], w[2 * j][...].reshape(width, 2 * sizes[j]))
            if j == 0:
                ha[i] = new
            elif j < count - 1:
                ha[i] = ha[i] + new
            else:
                hs[i] = (ha[i] + new).astype(jnp.bfloat16)
                st[i] = sb[i].T[:8, :]

                @pl.when(k < 3)
                def _():
                    copy(hs.at[i], hr.at[e], hsem.at[3 - k], hrec.at[3 - k], (dp, i)).start()
                    copy(st.at[i], sr.at[e], hsem.at[7 - k], hrec.at[7 - k], (dp, i)).start()

            return 0

        lax.fori_loop(0, 4, body, 0)
        if j == count - 1:
            for k in (1, 2, 3):
                i = near[k]
                sent.append((None, copy(hs.at[i], hr.at[e], hsem.at[k], hrec.at[k], (dp, i))))
                sent.append((None, copy(st.at[i], sr.at[e], hsem.at[4 + k], hrec.at[4 + k], (dp, i))))
            sr[e] = st[e]

    outs = [
        pltpu.make_async_copy(to, token_out, os.at[0, 2]),
        pltpu.make_async_copy(po, prob_out, os.at[1, 2]),
    ]

    def home_done():
        total = hs[e].astype(jnp.float32)
        for k in (1, 2, 3):
            arrive(hr.at[near[k]], hsem.at[k], hrec.at[k])
            total = total + hr[near[k]].astype(jnp.float32)
            arrive(sr.at[near[k]], hsem.at[4 + k], hrec.at[4 + k])
        to[...] = total.astype(jnp.bfloat16)
        top = routes.shape[0]
        score = sum(jnp.where(routes[...] == i, sr[i][:top, :], 0.0) for i in range(4))
        lane = lax.broadcasted_iota(jnp.int32, (top, toks), 1)
        po[...] = jnp.where(e * toks + lane < kept[0], score, 0.0).astype(jnp.bfloat16)
        for d in outs:
            d.start()

    def send_probs():
        for d in small[:2]:
            d.wait()
        lanes = lax.broadcasted_iota(jnp.int32, (8, toks), 1)
        rate = sum(
            jnp.where(
                routes[k : k + 1, :] == expert_rows, probs[k : k + 1, :].astype(jnp.float32), 0.0
            )
            for k in range(routes.shape[0])
        )
        q[e] = jnp.where(e * toks + lanes < kept[0], rate, 0.0)
        for k in (1, 2, 3):
            send(q.at[e], q.at[e], ds.at[17 + k], dr.at[17 + k], (dp, near[k]))

    def get_probs():
        for k in (1, 2, 3):
            arrive(q.at[near[k]], ds.at[17 + k], dr.at[17 + k])
        tall_probs()

    steps = []

    def at(time, *calls):
        steps.append((time, len(steps), calls))

    def do(f, *args):
        return lambda: f(*args)

    cost = [8.75 * ref.shape[2] / hidden for ref in w]
    order = [0, 2, 1, 3] + list(range(4, units))
    before = 0.0
    arrival = {}
    lag = 1.0
    for n, u in enumerate(order):
        s = cost[u]
        follow = order[n + 1] if n + 1 < units else None
        for r in range(3):
            arrival[u] = 3 * before + (r + 1) * s + lag
            at(arrival[u], do(gather_pass, u, pos(2 - r), None, edge))
        at(before + s + lag, do(gather_pass, u, pos(3), inn, middle),
           *([do(own_in, follow, middle)] if follow is not None else []))
        at(2 * before + s + lag, do(gather_pass, u, pos(1), out, middle))
        at(2 * before + 2 * s + lag, do(gather_pass, u, pos(0), out, middle),
           *([do(own_out, follow)] if follow is not None else []))
        before += s
    tail_in, tail_out = 2 * before, 3 * before

    spreads = ((x_dst, 0), (m_dst(early), 6), (m_dst(late), 12))
    at(6.8, do(spread_more, *spreads[0]), do(spread_own, grad_src(early), m_dst(early), 6))
    at(12.6, do(spread_rest, *spreads[0]), small[2].wait, do(turn_x, 0, 3))
    at(18.4, do(spread_done, *spreads[0]), do(turn_x, 3, 4), get_probs)
    at(21.4, do(spread_more, *spreads[1]), do(spread_own, grad_src(late), m_dst(late), 12))
    at(24.3, do(spread_rest, *spreads[1]), small[3].wait, small[4].wait, do(turn_m, early, 0, 3))
    at(27.2, do(spread_done, *spreads[1]), do(turn_m, early, 3, 4))
    at(30.1, do(spread_more, *spreads[2]))
    at(33.0, do(spread_rest, *spreads[2]), do(turn_m, late, 0, 3))
    at(36.0, do(spread_done, *spreads[2]), do(turn_m, late, 3, 4))

    def up_part(j):
        pairs_done(2 * j)
        forward_up(j)

    def down_part(j):
        pairs_done(2 * j + 1)
        forward_down(j)

    at(18.5, do(up_part, 0))
    at(27.3, do(gradient, 1, 0, 2))
    at(30.2, do(up_part, 1), do(gradient, 3, 0, 2))
    at(36.1, do(gradient, 1, 2, 4), do(gradient, 3, 2, 4), do(down_part, 0), do(gradient, 0))
    at(arrival[3] + 4.5, do(down_part, 1), do(gradient, 2))
    at(arrival[3] + 4.6, do(home, 0))
    at(arrival[3] + 4.7, do(home, 1))
    for j in range(2, count):
        at(arrival[2 * j] + 0.1, do(up_part, j), do(gradient, 2 * j + 1))
        at(arrival[2 * j + 1] + 0.1, do(down_part, j))
        if j == count - 1:
            at(arrival[2 * j + 1] + 0.2, do(home, j))
        at(arrival[2 * j + 1] + 0.3, do(gradient, 2 * j))
        if j < count - 1:
            at(arrival[2 * j + 1] + 0.4, do(home, j))

    reduce_order = [1, 3, 0, 2] + [u for j in range(2, count) for u in (2 * j + 1, 2 * j)]
    begin, done = 29.5, 0.0
    for u in reduce_order:
        s = cost[u]
        for r in range(2):
            at(begin + 3 * done + (r + 1) * s + lag + 0.5, do(relay, u, side_in, pos(r), inn))
        passed = max(begin + 3 * done + 2 * s, tail_in + 2 * done + s) + 2 * lag + 0.5
        at(passed, do(relay, u, side_out, pos(3), out))
        at(max(passed + s, tail_out + done + s) + lag + 0.5, do(final, u))
        done += s
    at(arrival[units - 1] + 27.0, home_done)

    spread_own(tok_src, x_dst, 0)
    for d in own[0]:
        d.wait()
    own_in(0, None)
    own_out(0)
    own_pair(0)
    for u in order[1:]:
        for d in own[u]:
            d.wait()
        own_in(u, edge)
        own_pair(u)
    send_probs()
    for _, _, calls in sorted(steps, key=lambda item: item[:2]):
        for call in calls:
            call()
    for cond, d in sent:
        if cond is None:
            d.wait_send()
        else:
            pl.when(cond)(d.wait_send)
    for u in range(units):
        for d in pieces(u):
            d.wait()
    for d in outs:
        d.wait()


def hand_over(*refs):
    came, go = refs[:3], refs[3:6]
    held, sem = refs[6:9], refs[9]
    into = [pltpu.make_async_copy(a, b, sem.at[k]) for k, (a, b) in enumerate(zip(came, held))]
    away = [pltpu.make_async_copy(a, b, sem.at[3 + k]) for k, (a, b) in enumerate(zip(held, go))]
    for d in into:
        d.start()
    for a, b in zip(into, away):
        a.wait()
        b.start()
    for d in away:
        d.wait()


def per_device_line(
    tokens, out_grad, routes, route_probs, kept_count, gate_weight, up_weight, down_weight
):
    toks, width = tokens.shape
    rows, hidden = gate_weight.shape[1:]
    sizes = [hidden * k // 6 for k in SHARES]
    cols = [n for size in sizes for n in (2 * size, size)]
    units = len(cols)
    low, full = jnp.bfloat16, jnp.float32
    dma, vmem = pltpu.SemaphoreType.DMA, pltpu.VMEM
    hbm = pl.BlockSpec(memory_space=pl.ANY)
    top = routes.shape[1]
    shapes = (
        jax.ShapeDtypeStruct((toks, width), low),
        jax.ShapeDtypeStruct((top, toks), low),
        jax.ShapeDtypeStruct((1, rows, 3 * hidden), low),
    )
    results = pl.pallas_call(
        kernel,
        out_shape=shapes,
        in_specs=[hbm] * 7 + [pl.BlockSpec(memory_space=pltpu.SMEM)],
        out_specs=(hbm,) * 3,
        scratch_shapes=[
            [vmem((8, rows, n), low) for n in cols],
            [vmem((8, rows, n), low) for n in cols],
            [vmem((4, rows, n), low) for n in cols],
            [vmem((2, 4, rows, n), low) for n in cols],
            [vmem((4 * toks, 2 * n), low) for n in sizes],
            [vmem((4 * toks, n), low) for n in sizes],
            vmem((4 * toks, 2 * hidden), full),
            vmem((4 * toks, hidden), low),
            vmem((4, toks, width), low),
            vmem((2, 4, toks, width // 2), low),
            vmem((width, 4 * toks), low),
            vmem((width, 4 * toks), low),
            vmem((4, 8, toks), full),
            vmem((4, toks, 128), full),
            vmem((4, toks, 128), full),
            vmem((4, 8, toks), full),
            vmem((4, 8, toks), full),
            vmem((4, toks, width), full),
            vmem((4, toks, width), low),
            vmem((4, toks, width), low),
            vmem((rows, 3 * hidden), low),
            vmem((toks, width), low),
            vmem((top, toks), low),
            vmem((top, toks), jnp.int32),
            vmem((top, toks), low),
            dma((units, 4, 2)), dma((units, 4)),
            dma((units, 4)), dma((units, 4)),
            dma((21,)), dma((21,)),
            dma((units, 4)), dma((units, 4)),
            dma((units, 4)), dma((units, 2, 4)),
            dma((8,)), dma((8,)),
            dma((units, 2)), dma((5,)), dma((units, 3)),
        ],
        compiler_params=pltpu.CompilerParams(
            collective_id=0, has_side_effects=True, vmem_limit_bytes=67043328
        ),
    )(
        gate_weight, up_weight, down_weight, tokens, out_grad, routes.T, route_probs.T, kept_count
    )
    token_grad, prob_grad, weight_grad = pl.pallas_call(
        hand_over,
        out_shape=shapes,
        in_specs=[hbm] * 3,
        out_specs=(hbm,) * 3,
        scratch_shapes=[vmem(s.shape, s.dtype) for s in shapes] + [dma((6,))],
    )(*results)
    return (token_grad, prob_grad.T, weight_grad)


def solution(mesh):
    in_specs = (
        P(("dp", "expert"), None),
        P(("dp", "expert"), None),
        P(("dp", "expert"), None),
        P(("dp", "expert"), None),
        P("dp"),
        P("expert", "dp", None),
        P("expert", "dp", None),
        P("expert", "dp", None),
    )
    out_specs = (P(("dp", "expert"), None), P(("dp", "expert"), None), P("expert", "dp", None))

    line = mesh.shape["dp"] == 4 * CORES and mesh.shape["expert"] == 4
    return jax.shard_map(
        per_device_line if line else per_device,
        mesh=mesh, in_specs=in_specs, out_specs=out_specs, check_vma=False,
    )
```

```python
import jax
import jax.numpy as jnp
from jax import lax
from jax.sharding import PartitionSpec as P
from jax.experimental import pallas as pl
from jax.experimental.pallas import tpu as pltpu

MESH = pl.DeviceIdType.MESH
CORES = 2
SHARES = (2, 1, 2, 1)
GATHER = (0, 2, 3, 1, 4, 5, 7, 6)
EDGE_STEPS = (
    ("more", 0), ("edge", 0, 0), ("rest", 0), ("edge", 0, 1), ("last", 0), ("more", 1),
    ("edge", 0, 2), ("up", 0), ("edge", 2, 0), ("rest", 1), ("last", 1), ("grad", 1, 0, 2),
    ("edge", 2, 1), ("more", 2), ("edge", 2, 2), ("edge", 3, 0), ("up", 1), ("rest", 2),
    ("edge", 3, 1), ("grad", 3, 0, 2), ("edge", 3, 2), ("last", 2), ("grad", 3, 2, 4),
    ("grad", 1, 2, 4), ("edge", 1, 0), ("down", 1), ("grad", 2, 0, 4), ("edge", 1, 1),
    ("edge", 1, 2), ("down", 0), ("grad", 0, 0, 4), ("edge", 4, 0), ("home", 0), ("edge", 4, 1),
    ("home", 1), ("edge", 4, 2), ("up", 2), ("edge", 5, 0), ("grad", 5, 0, 4), ("edge", 5, 1),
    ("edge", 5, 2), ("edge", 7, 0), ("down", 2), ("edge", 7, 1), ("grad", 4, 0, 4), ("edge", 7, 2),
    ("edge", 6, 0), ("home", 2), ("edge", 6, 1), ("edge", 6, 2), ("final", 3), ("up", 3),
    ("down", 3), ("home", 3), ("grad", 6, 0, 4), ("final", 1), ("final", 2), ("grad", 7, 0, 4),
    ("final", 0), ("final", 5), ("final", 4), ("final", 6), ("home_done",), ("final", 7),
)
MIDDLE_STEPS = (
    ("more", 0), ("in", 0), ("mid", 0), ("in", 2), ("in", 3), ("rest", 0), ("in", 1), ("far", 0),
    ("mid", 2), ("last", 0), ("up", 0), ("far", 2), ("in", 4), ("more", 1), ("mid", 3), ("up", 1),
    ("in", 5), ("far", 3), ("rest", 1), ("in", 7), ("mid", 1), ("last", 1), ("in", 6),
    ("grad", 3, 0, 2), ("far", 1), ("grad", 1, 0, 2), ("more", 2), ("rest", 2), ("mid", 4),
    ("last", 2), ("grad", 3, 2, 4), ("relay", 3, 0), ("grad", 1, 2, 4), ("far", 4), ("relay", 3, 1),
    ("relay", 1, 0), ("relay", 1, 1), ("down", 0), ("grad", 0, 0, 4), ("mid", 5), ("far", 5),
    ("mid", 7), ("far", 7), ("down", 1), ("grad", 2, 0, 4), ("mid", 6), ("far", 6), ("relay", 2, 0),
    ("relay", 2, 1), ("up", 2), ("relay_out", 3), ("grad", 5, 0, 4), ("relay_out", 1),
    ("relay", 0, 0), ("final", 3), ("down", 2), ("grad", 4, 0, 4), ("relay", 0, 1),
    ("relay_out", 2), ("final", 1), ("final", 2), ("up", 3), ("down", 3), ("grad", 6, 0, 4),
    ("relay_out", 0), ("relay", 5, 0), ("grad", 7, 0, 4), ("relay", 5, 1), ("home", 0),
    ("final", 0), ("home", 1), ("home", 2), ("relay_out", 5), ("relay", 4, 0), ("home", 3),
    ("final", 5), ("relay", 4, 1), ("relay_out", 4), ("relay", 6, 0), ("final", 4), ("relay", 6, 1),
    ("relay_out", 6), ("relay", 7, 0), ("final", 6), ("relay", 7, 1), ("relay_out", 7),
    ("final", 7), ("home_done",),
)


def dot_f32(left, right):
    return jnp.dot(left, right, preferred_element_type=jnp.float32)


def contract_rows(left, right):
    return lax.dot_general(
        left, right, (((0,), (0,)), ((), ())), preferred_element_type=jnp.float32
    )


def contract_last(left, right):
    return lax.dot_general(
        left, right, (((1,), (1,)), ((), ())), preferred_element_type=jnp.float32
    )


def hop(x, axis, mask, name):
    size = lax.axis_size(axis)
    with jax.named_scope(name):
        return lax.ppermute(x, axis, [(i, i ^ mask) for i in range(size)])


def z_send(x, moves, name):
    pairs = [(a * CORES + c, b * CORES + c) for a, b in moves for c in range(CORES)]
    with jax.named_scope(name):
        return lax.ppermute(x, "dp", pairs)


def xor_blocks(x, blocks):
    me = lax.axis_index("dp")
    rows, width = x.shape
    size = width // blocks
    depth = blocks // CORES
    parts = [x[:, i * size : (i + 1) * size] for i in range(blocks)]
    bit = 1
    while bit < blocks:
        flip = (me & bit) != 0
        parts = [jnp.where(flip, parts[i ^ bit], parts[i]) for i in range(blocks)]
        bit *= 2
    return parts, depth


def to_local(x, blocks):
    parts, depth = xor_blocks(x, blocks)
    return jnp.concatenate([parts[kz * CORES + kc] for kc in range(CORES) for kz in range(depth)], 1)


def from_local(x, blocks):
    depth = blocks // CORES
    size = x.shape[1] // blocks
    cut = [x[:, i * size : (i + 1) * size] for i in range(blocks)]
    natural = [cut[kc * depth + kz] for kz in range(depth) for kc in range(CORES)]
    parts, _ = xor_blocks(jnp.concatenate(natural, 1), blocks)
    return jnp.concatenate(parts, 1)


def spread(x, experts, name):
    if experts != 4:
        return jnp.concatenate([x] + [hop(x, "expert", k, f"{name}{k}") for k in range(1, experts)], 0)
    half = x.shape[0] // 2
    along_x = hop(x, "expert", 1, f"{name}_x")
    along_y = hop(x, "expert", 2, f"{name}_y")
    top = hop(along_x[:half], "expert", 2, f"{name}_xy")
    bottom = hop(along_y[half:], "expert", 1, f"{name}_yx")
    return jnp.concatenate([x, along_x, along_y, top, bottom], 0)


def reduce_line(q, depth, tag):
    def add(a, b):
        return (a.astype(jnp.float32) + b.astype(jnp.float32)).astype(jnp.bfloat16)

    if depth != 4:
        total = q[0].astype(jnp.float32)
        for kz in range(1, depth):
            total = total + hop(q[kz], "dp", kz * CORES, f"{tag}_{kz}").astype(jnp.float32)
        return total.astype(jnp.bfloat16)
    outer, middle, inner = [(3, 2), (0, 1)], [(2, 1), (1, 2)], [(1, 0), (2, 3)]
    a0 = z_send(q[3], outer, f"{tag}_a0")
    a1 = z_send(q[2], outer, f"{tag}_a1")
    a2 = z_send(q[1], outer, f"{tag}_a2")
    b0 = z_send(add(q[2], a0), middle, f"{tag}_b0")
    b1 = z_send(add(q[3], a1), middle, f"{tag}_b1")
    c0 = z_send(add(q[1], b0), inner, f"{tag}_c0")
    total = q[0].astype(jnp.float32) + a2.astype(jnp.float32)
    return (total + b1.astype(jnp.float32) + c0.astype(jnp.float32)).astype(jnp.bfloat16)


def gather_line(own, depth, tag):
    if depth != 4:
        return jnp.concatenate(
            [own] + [hop(own, "dp", kz * CORES, f"{tag}_{kz}") for kz in range(1, depth)], 0
        )
    z = lax.axis_index("dp") // CORES
    inside = (z == 1) | (z == 2)
    outer, middle, inner = [(3, 2), (0, 1)], [(2, 1), (1, 2)], [(1, 0), (2, 3)]
    o = z_send(own, outer, f"{tag}_o")
    m0 = z_send(own, middle, f"{tag}_m0")
    i0 = z_send(own, inner, f"{tag}_i0")
    m1 = z_send(o, middle, f"{tag}_m1")
    i1 = z_send(m0, inner, f"{tag}_i1")
    i2 = z_send(m1, inner, f"{tag}_i2")
    return jnp.concatenate(
        [own, jnp.where(inside, o, i0), jnp.where(inside, m1, i1), jnp.where(inside, m0, i2)], 0
    )


def chunks_of(hidden):
    return 3 if hidden % 384 == 0 else 1


def per_device(
    tokens, out_grad, routes, route_probs, kept_count, gate_weight, up_weight, down_weight
):
    tok_rows, width = tokens.shape
    experts = lax.axis_size("expert")
    groups = lax.axis_size("dp")
    depth = groups // CORES
    hidden = gate_weight.shape[2]
    count = chunks_of(hidden)
    step = hidden // count
    me = lax.axis_index("expert")

    row = me * tok_rows + jnp.arange(tok_rows, dtype=jnp.int32)
    kept = row < kept_count[0]
    masked = jnp.where(kept[:, None], out_grad, jnp.zeros_like(out_grad))
    probs = route_probs.astype(jnp.float32)

    def share(k):
        return jnp.sum(jnp.where(routes == (me ^ k), probs, 0.0), axis=1)

    prob_in = jnp.concatenate(
        [share(0)] + [hop(share(k)[None], "expert", k, f"prob{k}")[0] for k in range(1, experts)]
    )
    rows_in = spread(to_local(tokens, groups), experts, "rows")
    grad_in = spread(to_local(masked, groups), experts, "grad")

    half = width // CORES
    scores = 0.0
    back = [0.0, 0.0]
    sums = []
    for j in range(count):
        cut = slice(j * step, (j + 1) * step)
        own = jnp.concatenate(
            [gate_weight[0][:, cut], up_weight[0][:, cut], down_weight[0][:, cut]], 1
        )
        mine = gather_line(own, depth, f"g{j}")
        other = hop(mine, "dp", 1, f"pair{j}")
        both = (mine, other)
        pre = sum(dot_f32(rows_in[:, i * half : (i + 1) * half], both[i][:, : 2 * step]) for i in range(2))
        cot = sum(dot_f32(grad_in[:, i * half : (i + 1) * half], both[i][:, 2 * step :]) for i in range(2))
        a, b = pre[:, :step], pre[:, step:]
        sig = jax.nn.sigmoid(a)
        act = a * sig * b
        act_low = act.astype(jnp.bfloat16).astype(jnp.float32)
        scores = scores + jnp.sum(act_low * cot, axis=1)
        back_hidden = cot * prob_in[:, None]
        d_gate = (back_hidden * b * sig * (1.0 + a * (1.0 - sig))).astype(jnp.bfloat16)
        d_up = (back_hidden * a * sig).astype(jnp.bfloat16)
        d_both = jnp.concatenate([d_gate, d_up], 1)
        weighted = (act_low * prob_in[:, None]).astype(jnp.bfloat16)
        terms = [
            jnp.concatenate(
                [
                    contract_rows(rows_in[:, i * half : (i + 1) * half], d_both).astype(jnp.bfloat16),
                    contract_rows(grad_in[:, i * half : (i + 1) * half], weighted).astype(jnp.bfloat16),
                ],
                1,
            )
            for i in range(2)
        ]
        arrived = hop(terms[1], "dp", 1, f"swap{j}")
        block = half // depth
        q = tuple(
            (
                terms[0][kz * block : (kz + 1) * block].astype(jnp.float32)
                + arrived[kz * block : (kz + 1) * block].astype(jnp.float32)
            ).astype(jnp.bfloat16)
            for kz in range(depth)
        )
        sums.append(reduce_line(lax.optimization_barrier(q), depth, f"s{j}"))
        back = [back[i] + contract_last(d_both, both[i][:, : 2 * step]) for i in range(2)]

    route_back = jnp.concatenate(back, 1).astype(jnp.bfloat16)
    parts = [route_back[k * tok_rows : (k + 1) * tok_rows] for k in range(experts)]
    scored = [scores[k * tok_rows : (k + 1) * tok_rows] for k in range(experts)]
    for k in range(1, experts):
        parts[k] = hop(parts[k], "expert", k, f"home{k}")
        scored[k] = hop(scored[k][None], "expert", k, f"score{k}")[0]
    token_sum = parts[0].astype(jnp.float32)
    for k in range(1, experts):
        token_sum = token_sum + parts[k].astype(jnp.float32)
    token_grad = from_local(token_sum.astype(jnp.bfloat16), groups)
    prob_grad = sum(
        jnp.where(routes == (me ^ k), scored[k][:, None], 0.0) for k in range(experts)
    ).astype(jnp.bfloat16)
    weight_grad = jnp.concatenate(
        [s[:, i * step : (i + 1) * step] for i in range(3) for s in sums], 1
    )[None]
    return (token_grad, prob_grad, weight_grad)


def add_low(a, b):
    return (a.astype(jnp.float32) + b.astype(jnp.float32)).astype(jnp.bfloat16)


def kernel(
    gate, up_w, down_w, tok, grad, routes_in, probs_in, kept, token_out, prob_out, weight_out,
    w, term, swapped, inbox, du, wt, fac, low_act,
    x, m, xt, mt, q, pc, sb, st, sr, ha, hs, hr, wo, to, po, routes, probs,
    gs, gr, ps, pr, ds, dr, ws, wr, rs, rr, hsem, hrec, lw, ls, os,
):
    dp, e = lax.axis_index("dp"), lax.axis_index("expert")
    z, c = dp // 2, dp % 2
    ey, ex = e // 2, e % 2
    near = {1: 2 * ey + 1 - ex, 2: 2 * (1 - ey) + ex, 3: 2 * (1 - ey) + 1 - ex}
    units = len(w)
    count = units // 2
    rows = w[0].shape[1]
    sizes = [ref.shape[2] for ref in w[1::2]]
    offsets = [sum(sizes[:j]) for j in range(count)]
    hidden = sum(sizes)
    toks, width = tok.shape
    part = width // 2
    partner = z * 2 + 1 - c
    upper = z // 2
    middle = (z > 0) & (z < 3)
    edge = (z == 0) | (z == 3)

    def pos(k):
        return upper * k + (1 - upper) * (3 - k)

    side_in, side_out = upper, 1 - upper
    depth = jnp.where(edge, pos(2), pos(1))
    inn, out = (depth * 2 + c, e), (pos(3) * 2 + c, e)

    def copy(src, dst, s, r, dev):
        return pltpu.make_async_remote_copy(
            src_ref=src, dst_ref=dst, send_sem=s, recv_sem=r, device_id=dev, device_id_type=MESH
        )

    def send(src, dst, s, r, dev):
        copy(src, dst, s, r, dev).start()

    def arrive(dst, s, r):
        copy(dst, dst, s, r, (partner, e)).wait_recv()

    barrier = pltpu.get_barrier_semaphore()

    def greet(dev):
        pl.semaphore_signal(barrier, inc=1, device_id=dev, device_id_type=MESH)

    for dev in [(partner, e), inn] + [(dp, near[k]) for k in (1, 2, 3)]:
        greet(dev)
    pl.when(middle)(lambda: greet(out))

    own = []
    for u in range(units):
        j = u // 2
        at = pl.ds(offsets[j], sizes[j])
        if u % 2 == 0:
            pairs = [(gate, pl.ds(0, sizes[j])), (up_w, pl.ds(sizes[j], sizes[j]))]
        else:
            pairs = [(down_w, pl.ds(0, sizes[j]))]
        own.append([
            pltpu.make_async_copy(ref.at[0, :, at], w[u].at[dp, :, to_at], lw.at[u, k])
            for k, (ref, to_at) in enumerate(pairs)
        ])
    small = [
        pltpu.make_async_copy(routes_in, routes, ls.at[0]),
        pltpu.make_async_copy(probs_in, probs, ls.at[1]),
        pltpu.make_async_copy(tok, x.at[e], ls.at[2]),
        pltpu.make_async_copy(grad.at[:, pl.ds(0, part)], m.at[0, e], ls.at[3]),
        pltpu.make_async_copy(grad.at[:, pl.ds(part, part)], m.at[1, e], ls.at[4]),
    ]
    for d in own[0] + small[:2] + sum(own[1:], []) + small[2:]:
        d.start()
    pl.semaphore_wait(barrier, 5 + jnp.where(middle, 1, 0))

    half = toks // 2
    first, second = pl.ds(0, half), pl.ds(half, half)

    def spread_own(src, dst, at):
        for k, (row, n) in enumerate(((first, 1), (second, 2), (second, 1), (first, 2))):
            send(src(row), dst(e, row), ds.at[at + k], dr.at[at + k], (dp, near[n]))

    def spread_more(dst, at):
        top, low = dst(near[1], first), dst(near[2], second)
        arrive(top, ds.at[at], dr.at[at])
        send(top, top, ds.at[at + 4], dr.at[at + 4], (dp, near[2]))
        arrive(low, ds.at[at + 1], dr.at[at + 1])
        send(low, low, ds.at[at + 5], dr.at[at + 5], (dp, near[1]))

    def spread_rest(dst, at):
        arrive(dst(near[1], second), ds.at[at + 2], dr.at[at + 2])
        arrive(dst(near[2], first), ds.at[at + 3], dr.at[at + 3])

    def spread_done(dst, at):
        arrive(dst(near[3], first), ds.at[at + 4], dr.at[at + 4])
        arrive(dst(near[3], second), ds.at[at + 5], dr.at[at + 5])

    early, late = 1 - upper, upper

    def tok_src(row):
        return tok.at[row, :]

    def grad_src(side):
        return lambda row: grad.at[row, pl.ds(pl.multiple_of(side * part, part), part)]

    def x_dst(i, row):
        return x.at[i, row]

    def m_dst(side):
        return lambda i, row: m.at[side, i, row]

    def own_in(u):
        block = w[u].at[dp]
        send(block, block, gs.at[u, z, 0], gr.at[u, z], inn)

    def own_out(u):
        block = w[u].at[dp]
        send(block, block, gs.at[u, z, 1], gr.at[u, z], out)

    def own_pair(u):
        block = w[u].at[dp]
        send(block, block, ps.at[u, z], pr.at[u, z], (partner, e))

    def gather_pass(u, at, dev):
        block = w[u].at[at * 2 + c]
        arrive(block, gs.at[u, at, 0], gr.at[u, at])
        if dev is not None:
            send(block, block, gs.at[u, at, 0], gr.at[u, at], dev)
        send(block, block, ps.at[u, at], pr.at[u, at], (partner, e))

    def pairs_done(u):
        for i in range(4):
            arrive(w[u].at[i * 2 + 1 - c], ps.at[u, i], pr.at[u, i])

    def block_of(k):
        return ((ey + k // 2) % 2) * 2 + (ex + k % 2) % 2

    def rows_of(i):
        return pl.ds(pl.multiple_of(i * toks, toks), toks)

    expert_rows = lax.broadcasted_iota(jnp.int32, (8, toks), 0)

    def turn_x(lo, hi):
        def body(k, _):
            i = block_of(k)
            xt[:, rows_of(i)] = x[i].T
            return 0

        lax.fori_loop(lo, hi, body, 0)

    def turn_m(side, lo, hi):
        def body(k, _):
            i = block_of(k)
            mt[pl.ds(pl.multiple_of(side * part, part), part), rows_of(i)] = m[side, i].T
            return 0

        lax.fori_loop(lo, hi, body, 0)

    def tall_probs():
        def body(i, _):
            row = jnp.sum(jnp.where(expert_rows == e, q[i], 0.0), axis=0, keepdims=True)
            pc[i] = jnp.broadcast_to(row, (128, toks)).T
            return 0

        lax.fori_loop(0, 4, body, 0)

    def forward_up(j, lo=0, hi=4):
        size, at = sizes[j], offsets[j]

        def body(k, _):
            i = block_of(k)
            here = rows_of(i)
            a = dot_f32(x[i], w[2 * j][:, :, :size].reshape(width, size))
            b = dot_f32(x[i], w[2 * j][:, :, size:].reshape(width, size))
            sig = jax.nn.sigmoid(a)
            act = (a * sig * b).astype(jnp.bfloat16)
            low_act[here, at : at + size] = act
            wt[j][here, :] = (act.astype(jnp.float32) * pc[i][:, :1]).astype(jnp.bfloat16)
            fac[here, 2 * at : 2 * at + size] = b * sig * (1.0 + a * (1.0 - sig))
            fac[here, 2 * at + size : 2 * (at + size)] = a * sig
            return 0

        lax.fori_loop(lo, hi, body, 0)

    def forward_down(j):
        size, at = sizes[j], offsets[j]

        def body(k, _):
            i = block_of(k)
            here = rows_of(i)
            cot = dot_f32(m[0, i], w[2 * j + 1][:4].reshape(part, size))
            cot = cot + dot_f32(m[1, i], w[2 * j + 1][4:].reshape(part, size))
            act = low_act[here, at : at + size].astype(jnp.float32)
            score = jnp.sum(act * cot, axis=1, keepdims=True)
            sb[i] = sb[i] + jnp.broadcast_to(score, (toks, 128))
            back = cot * pc[i][:, :1]
            du[j][here, :size] = (back * fac[here, 2 * at : 2 * at + size]).astype(jnp.bfloat16)
            du[j][here, size:] = (
                back * fac[here, 2 * at + size : 2 * (at + size)]
            ).astype(jnp.bfloat16)
            return 0

        lax.fori_loop(0, 4, body, 0)

    def gradient(u, lo, hi, outer):
        left, right = (xt, du[u // 2]) if u % 2 == 0 else (mt, wt[u // 2])

        def swap(t):
            return copy(
                term[u].at[t * 2 + 1 - c], swapped[u].at[t], ws.at[u, t], wr.at[u, t], (partner, e)
            )

        def ship(t):
            return copy(
                term[u].at[t * 2 + c], inbox[u].at[side_in, t], rs.at[u, t], rr.at[u, side_in, t], inn
            )

        def settle(r):
            t = pos(r)
            arrive(swapped[u].at[t], ws.at[u, t], wr.at[u, t])
            term[u][t * 2 + c] = add_low(term[u][t * 2 + c], swapped[u][t])
            if outer:
                pl.when(r < 3)(lambda: ship(t).start())

        def body(r, _):
            t = pos(r)

            def pair(s, _):
                d = t * 2 + jnp.where(s == 0, 1 - c, c)
                here = pl.ds(pl.multiple_of(d * rows, rows), rows)
                term[u][d] = dot_f32(left[here, :], right[...]).astype(jnp.bfloat16)
                pl.when(s == 0)(lambda: swap(t).start())
                return 0

            lax.fori_loop(0, 2, pair, 0)
            pl.when(r > lo)(lambda: settle(r - 1))
            return 0

        lax.fori_loop(lo, hi, body, 0)
        settle(hi - 1)

    def relay(u, side, t, dev):
        box = inbox[u].at[side, t]
        arrive(box, rs.at[u, t], rr.at[u, side, t])
        term[u][t * 2 + c] = add_low(term[u][t * 2 + c], inbox[u][side, t])
        send(term[u].at[t * 2 + c], box, rs.at[u, t], rr.at[u, side, t], dev)

    def spots(u):
        at = offsets[u // 2]
        return [at, hidden + at] if u % 2 == 0 else [2 * hidden + at]

    def pieces(u):
        cuts = [pl.ds(spot, sizes[u // 2]) for spot in spots(u)]
        return [
            pltpu.make_async_copy(wo.at[:, cut], weight_out.at[0, :, cut], os.at[u, k])
            for k, cut in enumerate(cuts)
        ]

    def final(u, outer):
        size = sizes[u // 2]
        arrive(inbox[u].at[side_out, z], rs.at[u, z], rr.at[u, side_out, z])
        total = term[u][dp].astype(jnp.float32) + inbox[u][side_out, z].astype(jnp.float32)
        if not outer:
            arrive(inbox[u].at[side_in, z], rs.at[u, z], rr.at[u, side_in, z])
            total = total + inbox[u][side_in, z].astype(jnp.float32)
        total = total.astype(jnp.bfloat16)
        for k, spot in enumerate(spots(u)):
            wo[:, spot : spot + size] = total[:, k * size : (k + 1) * size]
        for d in pieces(u):
            d.start()

    def home(j):
        def body(k, _):
            i = block_of(3 - k)
            new = contract_last(du[j][rows_of(i), :], w[2 * j][...].reshape(width, 2 * sizes[j]))
            if j == 0:
                ha[i] = new
            elif j < count - 1:
                ha[i] = ha[i] + new
            else:
                hs[i] = (ha[i] + new).astype(jnp.bfloat16)
                st[i] = sb[i].T[:8, :]

                @pl.when(k < 3)
                def _():
                    copy(hs.at[i], hr.at[e], hsem.at[3 - k], hrec.at[3 - k], (dp, i)).start()
                    copy(st.at[i], sr.at[e], hsem.at[7 - k], hrec.at[7 - k], (dp, i)).start()

            return 0

        lax.fori_loop(0, 4, body, 0)
        if j == count - 1:
            sr[e] = st[e]

    outs = [
        pltpu.make_async_copy(to, token_out, os.at[0, 2]),
        pltpu.make_async_copy(po, prob_out, os.at[1, 2]),
    ]

    def home_done():
        total = hs[e].astype(jnp.float32)
        for k in (1, 2, 3):
            arrive(hr.at[near[k]], hsem.at[k], hrec.at[k])
            total = total + hr[near[k]].astype(jnp.float32)
            arrive(sr.at[near[k]], hsem.at[4 + k], hrec.at[4 + k])
        to[...] = total.astype(jnp.bfloat16)
        top = routes.shape[0]
        score = sum(jnp.where(routes[...] == i, sr[i][:top, :], 0.0) for i in range(4))
        lane = lax.broadcasted_iota(jnp.int32, (top, toks), 1)
        po[...] = jnp.where(e * toks + lane < kept[0], score, 0.0).astype(jnp.bfloat16)
        for d in outs:
            d.start()

    def send_probs():
        sb[...] = jnp.zeros_like(sb)
        for d in small[:2]:
            d.wait()
        lanes = lax.broadcasted_iota(jnp.int32, (8, toks), 1)
        rate = sum(
            jnp.where(
                routes[k : k + 1, :] == expert_rows, probs[k : k + 1, :].astype(jnp.float32), 0.0
            )
            for k in range(routes.shape[0])
        )
        q[e] = jnp.where(e * toks + lanes < kept[0], rate, 0.0)
        for k in (1, 2, 3):
            send(q.at[e], q.at[e], ds.at[17 + k], dr.at[17 + k], (dp, near[k]))

    def get_probs():
        for k in (1, 2, 3):
            arrive(q.at[near[k]], ds.at[17 + k], dr.at[17 + k])
        tall_probs()

    parts = (
        (tok_src, x_dst, 0),
        (grad_src(early), m_dst(early), 6),
        (grad_src(late), m_dst(late), 12),
    )

    def turn(p, lo, hi):
        if p == 0:
            turn_x(lo, hi)
        else:
            turn_m(early if p == 1 else late, lo, hi)

    def after(u):
        n = GATHER.index(u) + 1
        return GATHER[n] if n < units else None

    def more(p):
        spread_more(*parts[p][1:])
        if p + 1 < len(parts):
            spread_own(*parts[p + 1])

    def rest(p):
        spread_rest(*parts[p][1:])
        for d in (small[2:3], small[3:5], [])[p]:
            d.wait()
        turn(p, 0, 3)

    def last(p):
        spread_done(*parts[p][1:])
        turn(p, 3, 4)
        if p == 0:
            get_probs()

    def gather_far(u):
        gather_pass(u, pos(0), out)
        if after(u) is not None:
            own_out(after(u))

    def gather_in(u):
        gather_pass(u, pos(3), inn)
        if after(u) is not None:
            own_in(after(u))

    def up(j):
        pairs_done(2 * j)
        forward_up(j)

    def down(j):
        pairs_done(2 * j + 1)
        forward_down(j)

    def run(steps, outer):
        calls = {
            "more": more,
            "rest": rest,
            "last": last,
            "edge": lambda u, r: gather_pass(u, pos(2 - r), None),
            "in": gather_in,
            "mid": lambda u: gather_pass(u, pos(1), out),
            "far": gather_far,
            "up": up,
            "down": down,
            "grad": lambda u, lo, hi: gradient(u, lo, hi, outer),
            "relay": lambda u, r: relay(u, side_in, pos(r), inn),
            "relay_out": lambda u: relay(u, side_out, pos(3), out),
            "final": lambda u: final(u, outer),
            "home": home,
            "home_done": home_done,
        }
        for name, *args in steps:
            calls[name](*args)

    spread_own(*parts[0])
    for d in own[0]:
        d.wait()
    own_in(0)
    pl.when(middle)(lambda: own_out(0))
    own_pair(0)
    for u in GATHER[1:]:
        for d in own[u]:
            d.wait()
        pl.when(edge)(lambda: own_in(u))
        own_pair(u)
    send_probs()
    pl.when(edge)(lambda: run(EDGE_STEPS, True))
    pl.when(middle)(lambda: run(MIDDLE_STEPS, False))

    def left(ref, s, cond=None):
        d = copy(ref, ref, s, hrec.at[0], (partner, e))
        if cond is None:
            d.wait_send()
        else:
            pl.when(cond)(d.wait_send)

    for n, (_, dst, at) in enumerate(parts):
        for k in range(6):
            left(dst(e, first), ds.at[at + k])
    for k in (1, 2, 3):
        left(q.at[e], ds.at[17 + k])
        left(hs.at[e], hsem.at[k])
        left(st.at[e], hsem.at[4 + k])
    for u in range(units):
        left(w[u].at[dp], gs.at[u, z, 0])
        left(w[u].at[dp], gs.at[u, z, 1], middle)
        for k in (0, 1, 3):
            left(w[u].at[dp], gs.at[u, pos(k), 0], middle)
            left(term[u].at[dp], rs.at[u, pos(k)], middle)
        for k in range(3):
            left(term[u].at[dp], rs.at[u, pos(k)], edge)
        for k in range(4):
            left(w[u].at[dp], ps.at[u, k])
            left(term[u].at[dp], ws.at[u, k])
    for u in range(units):
        for d in pieces(u):
            d.wait()
    for d in outs:
        d.wait()


def hand_over(*refs):
    came, go = refs[:3], refs[3:6]
    held, sem = refs[6:9], refs[9]
    into = [pltpu.make_async_copy(a, b, sem.at[k]) for k, (a, b) in enumerate(zip(came, held))]
    away = [pltpu.make_async_copy(a, b, sem.at[3 + k]) for k, (a, b) in enumerate(zip(held, go))]
    for d in into:
        d.start()
    for a, b in zip(into, away):
        a.wait()
        b.start()
    for d in away:
        d.wait()


def per_device_line(
    tokens, out_grad, routes, route_probs, kept_count, gate_weight, up_weight, down_weight
):
    toks, width = tokens.shape
    rows, hidden = gate_weight.shape[1:]
    sizes = [hidden * k // 6 for k in SHARES]
    cols = [n for size in sizes for n in (2 * size, size)]
    units = len(cols)
    low, full = jnp.bfloat16, jnp.float32
    dma, vmem = pltpu.SemaphoreType.DMA, pltpu.VMEM
    hbm = pl.BlockSpec(memory_space=pl.ANY)
    top = routes.shape[1]
    shapes = (
        jax.ShapeDtypeStruct((toks, width), low),
        jax.ShapeDtypeStruct((top, toks), low),
        jax.ShapeDtypeStruct((1, rows, 3 * hidden), low),
    )
    results = pl.pallas_call(
        kernel,
        out_shape=shapes,
        in_specs=[hbm] * 7 + [pl.BlockSpec(memory_space=pltpu.SMEM)],
        out_specs=(hbm,) * 3,
        scratch_shapes=[
            [vmem((8, rows, n), low) for n in cols],
            [vmem((8, rows, n), low) for n in cols],
            [vmem((4, rows, n), low) for n in cols],
            [vmem((2, 4, rows, n), low) for n in cols],
            [vmem((4 * toks, 2 * n), low) for n in sizes],
            [vmem((4 * toks, n), low) for n in sizes],
            vmem((4 * toks, 2 * hidden), full),
            vmem((4 * toks, hidden), low),
            vmem((4, toks, width), low),
            vmem((2, 4, toks, width // 2), low),
            vmem((width, 4 * toks), low),
            vmem((width, 4 * toks), low),
            vmem((4, 8, toks), full),
            vmem((4, toks, 128), full),
            vmem((4, toks, 128), full),
            vmem((4, 8, toks), full),
            vmem((4, 8, toks), full),
            vmem((4, toks, width), full),
            vmem((4, toks, width), low),
            vmem((4, toks, width), low),
            vmem((rows, 3 * hidden), low),
            vmem((toks, width), low),
            vmem((top, toks), low),
            vmem((top, toks), jnp.int32),
            vmem((top, toks), low),
            dma((units, 4, 2)), dma((units, 4)),
            dma((units, 4)), dma((units, 4)),
            dma((21,)), dma((21,)),
            dma((units, 4)), dma((units, 4)),
            dma((units, 4)), dma((units, 2, 4)),
            dma((8,)), dma((8,)),
            dma((units, 2)), dma((5,)), dma((units, 3)),
        ],
        compiler_params=pltpu.CompilerParams(
            collective_id=0, has_side_effects=True, vmem_limit_bytes=67043328
        ),
    )(
        gate_weight, up_weight, down_weight, tokens, out_grad, routes.T, route_probs.T, kept_count
    )
    token_grad, prob_grad, weight_grad = pl.pallas_call(
        hand_over,
        out_shape=shapes,
        in_specs=[hbm] * 3,
        out_specs=(hbm,) * 3,
        scratch_shapes=[vmem(s.shape, s.dtype) for s in shapes] + [dma((6,))],
    )(*results)
    return (token_grad, prob_grad.T, weight_grad)


def solution(mesh):
    in_specs = (
        P(("dp", "expert"), None),
        P(("dp", "expert"), None),
        P(("dp", "expert"), None),
        P(("dp", "expert"), None),
        P("dp"),
        P("expert", "dp", None),
        P("expert", "dp", None),
        P("expert", "dp", None),
    )
    out_specs = (P(("dp", "expert"), None), P(("dp", "expert"), None), P("expert", "dp", None))

    line = mesh.shape["dp"] == 4 * CORES and mesh.shape["expert"] == 4
    return jax.shard_map(
        per_device_line if line else per_device,
        mesh=mesh, in_specs=in_specs, out_specs=out_specs, check_vma=False,
    )
```

```python
import jax
import jax.numpy as jnp
from jax import lax
from jax.sharding import PartitionSpec as P
from jax.experimental import pallas as pl
from jax.experimental.pallas import tpu as pltpu

MESH = pl.DeviceIdType.MESH
CORES = 2
(
    MORE, REST, LAST, TAKE, PASS_IN, PASS_OUT, PASS_FAR, UP, DOWN,
    GRAD, SUM_IN, SUM_OUT, FINAL, HOME, HOME_DONE, DRAIN,
) = range(16)
SHARES = (2, 1, 2, 1)
GATHER = (0, 2, 3, 1, 4, 5, 7, 6)
EDGE_STEPS = (
    (MORE, 0), (TAKE, 0, 0), (REST, 0), (TAKE, 0, 1), (LAST, 0), (MORE, 1), (TAKE, 0, 2), (UP, 0),
    (TAKE, 2, 0), (REST, 1), (LAST, 1), (GRAD, 1, 0, 2), (TAKE, 2, 1), (MORE, 2), (TAKE, 2, 2),
    (TAKE, 3, 0), (UP, 1), (REST, 2), (TAKE, 3, 1), (GRAD, 3, 0, 2), (TAKE, 3, 2), (LAST, 2),
    (GRAD, 3, 2, 4), (GRAD, 1, 2, 4), (TAKE, 1, 0), (DOWN, 1), (GRAD, 2, 0, 4), (TAKE, 1, 1),
    (TAKE, 1, 2), (DOWN, 0), (GRAD, 0, 0, 4), (TAKE, 4, 0), (HOME, 0), (TAKE, 4, 1), (HOME, 1),
    (TAKE, 4, 2), (UP, 2), (TAKE, 5, 0), (GRAD, 5, 0, 4), (TAKE, 5, 1), (TAKE, 5, 2), (TAKE, 7, 0),
    (DOWN, 2), (TAKE, 7, 1), (GRAD, 4, 0, 4), (TAKE, 7, 2), (TAKE, 6, 0), (HOME, 2), (TAKE, 6, 1),
    (TAKE, 6, 2), (FINAL, 3), (UP, 3), (DOWN, 3), (HOME, 3), (GRAD, 6, 0, 4), (FINAL, 1),
    (FINAL, 2), (GRAD, 7, 0, 4), (FINAL, 0), (FINAL, 5), (FINAL, 4), (FINAL, 6), (HOME_DONE,),
    (FINAL, 7), (DRAIN,),
)
MIDDLE_STEPS = (
    (MORE, 0), (PASS_IN, 0), (PASS_OUT, 0), (PASS_IN, 2), (PASS_IN, 3), (REST, 0), (PASS_IN, 1),
    (PASS_FAR, 0), (PASS_OUT, 2), (LAST, 0), (UP, 0), (PASS_FAR, 2), (PASS_IN, 4), (MORE, 1),
    (PASS_OUT, 3), (UP, 1), (PASS_IN, 5), (PASS_FAR, 3), (REST, 1), (PASS_IN, 7), (PASS_OUT, 1),
    (LAST, 1), (PASS_IN, 6), (GRAD, 3, 0, 2), (PASS_FAR, 1), (GRAD, 1, 0, 2), (MORE, 2), (REST, 2),
    (PASS_OUT, 4), (LAST, 2), (GRAD, 3, 2, 4), (SUM_IN, 3, 0), (GRAD, 1, 2, 4), (PASS_FAR, 4),
    (SUM_IN, 3, 1), (SUM_IN, 1, 0), (SUM_IN, 1, 1), (DOWN, 0), (GRAD, 0, 0, 4), (PASS_OUT, 5),
    (PASS_FAR, 5), (PASS_OUT, 7), (PASS_FAR, 7), (DOWN, 1), (GRAD, 2, 0, 4), (PASS_OUT, 6),
    (PASS_FAR, 6), (SUM_IN, 2, 0), (SUM_IN, 2, 1), (UP, 2), (SUM_OUT, 3), (GRAD, 5, 0, 4),
    (SUM_OUT, 1), (SUM_IN, 0, 0), (FINAL, 3), (DOWN, 2), (GRAD, 4, 0, 4), (SUM_IN, 0, 1),
    (SUM_OUT, 2), (FINAL, 1), (FINAL, 2), (UP, 3), (DOWN, 3), (GRAD, 6, 0, 4), (SUM_OUT, 0),
    (SUM_IN, 5, 0), (GRAD, 7, 0, 4), (SUM_IN, 5, 1), (HOME, 0), (FINAL, 0), (HOME, 1), (HOME, 2),
    (SUM_OUT, 5), (SUM_IN, 4, 0), (HOME, 3), (FINAL, 5), (SUM_IN, 4, 1), (SUM_OUT, 4),
    (SUM_IN, 6, 0), (FINAL, 4), (SUM_IN, 6, 1), (SUM_OUT, 6), (SUM_IN, 7, 0), (FINAL, 6),
    (SUM_IN, 7, 1), (SUM_OUT, 7), (FINAL, 7), (HOME_DONE,), (DRAIN,),
)


def dot_f32(left, right):
    return jnp.dot(left, right, preferred_element_type=jnp.float32)


def contract_rows(left, right):
    return lax.dot_general(
        left, right, (((0,), (0,)), ((), ())), preferred_element_type=jnp.float32
    )


def contract_last(left, right):
    return lax.dot_general(
        left, right, (((1,), (1,)), ((), ())), preferred_element_type=jnp.float32
    )


def hop(x, axis, mask, name):
    size = lax.axis_size(axis)
    with jax.named_scope(name):
        return lax.ppermute(x, axis, [(i, i ^ mask) for i in range(size)])


def z_send(x, moves, name):
    pairs = [(a * CORES + c, b * CORES + c) for a, b in moves for c in range(CORES)]
    with jax.named_scope(name):
        return lax.ppermute(x, "dp", pairs)


def xor_blocks(x, blocks):
    me = lax.axis_index("dp")
    rows, width = x.shape
    size = width // blocks
    depth = blocks // CORES
    parts = [x[:, i * size : (i + 1) * size] for i in range(blocks)]
    bit = 1
    while bit < blocks:
        flip = (me & bit) != 0
        parts = [jnp.where(flip, parts[i ^ bit], parts[i]) for i in range(blocks)]
        bit *= 2
    return parts, depth


def to_local(x, blocks):
    parts, depth = xor_blocks(x, blocks)
    return jnp.concatenate([parts[kz * CORES + kc] for kc in range(CORES) for kz in range(depth)], 1)


def from_local(x, blocks):
    depth = blocks // CORES
    size = x.shape[1] // blocks
    cut = [x[:, i * size : (i + 1) * size] for i in range(blocks)]
    natural = [cut[kc * depth + kz] for kz in range(depth) for kc in range(CORES)]
    parts, _ = xor_blocks(jnp.concatenate(natural, 1), blocks)
    return jnp.concatenate(parts, 1)


def spread(x, experts, name):
    if experts != 4:
        return jnp.concatenate([x] + [hop(x, "expert", k, f"{name}{k}") for k in range(1, experts)], 0)
    half = x.shape[0] // 2
    along_x = hop(x, "expert", 1, f"{name}_x")
    along_y = hop(x, "expert", 2, f"{name}_y")
    top = hop(along_x[:half], "expert", 2, f"{name}_xy")
    bottom = hop(along_y[half:], "expert", 1, f"{name}_yx")
    return jnp.concatenate([x, along_x, along_y, top, bottom], 0)


def reduce_line(q, depth, tag):
    def add(a, b):
        return (a.astype(jnp.float32) + b.astype(jnp.float32)).astype(jnp.bfloat16)

    if depth != 4:
        total = q[0].astype(jnp.float32)
        for kz in range(1, depth):
            total = total + hop(q[kz], "dp", kz * CORES, f"{tag}_{kz}").astype(jnp.float32)
        return total.astype(jnp.bfloat16)
    outer, middle, inner = [(3, 2), (0, 1)], [(2, 1), (1, 2)], [(1, 0), (2, 3)]
    a0 = z_send(q[3], outer, f"{tag}_a0")
    a1 = z_send(q[2], outer, f"{tag}_a1")
    a2 = z_send(q[1], outer, f"{tag}_a2")
    b0 = z_send(add(q[2], a0), middle, f"{tag}_b0")
    b1 = z_send(add(q[3], a1), middle, f"{tag}_b1")
    c0 = z_send(add(q[1], b0), inner, f"{tag}_c0")
    total = q[0].astype(jnp.float32) + a2.astype(jnp.float32)
    return (total + b1.astype(jnp.float32) + c0.astype(jnp.float32)).astype(jnp.bfloat16)


def gather_line(own, depth, tag):
    if depth != 4:
        return jnp.concatenate(
            [own] + [hop(own, "dp", kz * CORES, f"{tag}_{kz}") for kz in range(1, depth)], 0
        )
    z = lax.axis_index("dp") // CORES
    inside = (z == 1) | (z == 2)
    outer, middle, inner = [(3, 2), (0, 1)], [(2, 1), (1, 2)], [(1, 0), (2, 3)]
    o = z_send(own, outer, f"{tag}_o")
    m0 = z_send(own, middle, f"{tag}_m0")
    i0 = z_send(own, inner, f"{tag}_i0")
    m1 = z_send(o, middle, f"{tag}_m1")
    i1 = z_send(m0, inner, f"{tag}_i1")
    i2 = z_send(m1, inner, f"{tag}_i2")
    return jnp.concatenate(
        [own, jnp.where(inside, o, i0), jnp.where(inside, m1, i1), jnp.where(inside, m0, i2)], 0
    )


def chunks_of(hidden):
    return 3 if hidden % 384 == 0 else 1


def per_device(
    tokens, out_grad, routes, route_probs, kept_count, gate_weight, up_weight, down_weight
):
    tok_rows, width = tokens.shape
    experts = lax.axis_size("expert")
    groups = lax.axis_size("dp")
    depth = groups // CORES
    hidden = gate_weight.shape[2]
    count = chunks_of(hidden)
    step = hidden // count
    me = lax.axis_index("expert")

    row = me * tok_rows + jnp.arange(tok_rows, dtype=jnp.int32)
    kept = row < kept_count[0]
    masked = jnp.where(kept[:, None], out_grad, jnp.zeros_like(out_grad))
    probs = route_probs.astype(jnp.float32)

    def share(k):
        return jnp.sum(jnp.where(routes == (me ^ k), probs, 0.0), axis=1)

    prob_in = jnp.concatenate(
        [share(0)] + [hop(share(k)[None], "expert", k, f"prob{k}")[0] for k in range(1, experts)]
    )
    rows_in = spread(to_local(tokens, groups), experts, "rows")
    grad_in = spread(to_local(masked, groups), experts, "grad")

    half = width // CORES
    scores = 0.0
    back = [0.0, 0.0]
    sums = []
    for j in range(count):
        cut = slice(j * step, (j + 1) * step)
        own = jnp.concatenate(
            [gate_weight[0][:, cut], up_weight[0][:, cut], down_weight[0][:, cut]], 1
        )
        mine = gather_line(own, depth, f"g{j}")
        other = hop(mine, "dp", 1, f"pair{j}")
        both = (mine, other)
        pre = sum(dot_f32(rows_in[:, i * half : (i + 1) * half], both[i][:, : 2 * step]) for i in range(2))
        cot = sum(dot_f32(grad_in[:, i * half : (i + 1) * half], both[i][:, 2 * step :]) for i in range(2))
        a, b = pre[:, :step], pre[:, step:]
        sig = jax.nn.sigmoid(a)
        act = a * sig * b
        act_low = act.astype(jnp.bfloat16).astype(jnp.float32)
        scores = scores + jnp.sum(act_low * cot, axis=1)
        back_hidden = cot * prob_in[:, None]
        d_gate = (back_hidden * b * sig * (1.0 + a * (1.0 - sig))).astype(jnp.bfloat16)
        d_up = (back_hidden * a * sig).astype(jnp.bfloat16)
        d_both = jnp.concatenate([d_gate, d_up], 1)
        weighted = (act_low * prob_in[:, None]).astype(jnp.bfloat16)
        terms = [
            jnp.concatenate(
                [
                    contract_rows(rows_in[:, i * half : (i + 1) * half], d_both).astype(jnp.bfloat16),
                    contract_rows(grad_in[:, i * half : (i + 1) * half], weighted).astype(jnp.bfloat16),
                ],
                1,
            )
            for i in range(2)
        ]
        arrived = hop(terms[1], "dp", 1, f"swap{j}")
        block = half // depth
        q = tuple(
            (
                terms[0][kz * block : (kz + 1) * block].astype(jnp.float32)
                + arrived[kz * block : (kz + 1) * block].astype(jnp.float32)
            ).astype(jnp.bfloat16)
            for kz in range(depth)
        )
        sums.append(reduce_line(lax.optimization_barrier(q), depth, f"s{j}"))
        back = [back[i] + contract_last(d_both, both[i][:, : 2 * step]) for i in range(2)]

    route_back = jnp.concatenate(back, 1).astype(jnp.bfloat16)
    parts = [route_back[k * tok_rows : (k + 1) * tok_rows] for k in range(experts)]
    scored = [scores[k * tok_rows : (k + 1) * tok_rows] for k in range(experts)]
    for k in range(1, experts):
        parts[k] = hop(parts[k], "expert", k, f"home{k}")
        scored[k] = hop(scored[k][None], "expert", k, f"score{k}")[0]
    token_sum = parts[0].astype(jnp.float32)
    for k in range(1, experts):
        token_sum = token_sum + parts[k].astype(jnp.float32)
    token_grad = from_local(token_sum.astype(jnp.bfloat16), groups)
    prob_grad = sum(
        jnp.where(routes == (me ^ k), scored[k][:, None], 0.0) for k in range(experts)
    ).astype(jnp.bfloat16)
    weight_grad = jnp.concatenate(
        [s[:, i * step : (i + 1) * step] for i in range(3) for s in sums], 1
    )[None]
    return (token_grad, prob_grad, weight_grad)


def add_low(a, b):
    return (a.astype(jnp.float32) + b.astype(jnp.float32)).astype(jnp.bfloat16)


def kernel(
    gate, up_w, down_w, tok, grad, routes_in, probs_in, kept, token_out, prob_out, weight_out,
    w, term, swapped, inbox, du, wt, fac, low_act,
    x, m, xt, mt, q, pc, sb, st, sr, ha, hs, hr, wo, to, po, routes, probs,
    gs, gr, ps, pr, ds, dr, wr, rr, hsem, hrec, lw, ls, os,
):
    dp, e = lax.axis_index("dp"), lax.axis_index("expert")
    z, c = dp // 2, dp % 2
    ey, ex = e // 2, e % 2
    near = {1: 2 * ey + 1 - ex, 2: 2 * (1 - ey) + ex, 3: 2 * (1 - ey) + 1 - ex}
    units = len(w)
    count = units // 2
    rows = w[0].shape[1]
    sizes = [ref.shape[2] for ref in w[1::2]]
    offsets = [sum(sizes[:j]) for j in range(count)]
    hidden = sum(sizes)
    toks, width = tok.shape
    part = width // 2
    partner = z * 2 + 1 - c
    upper = z // 2
    middle = (z > 0) & (z < 3)
    edge = (z == 0) | (z == 3)

    def pos(k):
        return upper * k + (1 - upper) * (3 - k)

    side_in, side_out = upper, 1 - upper
    depth = jnp.where(edge, pos(2), pos(1))
    inn, out = (depth * 2 + c, e), (pos(3) * 2 + c, e)

    def copy(src, dst, s, r, dev):
        return pltpu.make_async_remote_copy(
            src_ref=src, dst_ref=dst, send_sem=s, recv_sem=r, device_id=dev, device_id_type=MESH
        )

    def send(src, dst, s, r, dev):
        copy(src, dst, s, r, dev).start()

    def arrive(size_of, s):
        copy(size_of, size_of, s, s, (partner, e)).wait_recv()

    def left(size_of, s):
        copy(size_of, size_of, s, s, (partner, e)).wait_send()

    barrier = pltpu.get_barrier_semaphore()

    def greet(dev):
        pl.semaphore_signal(barrier, inc=1, device_id=dev, device_id_type=MESH)

    for dev in [(partner, e), inn] + [(dp, near[k]) for k in (1, 2, 3)]:
        greet(dev)
    pl.when(middle)(lambda: greet(out))

    own = []
    for u in range(units):
        j = u // 2
        at = pl.ds(offsets[j], sizes[j])
        if u % 2 == 0:
            pairs = [(gate, pl.ds(0, sizes[j])), (up_w, pl.ds(sizes[j], sizes[j]))]
        else:
            pairs = [(down_w, pl.ds(0, sizes[j]))]
        own.append([
            pltpu.make_async_copy(ref.at[0, :, at], w[u].at[dp, :, to_at], lw.at[u])
            for ref, to_at in pairs
        ])

    def own_ready(u):
        pltpu.make_async_copy(w[u].at[dp], w[u].at[dp], lw.at[u]).wait()

    small = [
        pltpu.make_async_copy(routes_in, routes, ls.at[0]),
        pltpu.make_async_copy(probs_in, probs, ls.at[1]),
        pltpu.make_async_copy(tok, x.at[e], ls.at[2]),
        pltpu.make_async_copy(grad.at[:, pl.ds(0, part)], m.at[0, e], ls.at[3]),
        pltpu.make_async_copy(grad.at[:, pl.ds(part, part)], m.at[1, e], ls.at[4]),
    ]
    for d in own[0] + small[:2] + sum(own[1:], []) + small[2:]:
        d.start()
    pl.semaphore_wait(barrier, 5 + jnp.where(middle, 1, 0))

    half = toks // 2
    first, second, whole = pl.ds(0, half), pl.ds(half, half), pl.ds(0, toks)

    def spread_own(src, dst, p):
        for row, n, stage in ((first, 1, 0), (second, 2, 0), (second, 1, 1), (first, 2, 1)):
            send(src(row), dst(e, row), ds.at[p], dr.at[p, stage], (dp, near[n]))

    def spread_more(dst, p):
        arrive(dst(e, whole), dr.at[p, 0])
        for n, row, far in ((1, first, 2), (2, second, 1)):
            block = dst(near[n], row)
            send(block, block, ds.at[p], dr.at[p, 2], (dp, near[far]))

    def spread_rest(dst, p):
        arrive(dst(e, whole), dr.at[p, 1])

    def spread_done(dst, p):
        arrive(dst(e, whole), dr.at[p, 2])

    early, late = 1 - upper, upper

    def tok_src(row):
        return tok.at[row, :]

    def grad_src(side):
        return lambda row: grad.at[row, pl.ds(pl.multiple_of(side * part, part), part)]

    def x_dst(i, row):
        return x.at[i, row]

    def m_dst(side):
        return lambda i, row: m.at[side, i, row]

    def own_in(u):
        block = w[u].at[dp]
        send(block, block, gs.at[u], gr.at[u, jnp.where(edge, 0, 1)], inn)

    def own_out(u):
        block = w[u].at[dp]
        send(block, block, gs.at[u], gr.at[u, 0], out)

    def own_pair(u):
        block = w[u].at[dp]
        send(block, block, ps.at[u], pr.at[u], (partner, e))

    def gather_pass(u, at, stage, onward=None):
        block = w[u].at[at * 2 + c]
        arrive(block, gr.at[u, stage])
        if onward is not None:
            dev, later = onward
            send(block, block, gs.at[u], gr.at[u, later], dev)
        send(block, block, ps.at[u], pr.at[u], (partner, e))

    def pairs_done(u):
        arrive(w[u].at[pl.ds(0, 4)], pr.at[u])

    def block_of(k):
        return ((ey + k // 2) % 2) * 2 + (ex + k % 2) % 2

    def rows_of(i):
        return pl.ds(pl.multiple_of(i * toks, toks), toks)

    expert_rows = lax.broadcasted_iota(jnp.int32, (8, toks), 0)

    def turn_x(lo, hi):
        def body(k, _):
            i = block_of(k)
            xt[:, rows_of(i)] = x[i].T
            return 0

        lax.fori_loop(lo, hi, body, 0)

    def turn_m(side, lo, hi):
        def body(k, _):
            i = block_of(k)
            mt[pl.ds(pl.multiple_of(side * part, part), part), rows_of(i)] = m[side, i].T
            return 0

        lax.fori_loop(lo, hi, body, 0)

    def tall_probs():
        def body(i, _):
            row = jnp.sum(jnp.where(expert_rows == e, q[i], 0.0), axis=0, keepdims=True)
            pc[i] = jnp.broadcast_to(row, (128, toks)).T
            return 0

        lax.fori_loop(0, 4, body, 0)

    def forward_up(j, lo=0, hi=4):
        size, at = sizes[j], offsets[j]

        def body(k, _):
            i = block_of(k)
            here = rows_of(i)
            a = dot_f32(x[i], w[2 * j][:, :, :size].reshape(width, size))
            b = dot_f32(x[i], w[2 * j][:, :, size:].reshape(width, size))
            sig = jax.nn.sigmoid(a)
            act = (a * sig * b).astype(jnp.bfloat16)
            low_act[here, at : at + size] = act
            wt[j][here, :] = (act.astype(jnp.float32) * pc[i][:, :1]).astype(jnp.bfloat16)
            fac[here, 2 * at : 2 * at + size] = b * sig * (1.0 + a * (1.0 - sig))
            fac[here, 2 * at + size : 2 * (at + size)] = a * sig
            return 0

        lax.fori_loop(lo, hi, body, 0)

    def forward_down(j):
        size, at = sizes[j], offsets[j]

        def body(k, _):
            i = block_of(k)
            here = rows_of(i)
            cot = dot_f32(m[0, i], w[2 * j + 1][:4].reshape(part, size))
            cot = cot + dot_f32(m[1, i], w[2 * j + 1][4:].reshape(part, size))
            act = low_act[here, at : at + size].astype(jnp.float32)
            score = jnp.sum(act * cot, axis=1, keepdims=True)
            sb[i] = sb[i] + jnp.broadcast_to(score, (toks, 128))
            back = cot * pc[i][:, :1]
            du[j][here, :size] = (back * fac[here, 2 * at : 2 * at + size]).astype(jnp.bfloat16)
            du[j][here, size:] = (
                back * fac[here, 2 * at + size : 2 * (at + size)]
            ).astype(jnp.bfloat16)
            return 0

        lax.fori_loop(0, 4, body, 0)

    def gradient(u, lo, hi, outer):
        left, right = (xt, du[u // 2]) if u % 2 == 0 else (mt, wt[u // 2])

        def swap(t):
            return copy(
                term[u].at[t * 2 + 1 - c], swapped[u].at[t], ps.at[u], wr.at[u, t], (partner, e)
            )

        def ship(t, r):
            return copy(term[u].at[t * 2 + c], inbox[u].at[side_in, t], gs.at[u], rr.at[u, r], inn)

        def settle(r):
            t = pos(r)
            arrive(swapped[u].at[t], wr.at[u, t])
            term[u][t * 2 + c] = add_low(term[u][t * 2 + c], swapped[u][t])
            if outer:
                pl.when(r < 3)(lambda: ship(t, r).start())

        def body(r, _):
            t = pos(r)

            def pair(s, _):
                d = t * 2 + jnp.where(s == 0, 1 - c, c)
                here = pl.ds(pl.multiple_of(d * rows, rows), rows)
                term[u][d] = dot_f32(left[here, :], right[...]).astype(jnp.bfloat16)
                pl.when(s == 0)(lambda: swap(t).start())
                return 0

            lax.fori_loop(0, 2, pair, 0)
            pl.when(r > lo)(lambda: settle(r - 1))
            return 0

        lax.fori_loop(lo, hi, body, 0)
        settle(hi - 1)

    def relay(u, side, t, stage, dev, later):
        arrive(term[u].at[dp], rr.at[u, stage])
        term[u][t * 2 + c] = add_low(term[u][t * 2 + c], inbox[u][side, t])
        send(term[u].at[t * 2 + c], inbox[u].at[side, t], gs.at[u], rr.at[u, later], dev)

    def spots(u):
        at = offsets[u // 2]
        return [at, hidden + at] if u % 2 == 0 else [2 * hidden + at]

    def pieces(u):
        cuts = [pl.ds(spot, sizes[u // 2]) for spot in spots(u)]
        return [
            pltpu.make_async_copy(wo.at[:, cut], weight_out.at[0, :, cut], os.at[0])
            for cut in cuts
        ]

    def final(u, outer):
        size = sizes[u // 2]
        if outer:
            arrive(term[u].at[dp], rr.at[u, 3])
        else:
            arrive(term[u].at[pl.ds(0, 2)], rr.at[u, 2])
        total = term[u][dp].astype(jnp.float32) + inbox[u][side_out, z].astype(jnp.float32)
        if not outer:
            total = total + inbox[u][side_in, z].astype(jnp.float32)
        total = total.astype(jnp.bfloat16)
        for k, spot in enumerate(spots(u)):
            wo[:, spot : spot + size] = total[:, k * size : (k + 1) * size]
        for d in pieces(u):
            d.start()

    def home(j):
        def body(k, _):
            i = block_of(3 - k)
            new = contract_last(du[j][rows_of(i), :], w[2 * j][...].reshape(width, 2 * sizes[j]))
            if j == 0:
                ha[i] = new
            elif j < count - 1:
                ha[i] = ha[i] + new
            else:
                hs[i] = (ha[i] + new).astype(jnp.bfloat16)
                st[i] = sb[i].T[:8, :]

                @pl.when(k < 3)
                def _():
                    send(hs.at[i], hr.at[e], hsem.at[0], hrec.at[0], (dp, i))
                    send(st.at[i], sr.at[e], hsem.at[1], hrec.at[1], (dp, i))

            return 0

        lax.fori_loop(0, 4, body, 0)
        if j == count - 1:
            sr[e] = st[e]

    outs = [
        pltpu.make_async_copy(to, token_out, os.at[1]),
        pltpu.make_async_copy(po, prob_out, os.at[2]),
    ]

    def home_done():
        arrive(hr.at[pl.ds(0, 3)], hrec.at[0])
        arrive(sr.at[pl.ds(0, 3)], hrec.at[1])
        total = hs[e].astype(jnp.float32)
        for k in (1, 2, 3):
            total = total + hr[near[k]].astype(jnp.float32)
        to[...] = total.astype(jnp.bfloat16)
        top = routes.shape[0]
        score = sum(jnp.where(routes[...] == i, sr[i][:top, :], 0.0) for i in range(4))
        lane = lax.broadcasted_iota(jnp.int32, (top, toks), 1)
        po[...] = jnp.where(e * toks + lane < kept[0], score, 0.0).astype(jnp.bfloat16)
        for d in outs:
            d.start()

    def send_probs():
        sb[...] = jnp.zeros_like(sb)
        for d in small[:2]:
            d.wait()
        lanes = lax.broadcasted_iota(jnp.int32, (8, toks), 1)
        rate = sum(
            jnp.where(
                routes[k : k + 1, :] == expert_rows, probs[k : k + 1, :].astype(jnp.float32), 0.0
            )
            for k in range(routes.shape[0])
        )
        q[e] = jnp.where(e * toks + lanes < kept[0], rate, 0.0)
        for k in (1, 2, 3):
            send(q.at[e], q.at[e], ds.at[3], dr.at[3, 0], (dp, near[k]))

    def get_probs():
        arrive(q.at[pl.ds(0, 3)], dr.at[3, 0])
        tall_probs()

    parts = (
        (tok_src, x_dst, 0),
        (grad_src(early), m_dst(early), 1),
        (grad_src(late), m_dst(late), 2),
    )

    def turn(p, lo, hi):
        if p == 0:
            turn_x(lo, hi)
        else:
            turn_m(early if p == 1 else late, lo, hi)

    def after(u):
        n = GATHER.index(u) + 1
        return GATHER[n] if n < units else None

    def more(p):
        spread_more(*parts[p][1:])
        if p + 1 < len(parts):
            spread_own(*parts[p + 1])

    def rest(p):
        spread_rest(*parts[p][1:])
        for d in (small[2:3], small[3:5], [])[p]:
            d.wait()
        turn(p, 0, 3)

    def last(p):
        spread_done(*parts[p][1:])
        turn(p, 3, 4)
        if p == 0:
            get_probs()

    def gather_far(u):
        gather_pass(u, pos(0), 2, (out, 2))
        if after(u) is not None:
            own_out(after(u))

    def gather_in(u):
        gather_pass(u, pos(3), 0, (inn, 2))
        if after(u) is not None:
            own_in(after(u))

    def up(j):
        pairs_done(2 * j)
        forward_up(j)

    def down(j):
        pairs_done(2 * j + 1)
        forward_down(j)

    def drain(outer):
        left(x.at[pl.ds(0, 3)], ds.at[0])
        for p in (1, 2):
            left(m.at[0, pl.ds(0, 3)], ds.at[p])
        left(q.at[pl.ds(0, 3)], ds.at[3])
        left(hs.at[pl.ds(0, 3)], hsem.at[0])
        left(st.at[pl.ds(0, 3)], hsem.at[1])
        for u in range(units):
            left(w[u].at[pl.ds(0, 4 if outer else 8)], gs.at[u])
            left(w[u], ps.at[u])

    def run(steps, outer):
        calls = {
            MORE: more,
            REST: rest,
            LAST: last,
            TAKE: lambda u, r: gather_pass(u, pos(2 - r), r),
            PASS_IN: gather_in,
            PASS_OUT: lambda u: gather_pass(u, pos(1), 1, (out, 1)),
            PASS_FAR: gather_far,
            UP: up,
            DOWN: down,
            GRAD: lambda u, lo, hi: gradient(u, lo, hi, outer),
            SUM_IN: lambda u, r: relay(u, side_in, pos(r), r, inn, 3 - r),
            SUM_OUT: lambda u: relay(u, side_out, pos(3), 3, out, 3),
            FINAL: lambda u: final(u, outer),
            HOME: home,
            HOME_DONE: home_done,
            DRAIN: lambda: drain(outer),
        }
        for name, *args in steps:
            calls[name](*args)

    spread_own(*parts[0])
    own_ready(0)
    own_in(0)
    pl.when(middle)(lambda: own_out(0))
    own_pair(0)
    for u in GATHER[1:]:
        own_ready(u)
        pl.when(edge)(lambda: own_in(u))
        own_pair(u)
    send_probs()
    pl.when(edge)(lambda: run(EDGE_STEPS, True))
    pl.when(middle)(lambda: run(MIDDLE_STEPS, False))

    pltpu.make_async_copy(wo, weight_out.at[0], os.at[0]).wait()
    for d in outs:
        d.wait()


def hand_over(*refs):
    came, go = refs[:3], refs[3:6]
    held, sem = refs[6:9], refs[9]
    into = [pltpu.make_async_copy(a, b, sem.at[k]) for k, (a, b) in enumerate(zip(came, held))]
    away = [pltpu.make_async_copy(a, b, sem.at[3 + k]) for k, (a, b) in enumerate(zip(held, go))]
    for d in into:
        d.start()
    for a, b in zip(into, away):
        a.wait()
        b.start()
    for d in away:
        d.wait()


def per_device_line(
    tokens, out_grad, routes, route_probs, kept_count, gate_weight, up_weight, down_weight
):
    toks, width = tokens.shape
    rows, hidden = gate_weight.shape[1:]
    sizes = [hidden * k // 6 for k in SHARES]
    cols = [n for size in sizes for n in (2 * size, size)]
    units = len(cols)
    low, full = jnp.bfloat16, jnp.float32
    dma, vmem = pltpu.SemaphoreType.DMA, pltpu.VMEM
    hbm = pl.BlockSpec(memory_space=pl.ANY)
    top = routes.shape[1]
    shapes = (
        jax.ShapeDtypeStruct((toks, width), low),
        jax.ShapeDtypeStruct((top, toks), low),
        jax.ShapeDtypeStruct((1, rows, 3 * hidden), low),
    )
    results = pl.pallas_call(
        kernel,
        out_shape=shapes,
        in_specs=[hbm] * 7 + [pl.BlockSpec(memory_space=pltpu.SMEM)],
        out_specs=(hbm,) * 3,
        scratch_shapes=[
            [vmem((8, rows, n), low) for n in cols],
            [vmem((8, rows, n), low) for n in cols],
            [vmem((4, rows, n), low) for n in cols],
            [vmem((2, 4, rows, n), low) for n in cols],
            [vmem((4 * toks, 2 * n), low) for n in sizes],
            [vmem((4 * toks, n), low) for n in sizes],
            vmem((4 * toks, 2 * hidden), full),
            vmem((4 * toks, hidden), low),
            vmem((4, toks, width), low),
            vmem((2, 4, toks, width // 2), low),
            vmem((width, 4 * toks), low),
            vmem((width, 4 * toks), low),
            vmem((4, 8, toks), full),
            vmem((4, toks, 128), full),
            vmem((4, toks, 128), full),
            vmem((4, 8, toks), full),
            vmem((4, 8, toks), full),
            vmem((4, toks, width), full),
            vmem((4, toks, width), low),
            vmem((4, toks, width), low),
            vmem((rows, 3 * hidden), low),
            vmem((toks, width), low),
            vmem((top, toks), low),
            vmem((top, toks), jnp.int32),
            vmem((top, toks), low),
            dma((units,)), dma((units, 3)), dma((units,)), dma((units,)),
            dma((4,)), dma((4, 3)), dma((units, 4)), dma((units, 4)),
            dma((2,)), dma((2,)), dma((units,)), dma((5,)), dma((3,)),
        ],
        compiler_params=pltpu.CompilerParams(
            collective_id=0, has_side_effects=True, vmem_limit_bytes=67043328
        ),
    )(
        gate_weight, up_weight, down_weight, tokens, out_grad, routes.T, route_probs.T, kept_count
    )
    token_grad, prob_grad, weight_grad = pl.pallas_call(
        hand_over,
        out_shape=shapes,
        in_specs=[hbm] * 3,
        out_specs=(hbm,) * 3,
        scratch_shapes=[vmem(s.shape, s.dtype) for s in shapes] + [dma((6,))],
    )(*results)
    return (token_grad, prob_grad.T, weight_grad)


def solution(mesh):
    in_specs = (
        P(("dp", "expert"), None),
        P(("dp", "expert"), None),
        P(("dp", "expert"), None),
        P(("dp", "expert"), None),
        P("dp"),
        P("expert", "dp", None),
        P("expert", "dp", None),
        P("expert", "dp", None),
    )
    out_specs = (P(("dp", "expert"), None), P(("dp", "expert"), None), P("expert", "dp", None))

    line = mesh.shape["dp"] == 4 * CORES and mesh.shape["expert"] == 4
    return jax.shard_map(
        per_device_line if line else per_device,
        mesh=mesh, in_specs=in_specs, out_specs=out_specs, check_vma=False,
    )
```

```python
import jax
import jax.numpy as jnp
from jax import lax
from jax.sharding import PartitionSpec as P
from jax.experimental import pallas as pl
from jax.experimental.pallas import tpu as pltpu

MESH = pl.DeviceIdType.MESH
CORES = 2
(
    SHIP, MORE, REST, LAST, TAKE, PASS_IN, PASS_OUT, PASS_FAR, UP,
    DOWN, GRAD, SUM_IN, SUM_OUT, FINAL, HOME, HOME_DONE, DRAIN,
) = range(17)
SHARES = (2, 1, 2, 1)
GATHER = (0, 2, 1, 3, 4, 5, 6, 7)
FILLER = 1
HELD = (6, 5, 7)
EDGE_STEPS = (
    (TAKE, 0, 0), (MORE, 0), (TAKE, 1, 0), (REST, 0), (TAKE, 0, 1), (TAKE, 1, 1), (LAST, 0),
    (MORE, 1), (TAKE, 0, 2), (UP, 0), (TAKE, 2, 0), (REST, 1), (LAST, 1), (GRAD, 1, 0, 2),
    (TAKE, 2, 1), (MORE, 2), (TAKE, 2, 2), (TAKE, 3, 0), (UP, 1), (TAKE, 3, 1), (REST, 2),
    (GRAD, 3, 0, 2), (LAST, 2), (GRAD, 3, 2, 4), (TAKE, 1, 2), (TAKE, 3, 2), (GRAD, 1, 2, 4),
    (DOWN, 0), (GRAD, 0, 0, 4), (TAKE, 4, 0), (DOWN, 1), (GRAD, 2, 0, 4), (TAKE, 4, 1), (HOME, 0),
    (HOME, 1), (TAKE, 4, 2), (UP, 2), (TAKE, 5, 0), (GRAD, 5, 0, 2), (GRAD, 5, 2, 4), (TAKE, 5, 1),
    (TAKE, 5, 2), (DOWN, 2), (TAKE, 6, 0), (GRAD, 4, 0, 4), (TAKE, 6, 1), (HOME, 2), (TAKE, 6, 2),
    (TAKE, 7, 0), (TAKE, 7, 1), (UP, 3), (TAKE, 7, 2), (GRAD, 7, 0, 4), (DOWN, 3), (HOME, 3),
    (FINAL, 0), (GRAD, 6, 0, 4), (SHIP, 6, 0), (SHIP, 5, 0), (SHIP, 7, 0), (SHIP, 6, 1),
    (SHIP, 5, 1), (SHIP, 7, 1), (SHIP, 6, 2), (SHIP, 5, 2), (SHIP, 7, 2), (FINAL, 3), (FINAL, 1),
    (FINAL, 2), (FINAL, 4), (FINAL, 6), (FINAL, 5), (FINAL, 7), (HOME_DONE,), (DRAIN,),
)
MIDDLE_STEPS = (
    (PASS_IN, 0), (PASS_OUT, 0), (MORE, 0), (PASS_IN, 2), (PASS_OUT, 1), (PASS_IN, 1), (PASS_IN, 3),
    (REST, 0), (PASS_FAR, 0), (PASS_OUT, 2), (PASS_IN, 4), (LAST, 0), (UP, 0), (PASS_FAR, 2),
    (PASS_OUT, 3), (PASS_IN, 5), (MORE, 1), (UP, 1), (PASS_FAR, 1), (PASS_IN, 6), (REST, 1),
    (PASS_FAR, 3), (PASS_IN, 7), (LAST, 1), (GRAD, 3, 0, 2), (GRAD, 1, 0, 2), (MORE, 2),
    (PASS_OUT, 4), (REST, 2), (LAST, 2), (DOWN, 0), (PASS_FAR, 4), (PASS_OUT, 5), (GRAD, 0, 0, 4),
    (PASS_FAR, 5), (DOWN, 1), (PASS_OUT, 6), (GRAD, 2, 0, 4), (PASS_FAR, 6), (HOME, 0),
    (PASS_OUT, 7), (PASS_FAR, 7), (SUM_IN, 0, 0), (GRAD, 3, 2, 4), (SUM_IN, 3, 0), (SUM_IN, 3, 1),
    (GRAD, 1, 2, 4), (SUM_IN, 1, 0), (SUM_IN, 1, 1), (HOME, 1), (SUM_IN, 0, 1), (UP, 2),
    (SUM_OUT, 0), (DOWN, 2), (SUM_OUT, 3), (GRAD, 4, 0, 4), (SUM_IN, 2, 0), (SUM_OUT, 1),
    (FINAL, 3), (HOME, 2), (SUM_IN, 2, 1), (FINAL, 1), (GRAD, 5, 0, 2), (GRAD, 5, 2, 4), (UP, 3),
    (FINAL, 0), (DOWN, 3), (SUM_OUT, 2), (SUM_IN, 4, 0), (HOME, 3), (FINAL, 2), (GRAD, 6, 0, 4),
    (GRAD, 7, 0, 4), (SUM_IN, 4, 1), (SUM_OUT, 4), (SUM_IN, 6, 0), (FINAL, 4), (SUM_IN, 5, 0),
    (SUM_IN, 7, 0), (SUM_OUT, 6), (SUM_IN, 6, 1), (SUM_OUT, 5), (SUM_OUT, 7), (SUM_IN, 5, 1),
    (SUM_IN, 7, 1), (FINAL, 6), (HOME_DONE,), (FINAL, 5), (FINAL, 7), (DRAIN,),
)


def dot_f32(left, right):
    return jnp.dot(left, right, preferred_element_type=jnp.float32)


def contract_rows(left, right):
    return lax.dot_general(
        left, right, (((0,), (0,)), ((), ())), preferred_element_type=jnp.float32
    )


def contract_last(left, right):
    return lax.dot_general(
        left, right, (((1,), (1,)), ((), ())), preferred_element_type=jnp.float32
    )


def hop(x, axis, mask, name):
    size = lax.axis_size(axis)
    with jax.named_scope(name):
        return lax.ppermute(x, axis, [(i, i ^ mask) for i in range(size)])


def z_send(x, moves, name):
    pairs = [(a * CORES + c, b * CORES + c) for a, b in moves for c in range(CORES)]
    with jax.named_scope(name):
        return lax.ppermute(x, "dp", pairs)


def xor_blocks(x, blocks):
    me = lax.axis_index("dp")
    rows, width = x.shape
    size = width // blocks
    depth = blocks // CORES
    parts = [x[:, i * size : (i + 1) * size] for i in range(blocks)]
    bit = 1
    while bit < blocks:
        flip = (me & bit) != 0
        parts = [jnp.where(flip, parts[i ^ bit], parts[i]) for i in range(blocks)]
        bit *= 2
    return parts, depth


def to_local(x, blocks):
    parts, depth = xor_blocks(x, blocks)
    return jnp.concatenate([parts[kz * CORES + kc] for kc in range(CORES) for kz in range(depth)], 1)


def from_local(x, blocks):
    depth = blocks // CORES
    size = x.shape[1] // blocks
    cut = [x[:, i * size : (i + 1) * size] for i in range(blocks)]
    natural = [cut[kc * depth + kz] for kz in range(depth) for kc in range(CORES)]
    parts, _ = xor_blocks(jnp.concatenate(natural, 1), blocks)
    return jnp.concatenate(parts, 1)


def spread(x, experts, name):
    if experts != 4:
        return jnp.concatenate([x] + [hop(x, "expert", k, f"{name}{k}") for k in range(1, experts)], 0)
    half = x.shape[0] // 2
    along_x = hop(x, "expert", 1, f"{name}_x")
    along_y = hop(x, "expert", 2, f"{name}_y")
    top = hop(along_x[:half], "expert", 2, f"{name}_xy")
    bottom = hop(along_y[half:], "expert", 1, f"{name}_yx")
    return jnp.concatenate([x, along_x, along_y, top, bottom], 0)


def reduce_line(q, depth, tag):
    def add(a, b):
        return (a.astype(jnp.float32) + b.astype(jnp.float32)).astype(jnp.bfloat16)

    if depth != 4:
        total = q[0].astype(jnp.float32)
        for kz in range(1, depth):
            total = total + hop(q[kz], "dp", kz * CORES, f"{tag}_{kz}").astype(jnp.float32)
        return total.astype(jnp.bfloat16)
    outer, middle, inner = [(3, 2), (0, 1)], [(2, 1), (1, 2)], [(1, 0), (2, 3)]
    a0 = z_send(q[3], outer, f"{tag}_a0")
    a1 = z_send(q[2], outer, f"{tag}_a1")
    a2 = z_send(q[1], outer, f"{tag}_a2")
    b0 = z_send(add(q[2], a0), middle, f"{tag}_b0")
    b1 = z_send(add(q[3], a1), middle, f"{tag}_b1")
    c0 = z_send(add(q[1], b0), inner, f"{tag}_c0")
    total = q[0].astype(jnp.float32) + a2.astype(jnp.float32)
    return (total + b1.astype(jnp.float32) + c0.astype(jnp.float32)).astype(jnp.bfloat16)


def gather_line(own, depth, tag):
    if depth != 4:
        return jnp.concatenate(
            [own] + [hop(own, "dp", kz * CORES, f"{tag}_{kz}") for kz in range(1, depth)], 0
        )
    z = lax.axis_index("dp") // CORES
    inside = (z == 1) | (z == 2)
    outer, middle, inner = [(3, 2), (0, 1)], [(2, 1), (1, 2)], [(1, 0), (2, 3)]
    o = z_send(own, outer, f"{tag}_o")
    m0 = z_send(own, middle, f"{tag}_m0")
    i0 = z_send(own, inner, f"{tag}_i0")
    m1 = z_send(o, middle, f"{tag}_m1")
    i1 = z_send(m0, inner, f"{tag}_i1")
    i2 = z_send(m1, inner, f"{tag}_i2")
    return jnp.concatenate(
        [own, jnp.where(inside, o, i0), jnp.where(inside, m1, i1), jnp.where(inside, m0, i2)], 0
    )


def chunks_of(hidden):
    return 3 if hidden % 384 == 0 else 1


def per_device(
    tokens, out_grad, routes, route_probs, kept_count, gate_weight, up_weight, down_weight
):
    tok_rows, width = tokens.shape
    experts = lax.axis_size("expert")
    groups = lax.axis_size("dp")
    depth = groups // CORES
    hidden = gate_weight.shape[2]
    count = chunks_of(hidden)
    step = hidden // count
    me = lax.axis_index("expert")

    row = me * tok_rows + jnp.arange(tok_rows, dtype=jnp.int32)
    kept = row < kept_count[0]
    masked = jnp.where(kept[:, None], out_grad, jnp.zeros_like(out_grad))
    probs = route_probs.astype(jnp.float32)

    def share(k):
        return jnp.sum(jnp.where(routes == (me ^ k), probs, 0.0), axis=1)

    prob_in = jnp.concatenate(
        [share(0)] + [hop(share(k)[None], "expert", k, f"prob{k}")[0] for k in range(1, experts)]
    )
    rows_in = spread(to_local(tokens, groups), experts, "rows")
    grad_in = spread(to_local(masked, groups), experts, "grad")

    half = width // CORES
    scores = 0.0
    back = [0.0, 0.0]
    sums = []
    for j in range(count):
        cut = slice(j * step, (j + 1) * step)
        own = jnp.concatenate(
            [gate_weight[0][:, cut], up_weight[0][:, cut], down_weight[0][:, cut]], 1
        )
        mine = gather_line(own, depth, f"g{j}")
        other = hop(mine, "dp", 1, f"pair{j}")
        both = (mine, other)
        pre = sum(dot_f32(rows_in[:, i * half : (i + 1) * half], both[i][:, : 2 * step]) for i in range(2))
        cot = sum(dot_f32(grad_in[:, i * half : (i + 1) * half], both[i][:, 2 * step :]) for i in range(2))
        a, b = pre[:, :step], pre[:, step:]
        sig = jax.nn.sigmoid(a)
        act = a * sig * b
        act_low = act.astype(jnp.bfloat16).astype(jnp.float32)
        scores = scores + jnp.sum(act_low * cot, axis=1)
        back_hidden = cot * prob_in[:, None]
        d_gate = (back_hidden * b * sig * (1.0 + a * (1.0 - sig))).astype(jnp.bfloat16)
        d_up = (back_hidden * a * sig).astype(jnp.bfloat16)
        d_both = jnp.concatenate([d_gate, d_up], 1)
        weighted = (act_low * prob_in[:, None]).astype(jnp.bfloat16)
        terms = [
            jnp.concatenate(
                [
                    contract_rows(rows_in[:, i * half : (i + 1) * half], d_both).astype(jnp.bfloat16),
                    contract_rows(grad_in[:, i * half : (i + 1) * half], weighted).astype(jnp.bfloat16),
                ],
                1,
            )
            for i in range(2)
        ]
        arrived = hop(terms[1], "dp", 1, f"swap{j}")
        block = half // depth
        q = tuple(
            (
                terms[0][kz * block : (kz + 1) * block].astype(jnp.float32)
                + arrived[kz * block : (kz + 1) * block].astype(jnp.float32)
            ).astype(jnp.bfloat16)
            for kz in range(depth)
        )
        sums.append(reduce_line(lax.optimization_barrier(q), depth, f"s{j}"))
        back = [back[i] + contract_last(d_both, both[i][:, : 2 * step]) for i in range(2)]

    route_back = jnp.concatenate(back, 1).astype(jnp.bfloat16)
    parts = [route_back[k * tok_rows : (k + 1) * tok_rows] for k in range(experts)]
    scored = [scores[k * tok_rows : (k + 1) * tok_rows] for k in range(experts)]
    for k in range(1, experts):
        parts[k] = hop(parts[k], "expert", k, f"home{k}")
        scored[k] = hop(scored[k][None], "expert", k, f"score{k}")[0]
    token_sum = parts[0].astype(jnp.float32)
    for k in range(1, experts):
        token_sum = token_sum + parts[k].astype(jnp.float32)
    token_grad = from_local(token_sum.astype(jnp.bfloat16), groups)
    prob_grad = sum(
        jnp.where(routes == (me ^ k), scored[k][:, None], 0.0) for k in range(experts)
    ).astype(jnp.bfloat16)
    weight_grad = jnp.concatenate(
        [s[:, i * step : (i + 1) * step] for i in range(3) for s in sums], 1
    )[None]
    return (token_grad, prob_grad, weight_grad)


def add_low(a, b):
    return (a.astype(jnp.float32) + b.astype(jnp.float32)).astype(jnp.bfloat16)


def kernel(
    gate, up_w, down_w, tok, grad, routes_in, probs_in, kept, token_out, prob_out, weight_out,
    w, term, swapped, inbox, du, wt, fac, low_act,
    x, m, xt, mt, q, pc, sb, st, sr, ha, hs, hr, wo, to, po, routes, probs,
    gs, gr, ps, pr, ds, dr, wr, rr, hsem, hrec, lw, ls, os,
):
    dp, e = lax.axis_index("dp"), lax.axis_index("expert")
    z, c = dp // 2, dp % 2
    ey, ex = e // 2, e % 2
    near = {1: 2 * ey + 1 - ex, 2: 2 * (1 - ey) + ex, 3: 2 * (1 - ey) + 1 - ex}
    units = len(w)
    count = units // 2
    rows = w[0].shape[1]
    sizes = [ref.shape[2] for ref in w[1::2]]
    offsets = [sum(sizes[:j]) for j in range(count)]
    hidden = sum(sizes)
    toks, width = tok.shape
    part = width // 2
    partner = z * 2 + 1 - c
    upper = z // 2
    middle = (z > 0) & (z < 3)
    edge = (z == 0) | (z == 3)

    def pos(k):
        return upper * k + (1 - upper) * (3 - k)

    side_in, side_out = upper, 1 - upper
    depth = jnp.where(edge, pos(2), pos(1))
    inn, out = (depth * 2 + c, e), (pos(3) * 2 + c, e)

    def copy(src, dst, s, r, dev):
        return pltpu.make_async_remote_copy(
            src_ref=src, dst_ref=dst, send_sem=s, recv_sem=r, device_id=dev, device_id_type=MESH
        )

    def send(src, dst, s, r, dev):
        copy(src, dst, s, r, dev).start()

    def arrive(size_of, s):
        copy(size_of, size_of, s, s, (partner, e)).wait_recv()

    def left(size_of, s):
        copy(size_of, size_of, s, s, (partner, e)).wait_send()

    barrier = pltpu.get_barrier_semaphore()

    def greet(dev):
        pl.semaphore_signal(barrier, inc=1, device_id=dev, device_id_type=MESH)

    for dev in [(partner, e), inn] + [(dp, near[k]) for k in (1, 2, 3)]:
        greet(dev)
    pl.when(middle)(lambda: greet(out))

    own = []
    for u in range(units):
        j = u // 2
        at = pl.ds(offsets[j], sizes[j])
        if u % 2 == 0:
            pairs = [(gate, pl.ds(0, sizes[j])), (up_w, pl.ds(sizes[j], sizes[j]))]
        else:
            pairs = [(down_w, pl.ds(0, sizes[j]))]
        own.append([
            pltpu.make_async_copy(ref.at[0, :, at], w[u].at[dp, :, to_at], lw.at[u])
            for ref, to_at in pairs
        ])

    def own_ready(u):
        pltpu.make_async_copy(w[u].at[dp], w[u].at[dp], lw.at[u]).wait()

    small = [
        pltpu.make_async_copy(routes_in, routes, ls.at[0]),
        pltpu.make_async_copy(probs_in, probs, ls.at[1]),
        pltpu.make_async_copy(tok, x.at[e], ls.at[2]),
        pltpu.make_async_copy(grad.at[:, pl.ds(0, part)], m.at[0, e], ls.at[3]),
        pltpu.make_async_copy(grad.at[:, pl.ds(part, part)], m.at[1, e], ls.at[4]),
    ]
    for d in own[0] + small[:2] + sum(own[1:], []) + small[2:]:
        d.start()
    pl.semaphore_wait(barrier, 5 + jnp.where(middle, 1, 0))

    half = toks // 2
    first, second, whole = pl.ds(0, half), pl.ds(half, half), pl.ds(0, toks)

    def spread_own(src, dst, p):
        for row, n, stage in ((first, 1, 0), (second, 2, 0), (second, 1, 1), (first, 2, 1)):
            send(src(row), dst(e, row), ds.at[p], dr.at[p, stage], (dp, near[n]))

    def spread_more(dst, p):
        arrive(dst(e, whole), dr.at[p, 0])
        for n, row, far in ((1, first, 2), (2, second, 1)):
            block = dst(near[n], row)
            send(block, block, ds.at[p], dr.at[p, 2], (dp, near[far]))

    def spread_rest(dst, p):
        arrive(dst(e, whole), dr.at[p, 1])

    def spread_done(dst, p):
        arrive(dst(e, whole), dr.at[p, 2])

    early, late = 1 - upper, upper

    def tok_src(row):
        return tok.at[row, :]

    def grad_src(side):
        return lambda row: grad.at[row, pl.ds(pl.multiple_of(side * part, part), part)]

    def x_dst(i, row):
        return x.at[i, row]

    def m_dst(side):
        return lambda i, row: m.at[side, i, row]

    def own_in(u):
        block = w[u].at[dp]
        send(block, block, gs.at[u], gr.at[u, jnp.where(edge, 0, 1)], inn)

    def own_out(u):
        block = w[u].at[dp]
        send(block, block, gs.at[u], gr.at[u, 0], out)

    def own_pair(u):
        block = w[u].at[dp]
        send(block, block, ps.at[u], pr.at[u], (partner, e))

    def gather_pass(u, at, stage, onward=None):
        block = w[u].at[at * 2 + c]
        arrive(block, gr.at[u, stage])
        if onward is not None:
            dev, later = onward
            send(block, block, gs.at[u], gr.at[u, later], dev)
        send(block, block, ps.at[u], pr.at[u], (partner, e))

    def pairs_done(u):
        arrive(w[u].at[pl.ds(0, 4)], pr.at[u])

    def block_of(k):
        return ((ey + k // 2) % 2) * 2 + (ex + k % 2) % 2

    def rows_of(i):
        return pl.ds(pl.multiple_of(i * toks, toks), toks)

    expert_rows = lax.broadcasted_iota(jnp.int32, (8, toks), 0)

    def turn_x(lo, hi):
        def body(k, _):
            i = block_of(k)
            xt[:, rows_of(i)] = x[i].T
            return 0

        lax.fori_loop(lo, hi, body, 0)

    def turn_m(side, lo, hi):
        def body(k, _):
            i = block_of(k)
            mt[pl.ds(pl.multiple_of(side * part, part), part), rows_of(i)] = m[side, i].T
            return 0

        lax.fori_loop(lo, hi, body, 0)

    def tall_probs():
        def body(i, _):
            row = jnp.sum(jnp.where(expert_rows == e, q[i], 0.0), axis=0, keepdims=True)
            pc[i] = jnp.broadcast_to(row, (128, toks)).T
            return 0

        lax.fori_loop(0, 4, body, 0)

    def forward_up(j, lo=0, hi=4):
        size, at = sizes[j], offsets[j]

        def body(k, _):
            i = block_of(k)
            here = rows_of(i)
            a = dot_f32(x[i], w[2 * j][:, :, :size].reshape(width, size))
            b = dot_f32(x[i], w[2 * j][:, :, size:].reshape(width, size))
            sig = jax.nn.sigmoid(a)
            act = (a * sig * b).astype(jnp.bfloat16)
            low_act[here, at : at + size] = act
            wt[j][here, :] = (act.astype(jnp.float32) * pc[i][:, :1]).astype(jnp.bfloat16)
            fac[here, 2 * at : 2 * at + size] = b * sig * (1.0 + a * (1.0 - sig))
            fac[here, 2 * at + size : 2 * (at + size)] = a * sig
            return 0

        lax.fori_loop(lo, hi, body, 0)

    def forward_down(j):
        size, at = sizes[j], offsets[j]

        def body(k, _):
            i = block_of(k)
            here = rows_of(i)
            cot = dot_f32(m[0, i], w[2 * j + 1][:4].reshape(part, size))
            cot = cot + dot_f32(m[1, i], w[2 * j + 1][4:].reshape(part, size))
            act = low_act[here, at : at + size].astype(jnp.float32)
            score = jnp.sum(act * cot, axis=1, keepdims=True)
            sb[i] = sb[i] + jnp.broadcast_to(score, (toks, 128))
            back = cot * pc[i][:, :1]
            du[j][here, :size] = (back * fac[here, 2 * at : 2 * at + size]).astype(jnp.bfloat16)
            du[j][here, size:] = (
                back * fac[here, 2 * at + size : 2 * (at + size)]
            ).astype(jnp.bfloat16)
            return 0

        lax.fori_loop(0, 4, body, 0)

    def ship(u, r):
        t = pos(r)
        send(term[u].at[t * 2 + c], inbox[u].at[side_in, t], gs.at[u], rr.at[u, r], inn)

    def gradient(u, lo, hi, outer):
        left, right = (xt, du[u // 2]) if u % 2 == 0 else (mt, wt[u // 2])

        def swap(t):
            return copy(
                term[u].at[t * 2 + 1 - c], swapped[u].at[t], ps.at[u], wr.at[u, t], (partner, e)
            )

        def block(d):
            here = pl.ds(pl.multiple_of(d * rows, rows), rows)
            term[u][d] = dot_f32(left[here, :], right[...]).astype(jnp.bfloat16)

        def give(r, _):
            block(pos(r) * 2 + 1 - c)
            swap(pos(r)).start()
            return 0

        def settle(r, _):
            t = pos(r)
            block(t * 2 + c)
            arrive(swapped[u].at[t], wr.at[u, t])
            term[u][t * 2 + c] = add_low(term[u][t * 2 + c], swapped[u][t])
            if outer and u not in HELD:
                pl.when(r < 3)(lambda: ship(u, r))
            return 0

        lax.fori_loop(lo, hi, give, 0)
        lax.fori_loop(lo, hi, settle, 0)

    def relay(u, side, t, stage, dev, later):
        arrive(term[u].at[dp], rr.at[u, stage])
        term[u][t * 2 + c] = add_low(term[u][t * 2 + c], inbox[u][side, t])
        send(term[u].at[t * 2 + c], inbox[u].at[side, t], gs.at[u], rr.at[u, later], dev)

    def spots(u):
        at = offsets[u // 2]
        return [at, hidden + at] if u % 2 == 0 else [2 * hidden + at]

    def pieces(u):
        cuts = [pl.ds(spot, sizes[u // 2]) for spot in spots(u)]
        return [
            pltpu.make_async_copy(wo.at[:, cut], weight_out.at[0, :, cut], os.at[0])
            for cut in cuts
        ]

    def final(u, outer):
        size = sizes[u // 2]
        if outer:
            arrive(term[u].at[dp], rr.at[u, 3])
        else:
            arrive(term[u].at[pl.ds(0, 2)], rr.at[u, 2])
        total = term[u][dp].astype(jnp.float32) + inbox[u][side_out, z].astype(jnp.float32)
        if not outer:
            total = total + inbox[u][side_in, z].astype(jnp.float32)
        total = total.astype(jnp.bfloat16)
        for k, spot in enumerate(spots(u)):
            wo[:, spot : spot + size] = total[:, k * size : (k + 1) * size]
        for d in pieces(u):
            d.start()

    def home(j):
        def body(k, _):
            i = block_of(3 - k)
            new = contract_last(du[j][rows_of(i), :], w[2 * j][...].reshape(width, 2 * sizes[j]))
            if j == 0:
                ha[i] = new
            elif j < count - 1:
                ha[i] = ha[i] + new
            else:
                hs[i] = (ha[i] + new).astype(jnp.bfloat16)
                st[i] = sb[i].T[:8, :]

                @pl.when(k < 3)
                def _():
                    send(hs.at[i], hr.at[e], hsem.at[0], hrec.at[0], (dp, i))
                    send(st.at[i], sr.at[e], hsem.at[1], hrec.at[1], (dp, i))

            return 0

        lax.fori_loop(0, 4, body, 0)
        if j == count - 1:
            sr[e] = st[e]

    outs = [
        pltpu.make_async_copy(to, token_out, os.at[1]),
        pltpu.make_async_copy(po, prob_out, os.at[2]),
    ]

    def home_done():
        arrive(hr.at[pl.ds(0, 3)], hrec.at[0])
        arrive(sr.at[pl.ds(0, 3)], hrec.at[1])
        total = hs[e].astype(jnp.float32)
        for k in (1, 2, 3):
            total = total + hr[near[k]].astype(jnp.float32)
        to[...] = total.astype(jnp.bfloat16)
        top = routes.shape[0]
        score = sum(jnp.where(routes[...] == i, sr[i][:top, :], 0.0) for i in range(4))
        lane = lax.broadcasted_iota(jnp.int32, (top, toks), 1)
        po[...] = jnp.where(e * toks + lane < kept[0], score, 0.0).astype(jnp.bfloat16)
        for d in outs:
            d.start()

    def send_probs():
        sb[...] = jnp.zeros_like(sb)
        for d in small[:2]:
            d.wait()
        lanes = lax.broadcasted_iota(jnp.int32, (8, toks), 1)
        rate = sum(
            jnp.where(
                routes[k : k + 1, :] == expert_rows, probs[k : k + 1, :].astype(jnp.float32), 0.0
            )
            for k in range(routes.shape[0])
        )
        q[e] = jnp.where(e * toks + lanes < kept[0], rate, 0.0)
        for k in (1, 2, 3):
            send(q.at[e], q.at[e], ds.at[3], dr.at[3, 0], (dp, near[k]))

    def get_probs():
        arrive(q.at[pl.ds(0, 3)], dr.at[3, 0])
        tall_probs()

    parts = (
        (tok_src, x_dst, 0),
        (grad_src(early), m_dst(early), 1),
        (grad_src(late), m_dst(late), 2),
    )

    def turn(p, lo, hi):
        if p == 0:
            turn_x(lo, hi)
        else:
            turn_m(early if p == 1 else late, lo, hi)

    def after(u):
        chain = [v for v in GATHER if v != FILLER] + [None]
        return None if u == FILLER else chain[chain.index(u) + 1]

    def more(p):
        spread_more(*parts[p][1:])
        if p + 1 < len(parts):
            spread_own(*parts[p + 1])

    def rest(p):
        spread_rest(*parts[p][1:])
        for d in (small[2:3], small[3:5], [])[p]:
            d.wait()
        turn(p, 0, 3)

    def last(p):
        spread_done(*parts[p][1:])
        turn(p, 3, 4)
        if p == 0:
            get_probs()

    def gather_far(u):
        gather_pass(u, pos(0), 2, (out, 2))
        if after(u) is not None:
            own_out(after(u))

    def gather_in(u):
        gather_pass(u, pos(3), 0, (inn, 2))
        if after(u) is not None:
            own_in(after(u))

    def up(j):
        pairs_done(2 * j)
        forward_up(j)

    def down(j):
        pairs_done(2 * j + 1)
        forward_down(j)

    def drain(outer):
        left(x.at[pl.ds(0, 3)], ds.at[0])
        for p in (1, 2):
            left(m.at[0, pl.ds(0, 3)], ds.at[p])
        left(q.at[pl.ds(0, 3)], ds.at[3])
        left(hs.at[pl.ds(0, 3)], hsem.at[0])
        left(st.at[pl.ds(0, 3)], hsem.at[1])
        for u in range(units):
            left(w[u].at[pl.ds(0, 4 if outer else 8)], gs.at[u])
            left(w[u], ps.at[u])

    def run(steps, outer):
        calls = {
            MORE: more,
            REST: rest,
            LAST: last,
            TAKE: lambda u, r: gather_pass(u, pos(2 - r), r),
            PASS_IN: gather_in,
            PASS_OUT: lambda u: gather_pass(u, pos(1), 1, (out, 1)),
            PASS_FAR: gather_far,
            UP: up,
            DOWN: down,
            GRAD: lambda u, lo, hi: gradient(u, lo, hi, outer),
            SUM_IN: lambda u, r: relay(u, side_in, pos(r), r, inn, 3 - r),
            SUM_OUT: lambda u: relay(u, side_out, pos(3), 3, out, 3),
            FINAL: lambda u: final(u, outer),
            HOME: home,
            HOME_DONE: home_done,
            SHIP: ship,
            DRAIN: lambda: drain(outer),
        }
        for name, *args in steps:
            calls[name](*args)

    spread_own(*parts[0])
    own_ready(0)
    own_in(0)
    pl.when(middle)(lambda: own_out(0))
    own_pair(0)
    for u in GATHER[1:]:
        own_ready(u)
        pl.when(edge)(lambda: own_in(u))
        if u == FILLER:
            pl.when(middle)(lambda: own_in(u))
            pl.when(middle)(lambda: own_out(u))
        own_pair(u)
    send_probs()
    pl.when(edge)(lambda: run(EDGE_STEPS, True))
    pl.when(middle)(lambda: run(MIDDLE_STEPS, False))

    pltpu.make_async_copy(wo, weight_out.at[0], os.at[0]).wait()
    for d in outs:
        d.wait()


def hand_over(*refs):
    came, go = refs[:3], refs[3:6]
    held, sem = refs[6:9], refs[9]
    into = [pltpu.make_async_copy(a, b, sem.at[k]) for k, (a, b) in enumerate(zip(came, held))]
    away = [pltpu.make_async_copy(a, b, sem.at[3 + k]) for k, (a, b) in enumerate(zip(held, go))]
    for d in into:
        d.start()
    for a, b in zip(into, away):
        a.wait()
        b.start()
    for d in away:
        d.wait()


def per_device_line(
    tokens, out_grad, routes, route_probs, kept_count, gate_weight, up_weight, down_weight
):
    toks, width = tokens.shape
    rows, hidden = gate_weight.shape[1:]
    sizes = [hidden * k // 6 for k in SHARES]
    cols = [n for size in sizes for n in (2 * size, size)]
    units = len(cols)
    low, full = jnp.bfloat16, jnp.float32
    dma, vmem = pltpu.SemaphoreType.DMA, pltpu.VMEM
    hbm = pl.BlockSpec(memory_space=pl.ANY)
    top = routes.shape[1]
    shapes = (
        jax.ShapeDtypeStruct((toks, width), low),
        jax.ShapeDtypeStruct((top, toks), low),
        jax.ShapeDtypeStruct((1, rows, 3 * hidden), low),
    )
    results = pl.pallas_call(
        kernel,
        out_shape=shapes,
        in_specs=[hbm] * 7 + [pl.BlockSpec(memory_space=pltpu.SMEM)],
        out_specs=(hbm,) * 3,
        scratch_shapes=[
            [vmem((8, rows, n), low) for n in cols],
            [vmem((8, rows, n), low) for n in cols],
            [vmem((4, rows, n), low) for n in cols],
            [vmem((2, 4, rows, n), low) for n in cols],
            [vmem((4 * toks, 2 * n), low) for n in sizes],
            [vmem((4 * toks, n), low) for n in sizes],
            vmem((4 * toks, 2 * hidden), full),
            vmem((4 * toks, hidden), low),
            vmem((4, toks, width), low),
            vmem((2, 4, toks, width // 2), low),
            vmem((width, 4 * toks), low),
            vmem((width, 4 * toks), low),
            vmem((4, 8, toks), full),
            vmem((4, toks, 128), full),
            vmem((4, toks, 128), full),
            vmem((4, 8, toks), full),
            vmem((4, 8, toks), full),
            vmem((4, toks, width), full),
            vmem((4, toks, width), low),
            vmem((4, toks, width), low),
            vmem((rows, 3 * hidden), low),
            vmem((toks, width), low),
            vmem((top, toks), low),
            vmem((top, toks), jnp.int32),
            vmem((top, toks), low),
            dma((units,)), dma((units, 3)), dma((units,)), dma((units,)),
            dma((4,)), dma((4, 3)), dma((units, 4)), dma((units, 4)),
            dma((2,)), dma((2,)), dma((units,)), dma((5,)), dma((3,)),
        ],
        compiler_params=pltpu.CompilerParams(
            collective_id=0, has_side_effects=True, vmem_limit_bytes=67043328
        ),
    )(
        gate_weight, up_weight, down_weight, tokens, out_grad, routes.T, route_probs.T, kept_count
    )
    token_grad, prob_grad, weight_grad = pl.pallas_call(
        hand_over,
        out_shape=shapes,
        in_specs=[hbm] * 3,
        out_specs=(hbm,) * 3,
        scratch_shapes=[vmem(s.shape, s.dtype) for s in shapes] + [dma((6,))],
    )(*results)
    return (token_grad, prob_grad.T, weight_grad)


def solution(mesh):
    in_specs = (
        P(("dp", "expert"), None),
        P(("dp", "expert"), None),
        P(("dp", "expert"), None),
        P(("dp", "expert"), None),
        P("dp"),
        P("expert", "dp", None),
        P("expert", "dp", None),
        P("expert", "dp", None),
    )
    out_specs = (P(("dp", "expert"), None), P(("dp", "expert"), None), P("expert", "dp", None))

    line = mesh.shape["dp"] == 4 * CORES and mesh.shape["expert"] == 4
    return jax.shard_map(
        per_device_line if line else per_device,
        mesh=mesh, in_specs=in_specs, out_specs=out_specs, check_vma=False,
    )
```

```python
import jax
import jax.numpy as jnp
from jax import lax
from jax.sharding import PartitionSpec as P
from jax.experimental import pallas as pl
from jax.experimental.pallas import tpu as pltpu

MESH = pl.DeviceIdType.MESH
CORES = 2
(
    SHIP, MORE, REST, LAST, TAKE, PASS_IN, PASS_OUT, PASS_FAR, UP,
    DOWN, GRAD, SUM_IN, SUM_OUT, FINAL, HOME, HOME_DONE, DRAIN,
) = range(17)
SHARES = (2, 1, 2, 1)
GATHER = (0, 2, 1, 3, 4, 5, 6, 7)
FILLER = 1
HELD = (6, 5, 7)
EDGE_STEPS = (
    (TAKE, 0, 0), (MORE, 0), (TAKE, 1, 0), (REST, 0), (TAKE, 0, 1), (TAKE, 1, 1), (LAST, 0),
    (MORE, 1), (TAKE, 0, 2), (UP, 0), (TAKE, 2, 0), (REST, 1), (LAST, 1), (GRAD, 1, 0, 2),
    (TAKE, 2, 1), (MORE, 2), (TAKE, 2, 2), (TAKE, 3, 0), (UP, 1), (TAKE, 3, 1), (REST, 2),
    (GRAD, 3, 0, 2), (LAST, 2), (GRAD, 3, 2, 4), (TAKE, 1, 2), (TAKE, 3, 2), (GRAD, 1, 2, 4),
    (DOWN, 0), (GRAD, 0, 0, 4), (TAKE, 4, 0), (DOWN, 1), (GRAD, 2, 0, 4), (TAKE, 4, 1), (HOME, 0),
    (HOME, 1), (TAKE, 4, 2), (UP, 2), (TAKE, 5, 0), (GRAD, 5, 0, 2), (GRAD, 5, 2, 4), (TAKE, 5, 1),
    (TAKE, 5, 2), (DOWN, 2), (TAKE, 6, 0), (GRAD, 4, 0, 4), (TAKE, 6, 1), (HOME, 2), (TAKE, 6, 2),
    (TAKE, 7, 0), (TAKE, 7, 1), (UP, 3), (TAKE, 7, 2), (GRAD, 7, 0, 4), (DOWN, 3), (HOME, 3),
    (FINAL, 0), (GRAD, 6, 0, 4), (SHIP, 6, 0), (SHIP, 5, 0), (SHIP, 7, 0), (SHIP, 6, 1),
    (SHIP, 5, 1), (SHIP, 7, 1), (SHIP, 6, 2), (SHIP, 5, 2), (SHIP, 7, 2), (FINAL, 3), (FINAL, 1),
    (FINAL, 2), (FINAL, 4), (FINAL, 6), (FINAL, 5), (FINAL, 7), (HOME_DONE,), (DRAIN,),
)
MIDDLE_STEPS = (
    (PASS_IN, 0), (PASS_OUT, 0), (MORE, 0), (PASS_IN, 2), (PASS_OUT, 1), (PASS_IN, 1), (PASS_IN, 3),
    (REST, 0), (PASS_FAR, 0), (PASS_OUT, 2), (PASS_IN, 4), (LAST, 0), (UP, 0), (PASS_FAR, 2),
    (PASS_OUT, 3), (PASS_IN, 5), (MORE, 1), (UP, 1), (PASS_FAR, 1), (PASS_IN, 6), (REST, 1),
    (PASS_FAR, 3), (PASS_IN, 7), (LAST, 1), (GRAD, 3, 0, 2), (GRAD, 1, 0, 2), (MORE, 2),
    (PASS_OUT, 4), (REST, 2), (LAST, 2), (DOWN, 0), (PASS_FAR, 4), (PASS_OUT, 5), (GRAD, 0, 0, 4),
    (PASS_FAR, 5), (DOWN, 1), (PASS_OUT, 6), (GRAD, 2, 0, 4), (PASS_FAR, 6), (HOME, 0),
    (PASS_OUT, 7), (PASS_FAR, 7), (SUM_IN, 0, 0), (GRAD, 3, 2, 4), (SUM_IN, 3, 0), (SUM_IN, 3, 1),
    (GRAD, 1, 2, 4), (SUM_IN, 1, 0), (SUM_IN, 1, 1), (HOME, 1), (SUM_IN, 0, 1), (UP, 2),
    (SUM_OUT, 0), (DOWN, 2), (SUM_OUT, 3), (GRAD, 4, 0, 4), (SUM_IN, 2, 0), (SUM_OUT, 1),
    (FINAL, 3), (HOME, 2), (SUM_IN, 2, 1), (FINAL, 1), (GRAD, 5, 0, 2), (GRAD, 5, 2, 4), (UP, 3),
    (FINAL, 0), (DOWN, 3), (SUM_OUT, 2), (SUM_IN, 4, 0), (HOME, 3), (FINAL, 2), (GRAD, 6, 0, 4),
    (GRAD, 7, 0, 4), (SUM_IN, 4, 1), (SUM_OUT, 4), (SUM_IN, 6, 0), (FINAL, 4), (SUM_IN, 5, 0),
    (SUM_IN, 7, 0), (SUM_OUT, 6), (SUM_IN, 6, 1), (SUM_OUT, 5), (SUM_OUT, 7), (SUM_IN, 5, 1),
    (SUM_IN, 7, 1), (FINAL, 6), (HOME_DONE,), (FINAL, 5), (FINAL, 7), (DRAIN,),
)


def dot_f32(left, right):
    return jnp.dot(left, right, preferred_element_type=jnp.float32)


def contract_rows(left, right):
    return lax.dot_general(
        left, right, (((0,), (0,)), ((), ())), preferred_element_type=jnp.float32
    )


def contract_last(left, right):
    return lax.dot_general(
        left, right, (((1,), (1,)), ((), ())), preferred_element_type=jnp.float32
    )


def hop(x, axis, mask, name):
    size = lax.axis_size(axis)
    with jax.named_scope(name):
        return lax.ppermute(x, axis, [(i, i ^ mask) for i in range(size)])


def z_send(x, moves, name):
    pairs = [(a * CORES + c, b * CORES + c) for a, b in moves for c in range(CORES)]
    with jax.named_scope(name):
        return lax.ppermute(x, "dp", pairs)


def xor_blocks(x, blocks):
    me = lax.axis_index("dp")
    rows, width = x.shape
    size = width // blocks
    depth = blocks // CORES
    parts = [x[:, i * size : (i + 1) * size] for i in range(blocks)]
    bit = 1
    while bit < blocks:
        flip = (me & bit) != 0
        parts = [jnp.where(flip, parts[i ^ bit], parts[i]) for i in range(blocks)]
        bit *= 2
    return parts, depth


def to_local(x, blocks):
    parts, depth = xor_blocks(x, blocks)
    return jnp.concatenate([parts[kz * CORES + kc] for kc in range(CORES) for kz in range(depth)], 1)


def from_local(x, blocks):
    depth = blocks // CORES
    size = x.shape[1] // blocks
    cut = [x[:, i * size : (i + 1) * size] for i in range(blocks)]
    natural = [cut[kc * depth + kz] for kz in range(depth) for kc in range(CORES)]
    parts, _ = xor_blocks(jnp.concatenate(natural, 1), blocks)
    return jnp.concatenate(parts, 1)


def spread(x, experts, name):
    if experts != 4:
        return jnp.concatenate([x] + [hop(x, "expert", k, f"{name}{k}") for k in range(1, experts)], 0)
    half = x.shape[0] // 2
    along_x = hop(x, "expert", 1, f"{name}_x")
    along_y = hop(x, "expert", 2, f"{name}_y")
    top = hop(along_x[:half], "expert", 2, f"{name}_xy")
    bottom = hop(along_y[half:], "expert", 1, f"{name}_yx")
    return jnp.concatenate([x, along_x, along_y, top, bottom], 0)


def reduce_line(q, depth, tag):
    def add(a, b):
        return (a.astype(jnp.float32) + b.astype(jnp.float32)).astype(jnp.bfloat16)

    if depth != 4:
        total = q[0].astype(jnp.float32)
        for kz in range(1, depth):
            total = total + hop(q[kz], "dp", kz * CORES, f"{tag}_{kz}").astype(jnp.float32)
        return total.astype(jnp.bfloat16)
    outer, middle, inner = [(3, 2), (0, 1)], [(2, 1), (1, 2)], [(1, 0), (2, 3)]
    a0 = z_send(q[3], outer, f"{tag}_a0")
    a1 = z_send(q[2], outer, f"{tag}_a1")
    a2 = z_send(q[1], outer, f"{tag}_a2")
    b0 = z_send(add(q[2], a0), middle, f"{tag}_b0")
    b1 = z_send(add(q[3], a1), middle, f"{tag}_b1")
    c0 = z_send(add(q[1], b0), inner, f"{tag}_c0")
    total = q[0].astype(jnp.float32) + a2.astype(jnp.float32)
    return (total + b1.astype(jnp.float32) + c0.astype(jnp.float32)).astype(jnp.bfloat16)


def gather_line(own, depth, tag):
    if depth != 4:
        return jnp.concatenate(
            [own] + [hop(own, "dp", kz * CORES, f"{tag}_{kz}") for kz in range(1, depth)], 0
        )
    z = lax.axis_index("dp") // CORES
    inside = (z == 1) | (z == 2)
    outer, middle, inner = [(3, 2), (0, 1)], [(2, 1), (1, 2)], [(1, 0), (2, 3)]
    o = z_send(own, outer, f"{tag}_o")
    m0 = z_send(own, middle, f"{tag}_m0")
    i0 = z_send(own, inner, f"{tag}_i0")
    m1 = z_send(o, middle, f"{tag}_m1")
    i1 = z_send(m0, inner, f"{tag}_i1")
    i2 = z_send(m1, inner, f"{tag}_i2")
    return jnp.concatenate(
        [own, jnp.where(inside, o, i0), jnp.where(inside, m1, i1), jnp.where(inside, m0, i2)], 0
    )


def chunks_of(hidden):
    return 3 if hidden % 384 == 0 else 1


def per_device(
    tokens, out_grad, routes, route_probs, kept_count, gate_weight, up_weight, down_weight
):
    tok_rows, width = tokens.shape
    experts = lax.axis_size("expert")
    groups = lax.axis_size("dp")
    depth = groups // CORES
    hidden = gate_weight.shape[2]
    count = chunks_of(hidden)
    step = hidden // count
    me = lax.axis_index("expert")

    row = me * tok_rows + jnp.arange(tok_rows, dtype=jnp.int32)
    kept = row < kept_count[0]
    masked = jnp.where(kept[:, None], out_grad, jnp.zeros_like(out_grad))
    probs = route_probs.astype(jnp.float32)

    def share(k):
        return jnp.sum(jnp.where(routes == (me ^ k), probs, 0.0), axis=1)

    prob_in = jnp.concatenate(
        [share(0)] + [hop(share(k)[None], "expert", k, f"prob{k}")[0] for k in range(1, experts)]
    )
    rows_in = spread(to_local(tokens, groups), experts, "rows")
    grad_in = spread(to_local(masked, groups), experts, "grad")

    half = width // CORES
    scores = 0.0
    back = [0.0, 0.0]
    sums = []
    for j in range(count):
        cut = slice(j * step, (j + 1) * step)
        own = jnp.concatenate(
            [gate_weight[0][:, cut], up_weight[0][:, cut], down_weight[0][:, cut]], 1
        )
        mine = gather_line(own, depth, f"g{j}")
        other = hop(mine, "dp", 1, f"pair{j}")
        both = (mine, other)
        pre = sum(dot_f32(rows_in[:, i * half : (i + 1) * half], both[i][:, : 2 * step]) for i in range(2))
        cot = sum(dot_f32(grad_in[:, i * half : (i + 1) * half], both[i][:, 2 * step :]) for i in range(2))
        a, b = pre[:, :step], pre[:, step:]
        sig = jax.nn.sigmoid(a)
        act = a * sig * b
        act_low = act.astype(jnp.bfloat16).astype(jnp.float32)
        scores = scores + jnp.sum(act_low * cot, axis=1)
        back_hidden = cot * prob_in[:, None]
        d_gate = (back_hidden * b * sig * (1.0 + a * (1.0 - sig))).astype(jnp.bfloat16)
        d_up = (back_hidden * a * sig).astype(jnp.bfloat16)
        d_both = jnp.concatenate([d_gate, d_up], 1)
        weighted = (act_low * prob_in[:, None]).astype(jnp.bfloat16)
        terms = [
            jnp.concatenate(
                [
                    contract_rows(rows_in[:, i * half : (i + 1) * half], d_both).astype(jnp.bfloat16),
                    contract_rows(grad_in[:, i * half : (i + 1) * half], weighted).astype(jnp.bfloat16),
                ],
                1,
            )
            for i in range(2)
        ]
        arrived = hop(terms[1], "dp", 1, f"swap{j}")
        block = half // depth
        q = tuple(
            (
                terms[0][kz * block : (kz + 1) * block].astype(jnp.float32)
                + arrived[kz * block : (kz + 1) * block].astype(jnp.float32)
            ).astype(jnp.bfloat16)
            for kz in range(depth)
        )
        sums.append(reduce_line(lax.optimization_barrier(q), depth, f"s{j}"))
        back = [back[i] + contract_last(d_both, both[i][:, : 2 * step]) for i in range(2)]

    route_back = jnp.concatenate(back, 1).astype(jnp.bfloat16)
    parts = [route_back[k * tok_rows : (k + 1) * tok_rows] for k in range(experts)]
    scored = [scores[k * tok_rows : (k + 1) * tok_rows] for k in range(experts)]
    for k in range(1, experts):
        parts[k] = hop(parts[k], "expert", k, f"home{k}")
        scored[k] = hop(scored[k][None], "expert", k, f"score{k}")[0]
    token_sum = parts[0].astype(jnp.float32)
    for k in range(1, experts):
        token_sum = token_sum + parts[k].astype(jnp.float32)
    token_grad = from_local(token_sum.astype(jnp.bfloat16), groups)
    prob_grad = sum(
        jnp.where(routes == (me ^ k), scored[k][:, None], 0.0) for k in range(experts)
    ).astype(jnp.bfloat16)
    weight_grad = jnp.concatenate(
        [s[:, i * step : (i + 1) * step] for i in range(3) for s in sums], 1
    )[None]
    return (token_grad, prob_grad, weight_grad)


def add_low(a, b):
    return (a.astype(jnp.float32) + b.astype(jnp.float32)).astype(jnp.bfloat16)


def kernel(
    gate, up_w, down_w, tok, grad, routes_in, probs_in, kept, token_out, prob_out, weight_out,
    w, term, swapped, inbox, du, wt, fac, low_act,
    x, m, xt, mt, q, pc, sb, st, sr, ha, hs, hr, routes, probs,
    gs, gr, ps, pr, ds, dr, wr, rr, hsem, hrec, lw, ls,
):
    dp, e = lax.axis_index("dp"), lax.axis_index("expert")
    z, c = dp // 2, dp % 2
    ey, ex = e // 2, e % 2
    near = {1: 2 * ey + 1 - ex, 2: 2 * (1 - ey) + ex, 3: 2 * (1 - ey) + 1 - ex}
    units = len(w)
    count = units // 2
    rows = w[0].shape[1]
    sizes = [ref.shape[2] for ref in w[1::2]]
    offsets = [sum(sizes[:j]) for j in range(count)]
    hidden = sum(sizes)
    toks, width = tok.shape
    part = width // 2
    partner = z * 2 + 1 - c
    upper = z // 2
    middle = (z > 0) & (z < 3)
    edge = (z == 0) | (z == 3)

    def pos(k):
        return upper * k + (1 - upper) * (3 - k)

    side_in, side_out = upper, 1 - upper
    depth = jnp.where(edge, pos(2), pos(1))
    inn, out = (depth * 2 + c, e), (pos(3) * 2 + c, e)

    def copy(src, dst, s, r, dev):
        return pltpu.make_async_remote_copy(
            src_ref=src, dst_ref=dst, send_sem=s, recv_sem=r, device_id=dev, device_id_type=MESH
        )

    def send(src, dst, s, r, dev):
        copy(src, dst, s, r, dev).start()

    def arrive(size_of, s):
        copy(size_of, size_of, s, s, (partner, e)).wait_recv()

    def left(size_of, s):
        copy(size_of, size_of, s, s, (partner, e)).wait_send()

    barrier = pltpu.get_barrier_semaphore()

    def greet(dev):
        pl.semaphore_signal(barrier, inc=1, device_id=dev, device_id_type=MESH)

    for dev in [(partner, e), inn] + [(dp, near[k]) for k in (1, 2, 3)]:
        greet(dev)
    pl.when(middle)(lambda: greet(out))

    own = []
    for u in range(units):
        j = u // 2
        at = pl.ds(offsets[j], sizes[j])
        if u % 2 == 0:
            pairs = [(gate, pl.ds(0, sizes[j])), (up_w, pl.ds(sizes[j], sizes[j]))]
        else:
            pairs = [(down_w, pl.ds(0, sizes[j]))]
        own.append([
            pltpu.make_async_copy(ref.at[0, :, at], w[u].at[dp, :, to_at], lw.at[u])
            for ref, to_at in pairs
        ])

    def own_ready(u):
        pltpu.make_async_copy(w[u].at[dp], w[u].at[dp], lw.at[u]).wait()

    small = [
        pltpu.make_async_copy(routes_in, routes, ls.at[0]),
        pltpu.make_async_copy(probs_in, probs, ls.at[1]),
        pltpu.make_async_copy(tok, x.at[e], ls.at[2]),
        pltpu.make_async_copy(grad.at[:, pl.ds(0, part)], m.at[0, e], ls.at[3]),
        pltpu.make_async_copy(grad.at[:, pl.ds(part, part)], m.at[1, e], ls.at[4]),
    ]
    for d in own[0] + small[:2] + sum(own[1:], []) + small[2:]:
        d.start()
    pl.semaphore_wait(barrier, 5 + jnp.where(middle, 1, 0))

    half = toks // 2
    first, second, whole = pl.ds(0, half), pl.ds(half, half), pl.ds(0, toks)

    def spread_own(src, dst, p):
        for row, n, stage in ((first, 1, 0), (second, 2, 0), (second, 1, 1), (first, 2, 1)):
            send(src(row), dst(e, row), ds.at[p], dr.at[p, stage], (dp, near[n]))

    def spread_more(dst, p):
        arrive(dst(e, whole), dr.at[p, 0])
        for n, row, far in ((1, first, 2), (2, second, 1)):
            block = dst(near[n], row)
            send(block, block, ds.at[p], dr.at[p, 2], (dp, near[far]))

    def spread_rest(dst, p):
        arrive(dst(e, whole), dr.at[p, 1])

    def spread_done(dst, p):
        arrive(dst(e, whole), dr.at[p, 2])

    early, late = 1 - upper, upper

    def tok_src(row):
        return tok.at[row, :]

    def grad_src(side):
        return lambda row: grad.at[row, pl.ds(pl.multiple_of(side * part, part), part)]

    def x_dst(i, row):
        return x.at[i, row]

    def m_dst(side):
        return lambda i, row: m.at[side, i, row]

    def own_in(u):
        block = w[u].at[dp]
        send(block, block, gs.at[u], gr.at[u, jnp.where(edge, 0, 1)], inn)

    def own_out(u):
        block = w[u].at[dp]
        send(block, block, gs.at[u], gr.at[u, 0], out)

    def own_pair(u):
        block = w[u].at[dp]
        send(block, block, ps.at[u], pr.at[u], (partner, e))

    def gather_pass(u, at, stage, onward=None):
        block = w[u].at[at * 2 + c]
        arrive(block, gr.at[u, stage])
        if onward is not None:
            dev, later = onward
            send(block, block, gs.at[u], gr.at[u, later], dev)
        send(block, block, ps.at[u], pr.at[u], (partner, e))

    def pairs_done(u):
        arrive(w[u].at[pl.ds(0, 4)], pr.at[u])

    def block_of(k):
        return ((ey + k // 2) % 2) * 2 + (ex + k % 2) % 2

    def rows_of(i):
        return pl.ds(pl.multiple_of(i * toks, toks), toks)

    expert_rows = lax.broadcasted_iota(jnp.int32, (8, toks), 0)

    def turn_x(lo, hi):
        def body(k, _):
            i = block_of(k)
            xt[:, rows_of(i)] = x[i].T
            return 0

        lax.fori_loop(lo, hi, body, 0)

    def turn_m(side, lo, hi):
        def body(k, _):
            i = block_of(k)
            mt[pl.ds(pl.multiple_of(side * part, part), part), rows_of(i)] = m[side, i].T
            return 0

        lax.fori_loop(lo, hi, body, 0)

    def tall_probs():
        def body(i, _):
            row = jnp.sum(jnp.where(expert_rows == e, q[i], 0.0), axis=0, keepdims=True)
            pc[i] = jnp.broadcast_to(row, (128, toks)).T
            return 0

        lax.fori_loop(0, 4, body, 0)

    def forward_up(j, lo=0, hi=4):
        size, at = sizes[j], offsets[j]

        def body(k, _):
            i = block_of(k)
            here = rows_of(i)
            a = dot_f32(x[i], w[2 * j][:, :, :size].reshape(width, size))
            b = dot_f32(x[i], w[2 * j][:, :, size:].reshape(width, size))
            sig = jax.nn.sigmoid(a)
            act = (a * sig * b).astype(jnp.bfloat16)
            low_act[here, at : at + size] = act
            wt[j][here, :] = (act.astype(jnp.float32) * pc[i][:, :1]).astype(jnp.bfloat16)
            fac[here, 2 * at : 2 * at + size] = b * sig * (1.0 + a * (1.0 - sig))
            fac[here, 2 * at + size : 2 * (at + size)] = a * sig
            return 0

        lax.fori_loop(lo, hi, body, 0)

    def forward_down(j):
        size, at = sizes[j], offsets[j]

        def body(k, _):
            i = block_of(k)
            here = rows_of(i)
            cot = dot_f32(m[0, i], w[2 * j + 1][:4].reshape(part, size))
            cot = cot + dot_f32(m[1, i], w[2 * j + 1][4:].reshape(part, size))
            act = low_act[here, at : at + size].astype(jnp.float32)
            score = jnp.sum(act * cot, axis=1, keepdims=True)
            sb[i] = sb[i] + jnp.broadcast_to(score, (toks, 128))
            back = cot * pc[i][:, :1]
            du[j][here, :size] = (back * fac[here, 2 * at : 2 * at + size]).astype(jnp.bfloat16)
            du[j][here, size:] = (
                back * fac[here, 2 * at + size : 2 * (at + size)]
            ).astype(jnp.bfloat16)
            return 0

        lax.fori_loop(0, 4, body, 0)

    def ship(u, r):
        t = pos(r)
        send(term[u].at[t * 2 + c], inbox[u].at[side_in, t], gs.at[u], rr.at[u, r], inn)

    def gradient(u, lo, hi, outer):
        left, right = (xt, du[u // 2]) if u % 2 == 0 else (mt, wt[u // 2])

        def swap(t):
            return copy(
                term[u].at[t * 2 + 1 - c], swapped[u].at[t], ps.at[u], wr.at[u, t], (partner, e)
            )

        def block(d):
            here = pl.ds(pl.multiple_of(d * rows, rows), rows)
            term[u][d] = dot_f32(left[here, :], right[...]).astype(jnp.bfloat16)

        def give(r, _):
            block(pos(r) * 2 + 1 - c)
            swap(pos(r)).start()
            return 0

        def settle(r, _):
            t = pos(r)
            block(t * 2 + c)
            arrive(swapped[u].at[t], wr.at[u, t])
            term[u][t * 2 + c] = add_low(term[u][t * 2 + c], swapped[u][t])
            if outer and u not in HELD:
                pl.when(r < 3)(lambda: ship(u, r))
            return 0

        lax.fori_loop(lo, hi, give, 0)
        lax.fori_loop(lo, hi, settle, 0)

    def relay(u, side, t, stage, dev, later):
        arrive(term[u].at[dp], rr.at[u, stage])
        term[u][t * 2 + c] = add_low(term[u][t * 2 + c], inbox[u][side, t])
        send(term[u].at[t * 2 + c], inbox[u].at[side, t], gs.at[u], rr.at[u, later], dev)

    def spots(u):
        at = offsets[u // 2]
        return [at, hidden + at] if u % 2 == 0 else [2 * hidden + at]

    def final(u, outer):
        size = sizes[u // 2]
        if outer:
            arrive(term[u].at[dp], rr.at[u, 3])
        else:
            arrive(term[u].at[pl.ds(0, 2)], rr.at[u, 2])
        total = term[u][dp].astype(jnp.float32) + inbox[u][side_out, z].astype(jnp.float32)
        if not outer:
            total = total + inbox[u][side_in, z].astype(jnp.float32)
        total = total.astype(jnp.bfloat16)
        for k, spot in enumerate(spots(u)):
            weight_out[0, :, spot : spot + size] = total[:, k * size : (k + 1) * size]
    def home(j):
        def body(k, _):
            i = block_of(3 - k)
            new = contract_last(du[j][rows_of(i), :], w[2 * j][...].reshape(width, 2 * sizes[j]))
            if j == 0:
                ha[i] = new
            elif j < count - 1:
                ha[i] = ha[i] + new
            else:
                hs[i] = (ha[i] + new).astype(jnp.bfloat16)
                st[i] = sb[i].T[:8, :]

                @pl.when(k < 3)
                def _():
                    send(hs.at[i], hr.at[e], hsem.at[0], hrec.at[0], (dp, i))
                    send(st.at[i], sr.at[e], hsem.at[1], hrec.at[1], (dp, i))

            return 0

        lax.fori_loop(0, 4, body, 0)
        if j == count - 1:
            sr[e] = st[e]

    def home_done():
        arrive(hr.at[pl.ds(0, 3)], hrec.at[0])
        arrive(sr.at[pl.ds(0, 3)], hrec.at[1])
        total = hs[e].astype(jnp.float32)
        for k in (1, 2, 3):
            total = total + hr[near[k]].astype(jnp.float32)
        token_out[...] = total.astype(jnp.bfloat16)
        top = routes.shape[0]
        score = sum(jnp.where(routes[...] == i, sr[i][:top, :], 0.0) for i in range(4))
        lane = lax.broadcasted_iota(jnp.int32, (top, toks), 1)
        prob_out[...] = jnp.where(e * toks + lane < kept[0], score, 0.0).astype(jnp.bfloat16)

    def send_probs():
        sb[...] = jnp.zeros_like(sb)
        for d in small[:2]:
            d.wait()
        lanes = lax.broadcasted_iota(jnp.int32, (8, toks), 1)
        rate = sum(
            jnp.where(
                routes[k : k + 1, :] == expert_rows, probs[k : k + 1, :].astype(jnp.float32), 0.0
            )
            for k in range(routes.shape[0])
        )
        q[e] = jnp.where(e * toks + lanes < kept[0], rate, 0.0)
        for k in (1, 2, 3):
            send(q.at[e], q.at[e], ds.at[3], dr.at[3, 0], (dp, near[k]))

    def get_probs():
        arrive(q.at[pl.ds(0, 3)], dr.at[3, 0])
        tall_probs()

    parts = (
        (tok_src, x_dst, 0),
        (grad_src(early), m_dst(early), 1),
        (grad_src(late), m_dst(late), 2),
    )

    def turn(p, lo, hi):
        if p == 0:
            turn_x(lo, hi)
        else:
            turn_m(early if p == 1 else late, lo, hi)

    def after(u):
        chain = [v for v in GATHER if v != FILLER] + [None]
        return None if u == FILLER else chain[chain.index(u) + 1]

    def more(p):
        spread_more(*parts[p][1:])
        if p + 1 < len(parts):
            spread_own(*parts[p + 1])

    def rest(p):
        spread_rest(*parts[p][1:])
        for d in (small[2:3], small[3:5], [])[p]:
            d.wait()
        turn(p, 0, 3)

    def last(p):
        spread_done(*parts[p][1:])
        turn(p, 3, 4)
        if p == 0:
            get_probs()

    def gather_far(u):
        gather_pass(u, pos(0), 2, (out, 2))
        if after(u) is not None:
            own_out(after(u))

    def gather_in(u):
        gather_pass(u, pos(3), 0, (inn, 2))
        if after(u) is not None:
            own_in(after(u))

    def up(j):
        pairs_done(2 * j)
        forward_up(j)

    def down(j):
        pairs_done(2 * j + 1)
        forward_down(j)

    def drain(outer):
        left(x.at[pl.ds(0, 3)], ds.at[0])
        for p in (1, 2):
            left(m.at[0, pl.ds(0, 3)], ds.at[p])
        left(q.at[pl.ds(0, 3)], ds.at[3])
        left(hs.at[pl.ds(0, 3)], hsem.at[0])
        left(st.at[pl.ds(0, 3)], hsem.at[1])
        for u in range(units):
            left(w[u].at[pl.ds(0, 4 if outer else 8)], gs.at[u])
            left(w[u], ps.at[u])

    def run(steps, outer):
        calls = {
            MORE: more,
            REST: rest,
            LAST: last,
            TAKE: lambda u, r: gather_pass(u, pos(2 - r), r),
            PASS_IN: gather_in,
            PASS_OUT: lambda u: gather_pass(u, pos(1), 1, (out, 1)),
            PASS_FAR: gather_far,
            UP: up,
            DOWN: down,
            GRAD: lambda u, lo, hi: gradient(u, lo, hi, outer),
            SUM_IN: lambda u, r: relay(u, side_in, pos(r), r, inn, 3 - r),
            SUM_OUT: lambda u: relay(u, side_out, pos(3), 3, out, 3),
            FINAL: lambda u: final(u, outer),
            HOME: home,
            HOME_DONE: home_done,
            SHIP: ship,
            DRAIN: lambda: drain(outer),
        }
        for name, *args in steps:
            calls[name](*args)

    spread_own(*parts[0])
    own_ready(0)
    own_in(0)
    pl.when(middle)(lambda: own_out(0))
    own_pair(0)
    for u in GATHER[1:]:
        own_ready(u)
        pl.when(edge)(lambda: own_in(u))
        if u == FILLER:
            pl.when(middle)(lambda: own_in(u))
            pl.when(middle)(lambda: own_out(u))
        own_pair(u)
    send_probs()
    pl.when(edge)(lambda: run(EDGE_STEPS, True))
    pl.when(middle)(lambda: run(MIDDLE_STEPS, False))


def hand_over(*refs):
    came, go, sem = refs[:3], refs[3:6], refs[6]
    away = [pltpu.make_async_copy(a, b, sem.at[k]) for k, (a, b) in enumerate(zip(came, go))]
    for d in away:
        d.start()
    for d in away:
        d.wait()


def per_device_line(
    tokens, out_grad, routes, route_probs, kept_count, gate_weight, up_weight, down_weight
):
    toks, width = tokens.shape
    rows, hidden = gate_weight.shape[1:]
    sizes = [hidden * k // 6 for k in SHARES]
    cols = [n for size in sizes for n in (2 * size, size)]
    units = len(cols)
    low, full = jnp.bfloat16, jnp.float32
    dma, vmem = pltpu.SemaphoreType.DMA, pltpu.VMEM
    hbm, chip = pl.BlockSpec(memory_space=pl.ANY), pl.BlockSpec(memory_space=vmem)
    top = routes.shape[1]
    shapes = (
        jax.ShapeDtypeStruct((toks, width), low),
        jax.ShapeDtypeStruct((top, toks), low),
        jax.ShapeDtypeStruct((1, rows, 3 * hidden), low),
    )
    results = pl.pallas_call(
        kernel,
        out_shape=tuple(vmem(s.shape, s.dtype) for s in shapes),
        in_specs=[hbm] * 7 + [pl.BlockSpec(memory_space=pltpu.SMEM)],
        out_specs=(chip,) * 3,
        scratch_shapes=[
            [vmem((8, rows, n), low) for n in cols],
            [vmem((8, rows, n), low) for n in cols],
            [vmem((4, rows, n), low) for n in cols],
            [vmem((2, 4, rows, n), low) for n in cols],
            [vmem((4 * toks, 2 * n), low) for n in sizes],
            [vmem((4 * toks, n), low) for n in sizes],
            vmem((4 * toks, 2 * hidden), full),
            vmem((4 * toks, hidden), low),
            vmem((4, toks, width), low),
            vmem((2, 4, toks, width // 2), low),
            vmem((width, 4 * toks), low),
            vmem((width, 4 * toks), low),
            vmem((4, 8, toks), full),
            vmem((4, toks, 128), full),
            vmem((4, toks, 128), full),
            vmem((4, 8, toks), full),
            vmem((4, 8, toks), full),
            vmem((4, toks, width), full),
            vmem((4, toks, width), low),
            vmem((4, toks, width), low),
            vmem((top, toks), jnp.int32),
            vmem((top, toks), low),
            dma((units,)), dma((units, 3)), dma((units,)), dma((units,)),
            dma((4,)), dma((4, 3)), dma((units, 4)), dma((units, 4)),
            dma((2,)), dma((2,)), dma((units,)), dma((5,)),
        ],
        compiler_params=pltpu.CompilerParams(
            collective_id=0, has_side_effects=True, vmem_limit_bytes=61 * 2**20
        ),
    )(
        gate_weight, up_weight, down_weight, tokens, out_grad, routes.T, route_probs.T, kept_count
    )
    token_grad, prob_grad, weight_grad = pl.pallas_call(
        hand_over,
        out_shape=shapes,
        in_specs=[chip] * 3,
        out_specs=(hbm,) * 3,
        scratch_shapes=[dma((3,))],
    )(*[pltpu.with_memory_space_constraint(r, vmem) for r in results])
    return (token_grad, prob_grad.T, weight_grad)


def solution(mesh):
    in_specs = (
        P(("dp", "expert"), None),
        P(("dp", "expert"), None),
        P(("dp", "expert"), None),
        P(("dp", "expert"), None),
        P("dp"),
        P("expert", "dp", None),
        P("expert", "dp", None),
        P("expert", "dp", None),
    )
    out_specs = (P(("dp", "expert"), None), P(("dp", "expert"), None), P("expert", "dp", None))

    line = mesh.shape["dp"] == 4 * CORES and mesh.shape["expert"] == 4
    return jax.shard_map(
        per_device_line if line else per_device,
        mesh=mesh, in_specs=in_specs, out_specs=out_specs, check_vma=False,
    )
```

```python
import jax
import jax.numpy as jnp
from jax import lax
from jax.sharding import PartitionSpec as P
from jax.experimental import pallas as pl
from jax.experimental.pallas import tpu as pltpu

MESH = pl.DeviceIdType.MESH
CORES = 2
(
    SHIP, MORE, REST, LAST, TAKE, PASS_IN, PASS_OUT, PASS_FAR, UP,
    DOWN, GRAD, SUM_IN, SUM_OUT, FINAL, HOME, HOME_DONE, DRAIN,
) = range(17)
SHARES = (2, 1, 2, 1)
GATHER = (0, 2, 1, 3, 4, 5, 6, 7)
FILLER = 1
HELD = (5, 6, 7)
EDGE_STEPS = (
    (TAKE, 0, 0), (MORE, 0), (TAKE, 1, 0), (REST, 0), (TAKE, 0, 1), (TAKE, 1, 1), (LAST, 0),
    (MORE, 1), (TAKE, 0, 2), (UP, 0), (TAKE, 2, 0), (REST, 1), (LAST, 1), (GRAD, 1, 0, 2),
    (TAKE, 2, 1), (MORE, 2), (TAKE, 2, 2), (TAKE, 3, 0), (UP, 1), (TAKE, 3, 1), (REST, 2),
    (GRAD, 3, 0, 2), (LAST, 2), (GRAD, 1, 2, 4), (TAKE, 1, 2), (TAKE, 3, 2), (GRAD, 3, 2, 4),
    (DOWN, 0), (GRAD, 0, 0, 4), (TAKE, 4, 0), (DOWN, 1), (GRAD, 2, 0, 4), (TAKE, 4, 1), (HOME, 0),
    (HOME, 1), (TAKE, 4, 2), (UP, 2), (TAKE, 5, 0), (GRAD, 5, 0, 2), (GRAD, 5, 2, 4), (TAKE, 5, 1),
    (TAKE, 5, 2), (DOWN, 2), (TAKE, 6, 0), (GRAD, 4, 0, 4), (TAKE, 6, 1), (HOME, 2), (TAKE, 6, 2),
    (TAKE, 7, 0), (TAKE, 7, 1), (UP, 3), (TAKE, 7, 2), (GRAD, 7, 0, 4), (DOWN, 3), (FINAL, 1),
    (HOME, 3), (FINAL, 3), (GRAD, 6, 0, 4), (SHIP, 5, 0), (SHIP, 6, 0), (SHIP, 7, 0), (SHIP, 5, 1),
    (SHIP, 6, 1), (SHIP, 7, 1), (SHIP, 5, 2), (SHIP, 6, 2), (SHIP, 7, 2), (FINAL, 0), (FINAL, 2),
    (FINAL, 4), (FINAL, 5), (FINAL, 6), (FINAL, 7), (HOME_DONE,), (DRAIN,),
)
MIDDLE_STEPS = (
    (PASS_IN, 0), (PASS_OUT, 0), (MORE, 0), (PASS_IN, 2), (PASS_OUT, 1), (PASS_IN, 1), (PASS_IN, 3),
    (REST, 0), (PASS_FAR, 0), (PASS_OUT, 2), (PASS_IN, 4), (LAST, 0), (UP, 0), (PASS_FAR, 2),
    (PASS_OUT, 3), (PASS_IN, 5), (MORE, 1), (UP, 1), (PASS_FAR, 1), (PASS_IN, 6), (REST, 1),
    (PASS_FAR, 3), (PASS_IN, 7), (LAST, 1), (GRAD, 1, 0, 2), (GRAD, 3, 0, 2), (MORE, 2),
    (PASS_OUT, 4), (REST, 2), (LAST, 2), (GRAD, 1, 2, 4), (PASS_FAR, 4), (SUM_IN, 1, 0),
    (SUM_IN, 1, 1), (GRAD, 3, 2, 4), (PASS_OUT, 5), (SUM_IN, 3, 0), (SUM_IN, 3, 1), (DOWN, 0),
    (PASS_FAR, 5), (GRAD, 0, 0, 4), (PASS_OUT, 6), (DOWN, 1), (PASS_FAR, 6), (GRAD, 2, 0, 4),
    (PASS_OUT, 7), (PASS_FAR, 7), (SUM_IN, 0, 0), (HOME, 0), (SUM_OUT, 1), (UP, 2), (SUM_IN, 0, 1),
    (FINAL, 1), (DOWN, 2), (SUM_OUT, 3), (GRAD, 4, 0, 4), (FINAL, 3), (GRAD, 5, 0, 2),
    (GRAD, 5, 2, 4), (SUM_OUT, 0), (SUM_IN, 2, 0), (HOME, 1), (SUM_IN, 2, 1), (HOME, 2), (FINAL, 0),
    (UP, 3), (SUM_OUT, 2), (DOWN, 3), (HOME, 3), (SUM_IN, 4, 0), (FINAL, 2), (GRAD, 6, 0, 4),
    (GRAD, 7, 0, 4), (SUM_IN, 4, 1), (SUM_OUT, 4), (SUM_IN, 5, 0), (FINAL, 4), (SUM_IN, 6, 0),
    (SUM_IN, 7, 0), (SUM_OUT, 5), (SUM_IN, 5, 1), (SUM_OUT, 6), (SUM_OUT, 7), (SUM_IN, 6, 1),
    (SUM_IN, 7, 1), (HOME_DONE,), (FINAL, 5), (FINAL, 6), (FINAL, 7), (DRAIN,),
)


def dot_f32(left, right):
    return jnp.dot(left, right, preferred_element_type=jnp.float32)


def contract_rows(left, right):
    return lax.dot_general(
        left, right, (((0,), (0,)), ((), ())), preferred_element_type=jnp.float32
    )


def contract_last(left, right):
    return lax.dot_general(
        left, right, (((1,), (1,)), ((), ())), preferred_element_type=jnp.float32
    )


def hop(x, axis, mask, name):
    size = lax.axis_size(axis)
    with jax.named_scope(name):
        return lax.ppermute(x, axis, [(i, i ^ mask) for i in range(size)])


def z_send(x, moves, name):
    pairs = [(a * CORES + c, b * CORES + c) for a, b in moves for c in range(CORES)]
    with jax.named_scope(name):
        return lax.ppermute(x, "dp", pairs)


def xor_blocks(x, blocks):
    me = lax.axis_index("dp")
    rows, width = x.shape
    size = width // blocks
    depth = blocks // CORES
    parts = [x[:, i * size : (i + 1) * size] for i in range(blocks)]
    bit = 1
    while bit < blocks:
        flip = (me & bit) != 0
        parts = [jnp.where(flip, parts[i ^ bit], parts[i]) for i in range(blocks)]
        bit *= 2
    return parts, depth


def to_local(x, blocks):
    parts, depth = xor_blocks(x, blocks)
    return jnp.concatenate([parts[kz * CORES + kc] for kc in range(CORES) for kz in range(depth)], 1)


def from_local(x, blocks):
    depth = blocks // CORES
    size = x.shape[1] // blocks
    cut = [x[:, i * size : (i + 1) * size] for i in range(blocks)]
    natural = [cut[kc * depth + kz] for kz in range(depth) for kc in range(CORES)]
    parts, _ = xor_blocks(jnp.concatenate(natural, 1), blocks)
    return jnp.concatenate(parts, 1)


def spread(x, experts, name):
    if experts != 4:
        return jnp.concatenate([x] + [hop(x, "expert", k, f"{name}{k}") for k in range(1, experts)], 0)
    half = x.shape[0] // 2
    along_x = hop(x, "expert", 1, f"{name}_x")
    along_y = hop(x, "expert", 2, f"{name}_y")
    top = hop(along_x[:half], "expert", 2, f"{name}_xy")
    bottom = hop(along_y[half:], "expert", 1, f"{name}_yx")
    return jnp.concatenate([x, along_x, along_y, top, bottom], 0)


def reduce_line(q, depth, tag):
    def add(a, b):
        return (a.astype(jnp.float32) + b.astype(jnp.float32)).astype(jnp.bfloat16)

    if depth != 4:
        total = q[0].astype(jnp.float32)
        for kz in range(1, depth):
            total = total + hop(q[kz], "dp", kz * CORES, f"{tag}_{kz}").astype(jnp.float32)
        return total.astype(jnp.bfloat16)
    outer, middle, inner = [(3, 2), (0, 1)], [(2, 1), (1, 2)], [(1, 0), (2, 3)]
    a0 = z_send(q[3], outer, f"{tag}_a0")
    a1 = z_send(q[2], outer, f"{tag}_a1")
    a2 = z_send(q[1], outer, f"{tag}_a2")
    b0 = z_send(add(q[2], a0), middle, f"{tag}_b0")
    b1 = z_send(add(q[3], a1), middle, f"{tag}_b1")
    c0 = z_send(add(q[1], b0), inner, f"{tag}_c0")
    total = q[0].astype(jnp.float32) + a2.astype(jnp.float32)
    return (total + b1.astype(jnp.float32) + c0.astype(jnp.float32)).astype(jnp.bfloat16)


def gather_line(own, depth, tag):
    if depth != 4:
        return jnp.concatenate(
            [own] + [hop(own, "dp", kz * CORES, f"{tag}_{kz}") for kz in range(1, depth)], 0
        )
    z = lax.axis_index("dp") // CORES
    inside = (z == 1) | (z == 2)
    outer, middle, inner = [(3, 2), (0, 1)], [(2, 1), (1, 2)], [(1, 0), (2, 3)]
    o = z_send(own, outer, f"{tag}_o")
    m0 = z_send(own, middle, f"{tag}_m0")
    i0 = z_send(own, inner, f"{tag}_i0")
    m1 = z_send(o, middle, f"{tag}_m1")
    i1 = z_send(m0, inner, f"{tag}_i1")
    i2 = z_send(m1, inner, f"{tag}_i2")
    return jnp.concatenate(
        [own, jnp.where(inside, o, i0), jnp.where(inside, m1, i1), jnp.where(inside, m0, i2)], 0
    )


def chunks_of(hidden):
    return 3 if hidden % 384 == 0 else 1


def per_device(
    tokens, out_grad, routes, route_probs, kept_count, gate_weight, up_weight, down_weight
):
    tok_rows, width = tokens.shape
    experts = lax.axis_size("expert")
    groups = lax.axis_size("dp")
    depth = groups // CORES
    hidden = gate_weight.shape[2]
    count = chunks_of(hidden)
    step = hidden // count
    me = lax.axis_index("expert")

    row = me * tok_rows + jnp.arange(tok_rows, dtype=jnp.int32)
    kept = row < kept_count[0]
    masked = jnp.where(kept[:, None], out_grad, jnp.zeros_like(out_grad))
    probs = route_probs.astype(jnp.float32)

    def share(k):
        return jnp.sum(jnp.where(routes == (me ^ k), probs, 0.0), axis=1)

    prob_in = jnp.concatenate(
        [share(0)] + [hop(share(k)[None], "expert", k, f"prob{k}")[0] for k in range(1, experts)]
    )
    rows_in = spread(to_local(tokens, groups), experts, "rows")
    grad_in = spread(to_local(masked, groups), experts, "grad")

    half = width // CORES
    scores = 0.0
    back = [0.0, 0.0]
    sums = []
    for j in range(count):
        cut = slice(j * step, (j + 1) * step)
        own = jnp.concatenate(
            [gate_weight[0][:, cut], up_weight[0][:, cut], down_weight[0][:, cut]], 1
        )
        mine = gather_line(own, depth, f"g{j}")
        other = hop(mine, "dp", 1, f"pair{j}")
        both = (mine, other)
        pre = sum(dot_f32(rows_in[:, i * half : (i + 1) * half], both[i][:, : 2 * step]) for i in range(2))
        cot = sum(dot_f32(grad_in[:, i * half : (i + 1) * half], both[i][:, 2 * step :]) for i in range(2))
        a, b = pre[:, :step], pre[:, step:]
        sig = jax.nn.sigmoid(a)
        act = a * sig * b
        act_low = act.astype(jnp.bfloat16).astype(jnp.float32)
        scores = scores + jnp.sum(act_low * cot, axis=1)
        back_hidden = cot * prob_in[:, None]
        d_gate = (back_hidden * b * sig * (1.0 + a * (1.0 - sig))).astype(jnp.bfloat16)
        d_up = (back_hidden * a * sig).astype(jnp.bfloat16)
        d_both = jnp.concatenate([d_gate, d_up], 1)
        weighted = (act_low * prob_in[:, None]).astype(jnp.bfloat16)
        terms = [
            jnp.concatenate(
                [
                    contract_rows(rows_in[:, i * half : (i + 1) * half], d_both).astype(jnp.bfloat16),
                    contract_rows(grad_in[:, i * half : (i + 1) * half], weighted).astype(jnp.bfloat16),
                ],
                1,
            )
            for i in range(2)
        ]
        arrived = hop(terms[1], "dp", 1, f"swap{j}")
        block = half // depth
        q = tuple(
            (
                terms[0][kz * block : (kz + 1) * block].astype(jnp.float32)
                + arrived[kz * block : (kz + 1) * block].astype(jnp.float32)
            ).astype(jnp.bfloat16)
            for kz in range(depth)
        )
        sums.append(reduce_line(lax.optimization_barrier(q), depth, f"s{j}"))
        back = [back[i] + contract_last(d_both, both[i][:, : 2 * step]) for i in range(2)]

    route_back = jnp.concatenate(back, 1).astype(jnp.bfloat16)
    parts = [route_back[k * tok_rows : (k + 1) * tok_rows] for k in range(experts)]
    scored = [scores[k * tok_rows : (k + 1) * tok_rows] for k in range(experts)]
    for k in range(1, experts):
        parts[k] = hop(parts[k], "expert", k, f"home{k}")
        scored[k] = hop(scored[k][None], "expert", k, f"score{k}")[0]
    token_sum = parts[0].astype(jnp.float32)
    for k in range(1, experts):
        token_sum = token_sum + parts[k].astype(jnp.float32)
    token_grad = from_local(token_sum.astype(jnp.bfloat16), groups)
    prob_grad = sum(
        jnp.where(routes == (me ^ k), scored[k][:, None], 0.0) for k in range(experts)
    ).astype(jnp.bfloat16)
    weight_grad = jnp.concatenate(
        [s[:, i * step : (i + 1) * step] for i in range(3) for s in sums], 1
    )[None]
    return (token_grad, prob_grad, weight_grad)


def add_low(a, b):
    return (a.astype(jnp.float32) + b.astype(jnp.float32)).astype(jnp.bfloat16)


def kernel(
    gate, up_w, down_w, tok, grad, routes_in, probs_in, kept, token_out, prob_out, weight_out,
    w, term, swapped, inbox, du, wt, fac, low_act,
    x, m, xt, mt, q, pc, sb, st, sr, ha, hs, hr, routes, probs,
    gs, gr, ps, pr, ds, dr, wr, rr, hsem, hrec, lw, ls,
):
    dp, e = lax.axis_index("dp"), lax.axis_index("expert")
    z, c = dp // 2, dp % 2
    ey, ex = e // 2, e % 2
    near = {1: 2 * ey + 1 - ex, 2: 2 * (1 - ey) + ex, 3: 2 * (1 - ey) + 1 - ex}
    units = len(w)
    count = units // 2
    rows = w[0].shape[1]
    sizes = [ref.shape[2] for ref in w[1::2]]
    offsets = [sum(sizes[:j]) for j in range(count)]
    hidden = sum(sizes)
    toks, width = tok.shape
    part = width // 2
    partner = z * 2 + 1 - c
    upper = z // 2
    middle = (z > 0) & (z < 3)
    edge = (z == 0) | (z == 3)

    def pos(k):
        return upper * k + (1 - upper) * (3 - k)

    side_in, side_out = upper, 1 - upper
    depth = jnp.where(edge, pos(2), pos(1))
    inn, out = (depth * 2 + c, e), (pos(3) * 2 + c, e)

    def copy(src, dst, s, r, dev):
        return pltpu.make_async_remote_copy(
            src_ref=src, dst_ref=dst, send_sem=s, recv_sem=r, device_id=dev, device_id_type=MESH
        )

    def send(src, dst, s, r, dev):
        copy(src, dst, s, r, dev).start()

    def arrive(size_of, s):
        copy(size_of, size_of, s, s, (partner, e)).wait_recv()

    def left(size_of, s):
        copy(size_of, size_of, s, s, (partner, e)).wait_send()

    barrier = pltpu.get_barrier_semaphore()

    def greet(dev):
        pl.semaphore_signal(barrier, inc=1, device_id=dev, device_id_type=MESH)

    for dev in [(partner, e), inn] + [(dp, near[k]) for k in (1, 2, 3)]:
        greet(dev)
    pl.when(middle)(lambda: greet(out))

    own = []
    for u in range(units):
        j = u // 2
        at = pl.ds(offsets[j], sizes[j])
        if u % 2 == 0:
            pairs = [(gate, pl.ds(0, sizes[j])), (up_w, pl.ds(sizes[j], sizes[j]))]
        else:
            pairs = [(down_w, pl.ds(0, sizes[j]))]
        own.append([
            pltpu.make_async_copy(ref.at[0, :, at], w[u].at[dp, :, to_at], lw.at[u])
            for ref, to_at in pairs
        ])

    def own_ready(u):
        pltpu.make_async_copy(w[u].at[dp], w[u].at[dp], lw.at[u]).wait()

    small = [
        pltpu.make_async_copy(routes_in, routes, ls.at[0]),
        pltpu.make_async_copy(probs_in, probs, ls.at[1]),
        pltpu.make_async_copy(tok, x.at[e], ls.at[2]),
        pltpu.make_async_copy(grad.at[:, pl.ds(0, part)], m.at[0, e], ls.at[3]),
        pltpu.make_async_copy(grad.at[:, pl.ds(part, part)], m.at[1, e], ls.at[4]),
    ]
    for d in own[0] + small[:2] + sum(own[1:], []) + small[2:]:
        d.start()
    pl.semaphore_wait(barrier, 5 + jnp.where(middle, 1, 0))

    half = toks // 2
    first, second, whole = pl.ds(0, half), pl.ds(half, half), pl.ds(0, toks)

    def spread_own(src, dst, p):
        for row, n, stage in ((first, 1, 0), (second, 2, 0), (second, 1, 1), (first, 2, 1)):
            send(src(row), dst(e, row), ds.at[p], dr.at[p, stage], (dp, near[n]))

    def spread_more(dst, p):
        arrive(dst(e, whole), dr.at[p, 0])
        for n, row, far in ((1, first, 2), (2, second, 1)):
            block = dst(near[n], row)
            send(block, block, ds.at[p], dr.at[p, 2], (dp, near[far]))

    def spread_rest(dst, p):
        arrive(dst(e, whole), dr.at[p, 1])

    def spread_done(dst, p):
        arrive(dst(e, whole), dr.at[p, 2])

    early, late = 1 - upper, upper

    def tok_src(row):
        return tok.at[row, :]

    def grad_src(side):
        return lambda row: grad.at[row, pl.ds(pl.multiple_of(side * part, part), part)]

    def x_dst(i, row):
        return x.at[i, row]

    def m_dst(side):
        return lambda i, row: m.at[side, i, row]

    def own_in(u):
        block = w[u].at[dp]
        send(block, block, gs.at[u], gr.at[u, jnp.where(edge, 0, 1)], inn)

    def own_out(u):
        block = w[u].at[dp]
        send(block, block, gs.at[u], gr.at[u, 0], out)

    def own_pair(u):
        block = w[u].at[dp]
        send(block, block, ps.at[u], pr.at[u], (partner, e))

    def gather_pass(u, at, stage, onward=None):
        block = w[u].at[at * 2 + c]
        arrive(block, gr.at[u, stage])
        if onward is not None:
            dev, later = onward
            send(block, block, gs.at[u], gr.at[u, later], dev)
        send(block, block, ps.at[u], pr.at[u], (partner, e))

    def pairs_done(u):
        arrive(w[u].at[pl.ds(0, 4)], pr.at[u])

    def block_of(k):
        return ((ey + k // 2) % 2) * 2 + (ex + k % 2) % 2

    def rows_of(i):
        return pl.ds(pl.multiple_of(i * toks, toks), toks)

    expert_rows = lax.broadcasted_iota(jnp.int32, (8, toks), 0)

    def turn_x(lo, hi):
        def body(k, _):
            i = block_of(k)
            xt[:, rows_of(i)] = x[i].T
            return 0

        lax.fori_loop(lo, hi, body, 0)

    def turn_m(side, lo, hi):
        def body(k, _):
            i = block_of(k)
            mt[pl.ds(pl.multiple_of(side * part, part), part), rows_of(i)] = m[side, i].T
            return 0

        lax.fori_loop(lo, hi, body, 0)

    def tall_probs():
        def body(i, _):
            row = jnp.sum(jnp.where(expert_rows == e, q[i], 0.0), axis=0, keepdims=True)
            pc[i] = jnp.broadcast_to(row, (128, toks)).T
            return 0

        lax.fori_loop(0, 4, body, 0)

    def forward_up(j, lo=0, hi=4):
        size, at = sizes[j], offsets[j]

        def body(k, _):
            i = block_of(k)
            here = rows_of(i)
            a = dot_f32(x[i], w[2 * j][:, :, :size].reshape(width, size))
            b = dot_f32(x[i], w[2 * j][:, :, size:].reshape(width, size))
            sig = jax.nn.sigmoid(a)
            act = (a * sig * b).astype(jnp.bfloat16)
            low_act[here, at : at + size] = act
            wt[j][here, :] = (act.astype(jnp.float32) * pc[i][:, :1]).astype(jnp.bfloat16)
            fac[here, 2 * at : 2 * at + size] = b * sig * (1.0 + a * (1.0 - sig))
            fac[here, 2 * at + size : 2 * (at + size)] = a * sig
            return 0

        lax.fori_loop(lo, hi, body, 0)

    def forward_down(j):
        size, at = sizes[j], offsets[j]

        def body(k, _):
            i = block_of(k)
            here = rows_of(i)
            cot = dot_f32(m[0, i], w[2 * j + 1][:4].reshape(part, size))
            cot = cot + dot_f32(m[1, i], w[2 * j + 1][4:].reshape(part, size))
            act = low_act[here, at : at + size].astype(jnp.float32)
            score = jnp.sum(act * cot, axis=1, keepdims=True)
            sb[i] = sb[i] + jnp.broadcast_to(score, (toks, 128))
            back = cot * pc[i][:, :1]
            du[j][here, :size] = (back * fac[here, 2 * at : 2 * at + size]).astype(jnp.bfloat16)
            du[j][here, size:] = (
                back * fac[here, 2 * at + size : 2 * (at + size)]
            ).astype(jnp.bfloat16)
            return 0

        lax.fori_loop(0, 4, body, 0)

    def ship(u, r):
        t = pos(r)
        send(term[u].at[t * 2 + c], inbox[u].at[side_in, t], gs.at[u], rr.at[u, r], inn)

    def gradient(u, lo, hi, outer):
        left, right = (xt, du[u // 2]) if u % 2 == 0 else (mt, wt[u // 2])

        def swap(t):
            return copy(
                term[u].at[t * 2 + 1 - c], swapped[u].at[t], ps.at[u], wr.at[u, t], (partner, e)
            )

        def block(d):
            here = pl.ds(pl.multiple_of(d * rows, rows), rows)
            term[u][d] = dot_f32(left[here, :], right[...]).astype(jnp.bfloat16)

        def give(r, _):
            block(pos(r) * 2 + 1 - c)
            swap(pos(r)).start()
            return 0

        def settle(r, _):
            t = pos(r)
            block(t * 2 + c)
            arrive(swapped[u].at[t], wr.at[u, t])
            term[u][t * 2 + c] = add_low(term[u][t * 2 + c], swapped[u][t])
            if outer and u not in HELD:
                pl.when(r < 3)(lambda: ship(u, r))
            return 0

        lax.fori_loop(lo, hi, give, 0)
        lax.fori_loop(lo, hi, settle, 0)

    def relay(u, side, t, stage, dev, later):
        arrive(term[u].at[dp], rr.at[u, stage])
        term[u][t * 2 + c] = add_low(term[u][t * 2 + c], inbox[u][side, t])
        send(term[u].at[t * 2 + c], inbox[u].at[side, t], gs.at[u], rr.at[u, later], dev)

    def spots(u):
        at = offsets[u // 2]
        return [at, hidden + at] if u % 2 == 0 else [2 * hidden + at]

    def final(u, outer):
        size = sizes[u // 2]
        if outer:
            arrive(term[u].at[dp], rr.at[u, 3])
        else:
            arrive(term[u].at[pl.ds(0, 2)], rr.at[u, 2])
        total = term[u][dp].astype(jnp.float32) + inbox[u][side_out, z].astype(jnp.float32)
        if not outer:
            total = total + inbox[u][side_in, z].astype(jnp.float32)
        total = total.astype(jnp.bfloat16)
        for k, spot in enumerate(spots(u)):
            weight_out[0, :, spot : spot + size] = total[:, k * size : (k + 1) * size]
    def home(j):
        def body(k, _):
            i = block_of(3 - k)
            new = contract_last(du[j][rows_of(i), :], w[2 * j][...].reshape(width, 2 * sizes[j]))
            if j == 0:
                ha[i] = new
            elif j < count - 1:
                ha[i] = ha[i] + new
            else:
                hs[i] = (ha[i] + new).astype(jnp.bfloat16)
                st[i] = sb[i].T[:8, :]

                @pl.when(k < 3)
                def _():
                    send(hs.at[i], hr.at[e], hsem.at[0], hrec.at[0], (dp, i))
                    send(st.at[i], sr.at[e], hsem.at[1], hrec.at[1], (dp, i))

            return 0

        lax.fori_loop(0, 4, body, 0)
        if j == count - 1:
            sr[e] = st[e]

    def home_done():
        arrive(hr.at[pl.ds(0, 3)], hrec.at[0])
        arrive(sr.at[pl.ds(0, 3)], hrec.at[1])
        total = hs[e].astype(jnp.float32)
        for k in (1, 2, 3):
            total = total + hr[near[k]].astype(jnp.float32)
        token_out[...] = total.astype(jnp.bfloat16)
        top = routes.shape[0]
        score = sum(jnp.where(routes[...] == i, sr[i][:top, :], 0.0) for i in range(4))
        lane = lax.broadcasted_iota(jnp.int32, (top, toks), 1)
        prob_out[...] = jnp.where(e * toks + lane < kept[0], score, 0.0).astype(jnp.bfloat16)

    def send_probs():
        sb[...] = jnp.zeros_like(sb)
        for d in small[:2]:
            d.wait()
        lanes = lax.broadcasted_iota(jnp.int32, (8, toks), 1)
        rate = sum(
            jnp.where(
                routes[k : k + 1, :] == expert_rows, probs[k : k + 1, :].astype(jnp.float32), 0.0
            )
            for k in range(routes.shape[0])
        )
        q[e] = jnp.where(e * toks + lanes < kept[0], rate, 0.0)
        for k in (1, 2, 3):
            send(q.at[e], q.at[e], ds.at[3], dr.at[3, 0], (dp, near[k]))

    def get_probs():
        arrive(q.at[pl.ds(0, 3)], dr.at[3, 0])
        tall_probs()

    parts = (
        (tok_src, x_dst, 0),
        (grad_src(early), m_dst(early), 1),
        (grad_src(late), m_dst(late), 2),
    )

    def turn(p, lo, hi):
        if p == 0:
            turn_x(lo, hi)
        else:
            turn_m(early if p == 1 else late, lo, hi)

    def after(u):
        chain = [v for v in GATHER if v != FILLER] + [None]
        return None if u == FILLER else chain[chain.index(u) + 1]

    def more(p):
        spread_more(*parts[p][1:])
        if p + 1 < len(parts):
            spread_own(*parts[p + 1])

    def rest(p):
        spread_rest(*parts[p][1:])
        for d in (small[2:3], small[3:5], [])[p]:
            d.wait()
        turn(p, 0, 3)

    def last(p):
        spread_done(*parts[p][1:])
        turn(p, 3, 4)
        if p == 0:
            get_probs()

    def gather_far(u):
        gather_pass(u, pos(0), 2, (out, 2))
        if after(u) is not None:
            own_out(after(u))

    def gather_in(u):
        gather_pass(u, pos(3), 0, (inn, 2))
        if after(u) is not None:
            own_in(after(u))

    def up(j):
        pairs_done(2 * j)
        forward_up(j)

    def down(j):
        pairs_done(2 * j + 1)
        forward_down(j)

    def drain(outer):
        left(x.at[pl.ds(0, 3)], ds.at[0])
        for p in (1, 2):
            left(m.at[0, pl.ds(0, 3)], ds.at[p])
        left(q.at[pl.ds(0, 3)], ds.at[3])
        left(hs.at[pl.ds(0, 3)], hsem.at[0])
        left(st.at[pl.ds(0, 3)], hsem.at[1])
        for u in range(units):
            left(w[u].at[pl.ds(0, 4 if outer else 8)], gs.at[u])
            left(w[u], ps.at[u])

    def run(steps, outer):
        calls = {
            MORE: more,
            REST: rest,
            LAST: last,
            TAKE: lambda u, r: gather_pass(u, pos(2 - r), r),
            PASS_IN: gather_in,
            PASS_OUT: lambda u: gather_pass(u, pos(1), 1, (out, 1)),
            PASS_FAR: gather_far,
            UP: up,
            DOWN: down,
            GRAD: lambda u, lo, hi: gradient(u, lo, hi, outer),
            SUM_IN: lambda u, r: relay(u, side_in, pos(r), r, inn, 3 - r),
            SUM_OUT: lambda u: relay(u, side_out, pos(3), 3, out, 3),
            FINAL: lambda u: final(u, outer),
            HOME: home,
            HOME_DONE: home_done,
            SHIP: ship,
            DRAIN: lambda: drain(outer),
        }
        for name, *args in steps:
            calls[name](*args)

    spread_own(*parts[0])
    own_ready(0)
    own_in(0)
    pl.when(middle)(lambda: own_out(0))
    own_pair(0)
    for u in GATHER[1:]:
        own_ready(u)
        pl.when(edge)(lambda: own_in(u))
        if u == FILLER:
            pl.when(middle)(lambda: own_in(u))
            pl.when(middle)(lambda: own_out(u))
        own_pair(u)
    send_probs()
    pl.when(edge)(lambda: run(EDGE_STEPS, True))
    pl.when(middle)(lambda: run(MIDDLE_STEPS, False))


def hand_over(*refs):
    came, go, sem = refs[:3], refs[3:6], refs[6]
    away = [pltpu.make_async_copy(a, b, sem.at[k]) for k, (a, b) in enumerate(zip(came, go))]
    for d in away:
        d.start()
    for d in away:
        d.wait()


def per_device_line(
    tokens, out_grad, routes, route_probs, kept_count, gate_weight, up_weight, down_weight
):
    toks, width = tokens.shape
    rows, hidden = gate_weight.shape[1:]
    sizes = [hidden * k // 6 for k in SHARES]
    cols = [n for size in sizes for n in (2 * size, size)]
    units = len(cols)
    low, full = jnp.bfloat16, jnp.float32
    dma, vmem = pltpu.SemaphoreType.DMA, pltpu.VMEM
    hbm, chip = pl.BlockSpec(memory_space=pl.ANY), pl.BlockSpec(memory_space=vmem)
    top = routes.shape[1]
    shapes = (
        jax.ShapeDtypeStruct((toks, width), low),
        jax.ShapeDtypeStruct((top, toks), low),
        jax.ShapeDtypeStruct((1, rows, 3 * hidden), low),
    )
    results = pl.pallas_call(
        kernel,
        out_shape=tuple(vmem(s.shape, s.dtype) for s in shapes),
        in_specs=[hbm] * 7 + [pl.BlockSpec(memory_space=pltpu.SMEM)],
        out_specs=(chip,) * 3,
        scratch_shapes=[
            [vmem((8, rows, n), low) for n in cols],
            [vmem((8, rows, n), low) for n in cols],
            [vmem((4, rows, n), low) for n in cols],
            [vmem((2, 4, rows, n), low) for n in cols],
            [vmem((4 * toks, 2 * n), low) for n in sizes],
            [vmem((4 * toks, n), low) for n in sizes],
            vmem((4 * toks, 2 * hidden), full),
            vmem((4 * toks, hidden), low),
            vmem((4, toks, width), low),
            vmem((2, 4, toks, width // 2), low),
            vmem((width, 4 * toks), low),
            vmem((width, 4 * toks), low),
            vmem((4, 8, toks), full),
            vmem((4, toks, 128), full),
            vmem((4, toks, 128), full),
            vmem((4, 8, toks), full),
            vmem((4, 8, toks), full),
            vmem((4, toks, width), full),
            vmem((4, toks, width), low),
            vmem((4, toks, width), low),
            vmem((top, toks), jnp.int32),
            vmem((top, toks), low),
            dma((units,)), dma((units, 3)), dma((units,)), dma((units,)),
            dma((4,)), dma((4, 3)), dma((units, 4)), dma((units, 4)),
            dma((2,)), dma((2,)), dma((units,)), dma((5,)),
        ],
        compiler_params=pltpu.CompilerParams(
            collective_id=0, has_side_effects=True, vmem_limit_bytes=61 * 2**20
        ),
    )(
        gate_weight, up_weight, down_weight, tokens, out_grad, routes.T, route_probs.T, kept_count
    )
    token_grad, prob_grad, weight_grad = pl.pallas_call(
        hand_over,
        out_shape=shapes,
        in_specs=[chip] * 3,
        out_specs=(hbm,) * 3,
        scratch_shapes=[dma((3,))],
    )(*[pltpu.with_memory_space_constraint(r, vmem) for r in results])
    return (token_grad, prob_grad.T, weight_grad)


def solution(mesh):
    in_specs = (
        P(("dp", "expert"), None),
        P(("dp", "expert"), None),
        P(("dp", "expert"), None),
        P(("dp", "expert"), None),
        P("dp"),
        P("expert", "dp", None),
        P("expert", "dp", None),
        P("expert", "dp", None),
    )
    out_specs = (P(("dp", "expert"), None), P(("dp", "expert"), None), P("expert", "dp", None))

    line = mesh.shape["dp"] == 4 * CORES and mesh.shape["expert"] == 4
    return jax.shard_map(
        per_device_line if line else per_device,
        mesh=mesh, in_specs=in_specs, out_specs=out_specs, check_vma=False,
    )
```
